32 devices in a mesh: seq: 4 (over x, core), fsdp: 8 (over z, y).
Axes of the slice: x: 2, y: 2, z: 4, core: 2. Of those that a mesh axis runs over, the one named last changes fastest.
Arguments:
- layer_input: bfloat16 [8, 1536, 1024], P('fsdp', 'seq'), may hold values from -12 to 12
- query_weight: bfloat16 [1024, 1024], P('fsdp'), may hold values from -0.1875 to 0.1875
- key_weight: bfloat16 [1024, 1024], P('fsdp'), may hold values from -0.1875 to 0.1875
- value_weight: bfloat16 [1024, 1024], P('fsdp'), may hold values from -0.1875 to 0.1875
- output_weight: bfloat16 [1024, 1024], P('fsdp'), may hold values from -0.75 to 0.75
- query_bias: bfloat16 [1024], P('fsdp'), may hold values from -4 to 4
- value_bias: bfloat16 [1024], P('fsdp'), may hold values from -1.5 to 1.5
- output_bias: bfloat16 [1024], P('fsdp'), may hold values from -4 to 4
- attn_gain: bfloat16 [1024], P('fsdp'), may hold values from 0.5 to 1.5
- attn_shift: bfloat16 [1024], P('fsdp'), may hold values from -4 to 4
- in_weight: bfloat16 [1024, 4096], P('fsdp'), may hold values from -0.1875 to 0.1875
- in_bias: bfloat16 [4096], P('fsdp'), may hold values from -4 to 4
- out_weight: bfloat16 [4096, 1024], P('fsdp'), may hold values from -0.09375 to 0.09375
- out_bias: bfloat16 [1024], P('fsdp'), may hold values from -4 to 4
- out_gain: bfloat16 [1024], P('fsdp'), may hold values from 0.5 to 1.5
- out_shift: bfloat16 [1024], P('fsdp'), may hold values from -4 to 4
- out_cotangent: bfloat16 [8, 1536, 1024], P('fsdp', 'seq'), may hold values from -6 to 6
Outputs:
- layer_output: bfloat16 [8, 1536, 1024], P('fsdp', 'seq')
- input_grad: float32 [8, 1536, 1024], P('fsdp', 'seq')
- query_weight_grad: float32 [1024, 1024], P('fsdp')
- key_weight_grad: float32 [1024, 1024], P('fsdp')
- value_weight_grad: float32 [1024, 1024], P('fsdp')
- output_weight_grad: float32 [1024, 1024], P('fsdp')
- query_bias_grad: float32 [1024], P('fsdp')
- value_bias_grad: float32 [1024], P('fsdp')
- output_bias_grad: float32 [1024], P('fsdp')
- attn_gain_grad: float32 [1024], P('fsdp')
- attn_shift_grad: float32 [1024], P('fsdp')
- in_weight_grad: float32 [1024, 4096], P('fsdp')
- in_bias_grad: float32 [4096], P('fsdp')
- out_weight_grad: float32 [4096, 1024], P('fsdp')
- out_bias_grad: float32 [1024], P('fsdp')
- out_gain_grad: float32 [1024], P('fsdp')
- out_shift_grad: float32 [1024], P('fsdp')
- rms_values: float32 [5], replicated
The draws below stay inside these ranges and needn't reach their ends.
All inputs are finite; a program needn't handle non-finite values.
Results may differ from the reference program's by a relative error of at most 0.015.
Values may be sent and summed in bfloat16 or wider, within the bound.
A program may use at most 192 MiB of HBM per device.

```python
import jax
import jax.numpy as jnp
from jax import lax

D = 1024
H = 16
HD = 64
FF = 4096
LEN = 1536
SEQS = 8
TOKENS = 12288


def draw_layer_input(key, part):
    key_base, key_rough = jax.random.split(key, 2)
    seq_place = jnp.arange(SEQS, dtype=jnp.float32)[:, None, None] / max(SEQS - 1, 1)
    tok_place = jnp.arange(LEN, dtype=jnp.float32)[None, :, None] / max(LEN - 1, 1)
    ramp_scale = 0.7 * jnp.exp(jnp.log(15.0 / 7.0) * 0.5 * (seq_place + tok_place))
    rough_scale = jnp.exp(jax.random.uniform(key_rough, (SEQS, LEN, 1), jnp.float32, -0.25, 0.25))
    base_draw = jnp.clip(jax.random.normal(key_base, (SEQS, LEN, D), jnp.float32), -6.0, 6.0)
    return (base_draw * ramp_scale * rough_scale).astype(jnp.bfloat16)


def levels(key, shape, cuts, low, top_value):
    loudness = 1.0
    for axis_at, blocks in cuts:
        heights = jax.random.uniform(jax.random.fold_in(jax.random.fold_in(key, 6), axis_at), (blocks,), jnp.float32, low / len(cuts), top_value / len(cuts))
        loudness = loudness * jnp.repeat(jnp.exp(heights), shape[axis_at] // blocks).reshape((-1,) + (1,) * (len(shape) - 1 - axis_at))
    return loudness


def gaussian(stream_key, shape, deviation, most, cuts=(), kind=jnp.bfloat16):
    level = levels(stream_key, shape, cuts, -0.22, 0.18) if cuts else 1.0
    drawn = jax.random.normal(stream_key, shape, jnp.float32) * deviation * level
    return jnp.minimum(jnp.maximum(drawn, -most), most).astype(kind)


def setup_inputs(seed: int = 0) -> dict:
    keys = jax.random.split(jax.random.key(seed), 18)
    layer_input = draw_layer_input(jax.random.fold_in(keys[17], 71), 0)
    query_weight = gaussian(keys[1], (D, D), D ** -0.5, 0.1875, ((0, 8),))
    key_weight = gaussian(keys[2], (D, D), D ** -0.5, 0.1875, ((0, 8),))
    value_weight = gaussian(keys[3], (D, D), D ** -0.5, 0.1875, ((0, 8),))
    output_weight = gaussian(keys[4], (D, D), (D // 16) ** -0.5, 0.75, ((0, 8),))
    query_bias = gaussian(keys[5], (D,), 0.3, 4.0, ((0, 8),))
    value_bias = gaussian(keys[6], (D,), 0.1, 1.5, ((0, 8),))
    output_bias = gaussian(keys[7], (D,), 0.3, 4.0, ((0, 8),))
    attn_gain = jnp.clip(1.0 + 0.1 * jax.random.normal(keys[8], (D,), jnp.float32), 0.5, 1.5).astype(jnp.bfloat16)
    attn_shift = gaussian(keys[9], (D,), 0.3, 4.0, ((0, 8),))
    in_weight = gaussian(keys[10], (D, FF), D ** -0.5, 0.1875, ((0, 8),))
    in_bias = gaussian(keys[11], (FF,), 0.3, 4.0, ((0, 8),))
    out_weight = gaussian(keys[12], (FF, D), FF ** -0.5, 0.09375, ((0, 8),))
    out_bias = gaussian(keys[13], (D,), 0.3, 4.0, ((0, 8),))
    out_gain = jnp.clip(1.0 + 0.1 * jax.random.normal(keys[14], (D,), jnp.float32), 0.5, 1.5).astype(jnp.bfloat16)
    out_shift = gaussian(keys[15], (D,), 0.3, 4.0, ((0, 8),))
    out_cotangent = gaussian(keys[16], (SEQS, LEN, D), 1.0, 6.0, ((0, 8), (1, 4)))
    return {"layer_input": layer_input, "query_weight": query_weight, "key_weight": key_weight, "value_weight": value_weight, "output_weight": output_weight, "query_bias": query_bias, "value_bias": value_bias, "output_bias": output_bias, "attn_gain": attn_gain, "attn_shift": attn_shift, "in_weight": in_weight, "in_bias": in_bias, "out_weight": out_weight, "out_bias": out_bias, "out_gain": out_gain, "out_shift": out_shift, "out_cotangent": out_cotangent}


@jax.custom_vjp
def low(v):
    return lax.optimization_barrier(v.astype(jnp.bfloat16)).astype(jnp.float32)

@jax.custom_vjp
def low_back(v):
    return v

def low_keep(v):
    return (low(v), None)

def low_pass(kept, grad):
    return (grad,)

def back_keep(v):
    return (v, None)

def back_low(kept, grad):
    return (low(grad),)
low.defvjp(low_keep, low_pass)
low_back.defvjp(back_keep, back_low)
PRECISE = lax.Precision.HIGHEST

def matmul(left, right):
    return jnp.dot(left, right, precision=PRECISE, preferred_element_type=jnp.float32)

def layer_norm(stream, gain, shift):
    centre = stream - lax.optimization_barrier(jnp.mean(stream, axis=-1, keepdims=True))
    variance = lax.optimization_barrier(jnp.mean(centre * centre, axis=-1, keepdims=True))
    return centre * lax.rsqrt(variance + 1e-05) * gain + shift

def gelu_exact(inputs):
    return jax.nn.gelu(inputs, approximate=False)

def attention(query_rows, key_rows, value_rows):
    block_rows = min(512, LEN)

    def one_block(query_block):
        scores = low_back(jnp.einsum('qhd,khd->hqk', query_block, key_rows, precision=PRECISE) * 0.125)
        row_max = lax.optimization_barrier(jnp.max(scores, axis=-1, keepdims=True))
        exp_scores = jnp.exp(scores - row_max)
        attn_probs = exp_scores / lax.optimization_barrier(jnp.sum(exp_scores, axis=-1, keepdims=True))
        return jnp.einsum('hqk,khd->qhd', low(attn_probs), value_rows, precision=PRECISE)
    blocks = query_rows.reshape(LEN // block_rows, block_rows, H, HD)
    outputs = lax.map(jax.checkpoint(one_block), blocks)
    return outputs.reshape(LEN, H * HD)

def encoder_layer(seq_input, query_weight, key_weight, value_weight, output_weight, query_bias, value_bias, output_bias, attn_gain, attn_shift, in_weight, in_bias, out_weight, out_bias, out_gain, out_shift):
    query_rows = low_back(low(matmul(seq_input, query_weight) + query_bias)).reshape(LEN, H, HD)
    key_rows = low_back(low(matmul(seq_input, key_weight))).reshape(LEN, H, HD)
    value_rows = low_back(low(matmul(seq_input, value_weight) + value_bias)).reshape(LEN, H, HD)
    attn_mixed = low_back(low(attention(query_rows, key_rows, value_rows)))
    attn_out = low_back(matmul(attn_mixed, output_weight) + output_bias)
    normed = layer_norm(seq_input + attn_out, attn_gain, attn_shift)
    hidden_pre = low_back(matmul(low(normed), in_weight) + in_bias)
    hidden = low(gelu_exact(hidden_pre))
    branch = low_back(matmul(hidden, out_weight) + out_bias)
    layer_out = layer_norm(normed + branch, out_gain, out_shift)
    return (layer_out, (attn_out, normed, branch))

def reference(layer_input, query_weight, key_weight, value_weight, output_weight, query_bias, value_bias, output_bias, attn_gain, attn_shift, in_weight, in_bias, out_weight, out_bias, out_gain, out_shift, out_cotangent):
    weights = tuple((weight.astype(jnp.float32) for weight in (query_weight, key_weight, value_weight, output_weight, query_bias, value_bias, output_bias, attn_gain, attn_shift, in_weight, in_bias, out_weight, out_bias, out_gain, out_shift)))

    def advance(carry, seq_pair):
        grad_total, square_total = carry
        seq_input = seq_pair[0].astype(jnp.float32)
        cotangent = seq_pair[1].astype(jnp.float32)
        layer_out, pullback, extras = jax.vjp(encoder_layer, seq_input, *weights, has_aux=True)
        gradients = pullback(cotangent)
        attn_out, normed, branch = extras
        squares = jnp.stack([jnp.sum(seq_input * seq_input), jnp.sum(attn_out * attn_out), jnp.sum(normed * normed), jnp.sum(branch * branch), jnp.sum(layer_out * layer_out)])
        grad_total = tuple((total_grad + new_grad for total_grad, new_grad in zip(grad_total, gradients[1:])))
        return ((grad_total, square_total + squares), (layer_out.astype(jnp.bfloat16), gradients[0]))
    initial = (tuple((jnp.zeros_like(weight) for weight in weights)), jnp.zeros((5,), jnp.float32))
    (grad_total, square_total), (outputs, input_grad) = lax.scan(advance, initial, (layer_input, out_cotangent))
    rms_values = jnp.sqrt(square_total / jnp.float32(TOKENS * D))
    return (outputs, input_grad, grad_total[0], grad_total[1], grad_total[2], grad_total[3], grad_total[4], grad_total[5], grad_total[6], grad_total[7], grad_total[8], grad_total[9], grad_total[10], grad_total[11], grad_total[12], grad_total[13], grad_total[14], rms_values)
```

```python
import functools
import jax
import jax.numpy as jnp
from jax import lax
from jax.experimental import pallas as pl
from jax.experimental.pallas import tpu as pltpu
from jax.sharding import PartitionSpec as P

HD = 64
MESH = pl.DeviceIdType.MESH
bf16 = jnp.bfloat16
f32 = jnp.float32


def each(lo, hi, body):
    if hi - lo <= 8:
        for i in range(lo, hi):
            body(i)
    else:
        pl.loop(lo, hi)(body)


class Grid:
    def __init__(self, seq_count, fsdp_count):
        self.S, self.F = seq_count, fsdp_count
        self.H = seq_count // 2
        self.Y = 2 if fsdp_count % 2 == 0 and fsdp_count <= 8 else 4
        self.Z = fsdp_count // self.Y
        self.s = lax.axis_index("seq")
        self.f = lax.axis_index("fsdp")
        self.c = self.s % 2
        self.hi = self.s // 2
        self.z = self.f // self.Y
        self.y = self.f % self.Y

    def zp(self, k):
        return ((self.z + k) % self.Z) * self.Y + self.y

    def yp(self, j):
        return self.z * self.Y + (self.y + j) % self.Y

    def xp(self, m):
        return ((self.hi + m) % self.H) * 2 + self.c

    def sib(self):
        return self.hi * 2 + 1 - self.c

    def origin(self, r):
        j, k = r // self.Z, r % self.Z
        return ((self.z + self.Z - k) % self.Z) * self.Y + (self.y + self.Y - j) % self.Y

    def greet(self, barrier):
        count = 0
        for m in range(self.H):
            for flip in range(2):
                if m or flip:
                    to = ((self.hi + m) % self.H) * 2 + (self.c + flip) % 2
                    pl.semaphore_signal(barrier, inc=1, device_id=(to, self.f), device_id_type=MESH)
                    count += 1
        for k in range(1, self.Z):
            pl.semaphore_signal(barrier, inc=1, device_id=(self.s, self.zp(k)), device_id_type=MESH)
            count += 1
        for j in range(1, self.Y):
            pl.semaphore_signal(barrier, inc=1, device_id=(self.s, self.yp(j)), device_id_type=MESH)
            count += 1
        pl.semaphore_wait(barrier, count)


class Sems:
    def __init__(self):
        self.n = 0

    def take(self, n):
        at = self.n
        self.n += n
        return at


def rcopy(sems, src, dst, send, recv, to):
    return pltpu.make_async_remote_copy(
        src_ref=src,
        dst_ref=dst,
        send_sem=sems.at[send],
        recv_sem=sems.at[recv],
        device_id=to,
        device_id_type=MESH,
    )


class Gather:
    def __init__(self, alloc, S, F, Y, kind):
        self.kind = kind
        Z = F // Y
        self.zs = alloc.take(Z)
        self.ys = alloc.take(Y * Z)
        self.ir = alloc.take(F)
        if kind != "own":
            self.ss, self.sr = alloc.take(F), alloc.take(F)
        if kind == "quarter":
            H = S // 2
            self.xs, self.xr = alloc.take(H * F), alloc.take(H * F)
            self.ts, self.tr = alloc.take(H * F), alloc.take(H * F)

    def bind(self, g, sems, piece, place):
        self.g, self.sems, self.piece, self.place = g, sems, piece, place

    def part(self, hi=None, c=None):
        g = self.g
        c = g.c if c is None else c
        hi = g.hi if hi is None else hi
        return {"own": g.s, "half": c, "quarter": hi * 2 + c}[self.kind]

    def start(self):
        g, p = self.g, self.part()
        src, dst = self.piece(p), self.place(g.f, p)
        for k in range(1, g.Z):
            rcopy(self.sems, src, dst, self.zs + k, self.ir + k, (g.s, g.zp(k))).start()
        for j in range(1, g.Y):
            rcopy(self.sems, src, dst, self.ys + j * g.Z, self.ir + j * g.Z, (g.s, g.yp(j))).start()

    def wait_in(self, r):
        ref = self.place(self.g.origin(r), self.part())
        rcopy(self.sems, ref, ref, self.ir + r, self.ir + r, (self.g.sib(), self.g.f)).wait_recv()

    def pass_on(self, r):
        g = self.g
        ref = self.place(g.origin(r), self.part())
        if self.kind == "quarter":
            for m in range(1, g.H):
                rcopy(self.sems, ref, ref, self.xs + m * g.F + r, self.xr + m * g.F + r, (g.xp(m), g.f)).start()
        if self.kind != "own":
            rcopy(self.sems, ref, ref, self.ss + r, self.sr + r, (g.sib(), g.f)).start()

    def on_z(self):
        g = self.g

        def body(k):
            self.wait_in(k)
            ref = self.place(g.origin(k), self.part())
            for j in range(1, g.Y):
                at = j * g.Z + k
                rcopy(self.sems, ref, ref, self.ys + at, self.ir + at, (g.s, g.yp(j))).start()
            self.pass_on(k)

        each(1, g.Z, body)

    def on_y(self):
        def body(r):
            self.wait_in(r)
            self.pass_on(r)

        each(self.g.Z, self.g.F, body)

    def on_x(self):
        if self.kind != "quarter":
            return
        g = self.g
        for m in range(1, g.H):
            part = self.part(hi=(g.hi + g.H - m) % g.H)

            def body(r):
                ref = self.place(g.origin(r), part)
                at = m * g.F + r
                rcopy(self.sems, ref, ref, self.xr + at, self.xr + at, (g.sib(), g.f)).wait_recv()
                rcopy(self.sems, ref, ref, self.ts + at, self.tr + at, (g.sib(), g.f)).start()

            each(1, g.F, body)

    def finish(self):
        g = self.g
        other = 1 - g.c

        def sent(ref, at):
            rcopy(self.sems, ref, ref, at, at, (g.sib(), g.f)).wait_send()

        def got(ref, at):
            rcopy(self.sems, ref, ref, at, at, (g.sib(), g.f)).wait_recv()

        if self.kind != "own":
            each(1, g.F, lambda r: got(self.place(g.origin(r), self.part(c=other)), self.sr + r))
        if self.kind == "quarter":
            for m in range(1, g.H):
                part = self.part(hi=(g.hi + g.H - m) % g.H, c=other)
                each(1, g.F, lambda r: got(self.place(g.origin(r), part), self.tr + m * g.F + r))
        mine = self.piece(self.part())
        for k in range(1, g.Z):
            sent(mine, self.zs + k)
        for j in range(1, g.Y):
            each(0, g.Z, lambda k: sent(mine, self.ys + j * g.Z + k))
        if self.kind != "own":
            each(1, g.F, lambda r: sent(mine, self.ss + r))
        if self.kind == "quarter":
            for m in range(1, g.H):
                each(1, g.F, lambda r: sent(mine, self.xs + m * g.F + r))
                each(1, g.F, lambda r: sent(mine, self.ts + m * g.F + r))


def forward_kernel(plan, x, wq, wk, wv, small, wo, w1, w2, *rest):
    (xfull, wqkv, smalls, q_o, k_o, v_o, qt_o, kt_o, ot_o, lse_o, mixed, wo_f, w1_f, w2_f) = rest[:14]
    (xs, ws, sm, qn, kn, vn, qt, kt, vt, ot, lse, oblk, onat, sems) = rest[14:]
    S, F, rows, length, heads, wide, vec = plan.S, plan.F, plan.rows, plan.length, plan.heads, plan.wide, plan.vec
    g = Grid(S, F)
    g.greet(pltpu.get_barrier_semaphore())
    part_rows = wq.shape[0]
    local = []

    def keep(src, dst, at):
        copy = pltpu.make_async_copy(src, dst, sems.at[at])
        copy.start()
        return copy

    mine = xs.at[pl.ds(g.s * rows, rows)]
    x_out = [rcopy(sems, x, mine, plan.x_s, plan.x_r, (g.sib(), g.f))]
    for m in range(1, g.H):
        x_out.append(rcopy(sems, x, mine, plan.x_s + m, plan.x_r + m, (g.xp(m), g.f)))
    for copy in x_out[::-1]:
        copy.start()
    for item, src, col in ((plan.gq, wq, 0), (plan.gk, wk, 1), (plan.gv, wv, 2)):
        item.bind(
            g,
            sems,
            lambda p, src=src: src.at[:, pl.ds(p * wide, wide)],
            lambda o, p, col=col: ws.at[pl.ds(o * part_rows, part_rows), pl.ds(col * wide, wide)],
        )
        item.start()
    plan.gs.bind(g, sems, lambda p: small, lambda o, p: sm.at[pl.ds(o * 16, 16)])
    plan.gs.start()
    local.append(keep(x, mine, plan.l))
    for col, src in enumerate((wq, wk, wv)):
        local.append(
            keep(
                src.at[:, pl.ds(g.s * wide, wide)],
                ws.at[pl.ds(g.f * part_rows, part_rows), pl.ds(col * wide, wide)],
                plan.l + 1 + col,
            )
        )
    local.append(keep(small, sm.at[pl.ds(g.f * 16, 16)], plan.l + 4))
    own = []
    for i, (src, dst) in enumerate(((wo, wo_f), (w1, w1_f), (w2, w2_f))):
        n = src.shape[0]
        own.append(keep(src, dst.at[pl.ds(g.f * n, n)], plan.l + 5 + i))
    for src, dst, (item, lo, width) in [
        (src, dst, entry)
        for src, dst, entries in ((wo, wo_f, plan.go), (w1, w1_f, plan.g1), (w2, w2_f, plan.g2))
        for entry in entries
    ]:
        n = src.shape[0]
        item.bind(
            g,
            sems,
            lambda p, src=src, lo=lo, width=width: src.at[:, pl.ds(lo + p * width, width)],
            lambda o, p, dst=dst, n=n, lo=lo, width=width: dst.at[pl.ds(o * n, n), pl.ds(lo + p * width, width)],
        )
    big = [e[0] for e in plan.g1 + plan.go + plan.g2]
    for item in (plan.gq, plan.gk, plan.gv, plan.gs):
        item.on_z()
    x_pass = []
    for m in range(1, g.H):
        theirs = xs.at[pl.ds(((g.hi + g.H - m) % g.H * 2 + g.c) * rows, rows)]
        rcopy(sems, theirs, theirs, plan.x_s, plan.x_r + m, (g.sib(), g.f)).wait_recv()
        copy = rcopy(sems, theirs, theirs, plan.x_s + g.H + m, plan.x_r + g.H + m, (g.sib(), g.f))
        copy.start()
        x_pass.append(copy)
    for item in (plan.gq, plan.gk, plan.gv, plan.gs):
        item.on_y()
    for item in big:
        item.start()
    rcopy(sems, mine, mine, plan.x_s, plan.x_r, (g.sib(), g.f)).wait_recv()
    for m in range(1, g.H):
        rcopy(sems, mine, mine, plan.x_s, plan.x_r + g.H + m, (g.sib(), g.f)).wait_recv()
    for copy in local:
        copy.wait()

    table = sm[...]
    lane = lax.broadcasted_iota(jnp.int32, (vec, wide), 1)
    spread = (lane % vec == lax.broadcasted_iota(jnp.int32, (vec, wide), 0)).astype(f32).astype(bf16)
    spread = jnp.dot(table, spread, preferred_element_type=f32)
    row = lax.broadcasted_iota(jnp.int32, spread.shape, 0)
    column = lax.broadcasted_iota(jnp.int32, spread.shape, 1)

    def vector(i):
        want = (g.s * (wide // vec) + column // vec) * 16 + i
        return jnp.sum(jnp.where(row == want, spread, 0.0), axis=0, keepdims=True)

    bias_q, bias_v = vector(0), vector(1)

    @pl.loop(0, S)
    def _(b):
        at = pl.multiple_of(b * rows, rows)
        prod = jnp.dot(xs[pl.ds(at, rows), :], ws[...], preferred_element_type=f32)
        q = (prod[:, :wide] + bias_q).astype(bf16).astype(f32) * 0.125
        k = prod[:, wide : 2 * wide]
        v = prod[:, 2 * wide :] + bias_v
        qn[pl.ds(at, rows), :] = q.astype(bf16)
        kn[pl.ds(at, rows), :] = k.astype(bf16)
        vn[pl.ds(at, rows), :] = v.astype(bf16)
        qt[:, pl.ds(at, rows)] = q.T.astype(bf16)
        kt[:, pl.ds(at, rows)] = k.T.astype(bf16)
        vt[:, pl.ds(at, rows)] = v.T.astype(bf16)

    stores = [
        keep(src, dst, plan.l + 8 + i)
        for i, (src, dst) in enumerate(
            ((xs, xfull), (ws, wqkv), (sm, smalls), (qn, q_o), (kn, k_o), (vn, v_o), (qt, qt_o), (kt, kt_o))
        )
    ]
    head_of = lax.broadcasted_iota(jnp.int32, (wide, rows), 0) // HD
    sent = []
    for t in range(S):
        hi = (g.hi + 1 + t // 2) % g.H
        c = (g.c + t + t // (2 * (g.H - 1))) % 2
        to = hi * 2 + c
        at = pl.multiple_of(to * rows, rows)

        @pl.loop(0, heads)
        def _(h):
            q = jnp.where(head_of == h, qt[:, pl.ds(at, rows)], jnp.zeros((), bf16))
            s = jnp.dot(kn[...], q, preferred_element_type=f32)
            m = jnp.max(s, axis=0, keepdims=True)
            e = jnp.exp(s - m)
            l = jnp.sum(e, axis=0, keepdims=True)
            band = pl.ds(pl.multiple_of(h * HD, HD), HD)
            o = jnp.dot(vt[band, :], e.astype(bf16), preferred_element_type=f32) / l
            oblk[band, :] = o
            lse[pl.ds(h, 1), pl.ds(at, rows)] = m + jnp.log(l)

        ot[:, pl.ds(at, rows)] = oblk[...].astype(bf16)
        onat[t] = oblk[...].T.astype(bf16)
        dst = mixed.at[:, pl.ds(g.s * wide, wide)]
        if t < S - 1:
            copy = rcopy(sems, onat.at[t], dst, plan.o_s + t, plan.o_r + g.s, (to, g.f))
            copy.start()
            sent.append(copy)
        else:
            stores.append(keep(onat.at[t], dst, plan.o_s + t))
    stores.append(keep(ot, ot_o, plan.l + 16))
    stores.append(keep(lse, lse_o, plan.l + 17))
    for i, item in enumerate(big):
        if i == 0:
            item.on_z()
        item.on_y()
        if i + 1 < len(big):
            big[i + 1].on_z()
        item.on_x()
    for item in (plan.gq, plan.gk, plan.gv, plan.gs, *big):
        item.finish()
    for i in range(1, S):
        peer = (g.s + i) % S
        ref = mixed.at[:, pl.ds(peer * wide, wide)]
        rcopy(sems, ref, ref, plan.o_r + peer, plan.o_r + peer, (peer, g.f)).wait_recv()
    for copy in sent + x_out + x_pass:
        copy.wait_send()
    for copy in stores + own:
        copy.wait()


class Plan:
    pass


def forward_plan(S, F, rows, width, ff):
    plan = Plan()
    alloc = Sems()
    plan.S, plan.F, plan.rows, plan.length = S, F, rows, rows * S
    plan.wide = width // S
    plan.heads = plan.wide // HD
    plan.vec = width // F
    Y = 2 if F % 2 == 0 and F <= 8 else 4
    plan.x_s, plan.x_r = alloc.take(S), alloc.take(S)
    plan.gq, plan.gk, plan.gv, plan.gs = (Gather(alloc, S, F, Y, "own") for _ in range(4))
    half = width // 2
    plan.go = [(Gather(alloc, S, F, Y, "half"), 0, half)]
    eighth = ff // 2 // S
    plan.g1 = [(Gather(alloc, S, F, Y, "quarter"), i * S * eighth, eighth) for i in range(2)]
    plan.g2 = [(Gather(alloc, S, F, Y, "half"), i * half, half // 2) for i in range(2)]
    plan.o_s, plan.o_r = alloc.take(S), alloc.take(S)
    plan.l = alloc.take(20)
    plan.sems = alloc.n
    return plan


def forward(S, F, x, wq, wk, wv, small, wo, w1, w2):
    rows, width = x.shape
    ff = w1.shape[1]
    plan = forward_plan(S, F, rows, width, ff)
    length, wide, heads = plan.length, plan.wide, plan.heads
    sds = jax.ShapeDtypeStruct
    any_ = pl.BlockSpec(memory_space=pl.ANY)
    return pl.pallas_call(
        functools.partial(forward_kernel, plan),
        out_shape=(
            sds((length, width), bf16),
            sds((width, 3 * wide), bf16),
            sds((F * 16, plan.vec), bf16),
            sds((length, wide), bf16),
            sds((length, wide), bf16),
            sds((length, wide), bf16),
            sds((wide, length), bf16),
            sds((wide, length), bf16),
            sds((wide, length), bf16),
            sds((8, length), f32),
            sds((rows, width), bf16),
            sds((width, width), bf16),
            sds((width, ff), bf16),
            sds((ff, width), bf16),
        ),
        in_specs=[any_] * 8,
        out_specs=(any_,) * 14,
        scratch_shapes=[
            pltpu.VMEM((length, width), bf16),
            pltpu.VMEM((width, 3 * wide), bf16),
            pltpu.VMEM((F * 16, plan.vec), bf16),
            pltpu.VMEM((length, wide), bf16),
            pltpu.VMEM((length, wide), bf16),
            pltpu.VMEM((length, wide), bf16),
            pltpu.VMEM((wide, length), bf16),
            pltpu.VMEM((wide, length), bf16),
            pltpu.VMEM((wide, length), bf16),
            pltpu.VMEM((wide, length), bf16),
            pltpu.VMEM((8, length), f32),
            pltpu.VMEM((wide, rows), f32),
            pltpu.VMEM((S, rows, wide), bf16),
            pltpu.SemaphoreType.DMA((plan.sems,)),
        ],
        compiler_params=pltpu.CompilerParams(collective_id=0, has_side_effects=True, vmem_limit_bytes=48 << 20),
        name="attention_forward_and_weight_gather",
    )(x, wq, wk, wv, small, wo, w1, w2)


def layer_norm(stream, gain, shift):
    centre = stream - jnp.mean(stream, axis=-1, keepdims=True)
    variance = jnp.mean(centre * centre, axis=-1, keepdims=True)
    return centre * lax.rsqrt(variance + 1e-05) * gain + shift


def gelu_exact(inputs):
    return jax.nn.gelu(inputs, approximate=False)


def column_sums(matrix):
    return jnp.sum(matrix.astype(f32), axis=0)


def local(
    layer_input,
    query_weight,
    key_weight,
    value_weight,
    output_weight,
    query_bias,
    value_bias,
    output_bias,
    attn_gain,
    attn_shift,
    in_weight,
    in_bias,
    out_weight,
    out_bias,
    out_gain,
    out_shift,
    out_cotangent,
):
    F = lax.axis_size("fsdp")
    S = lax.axis_size("seq")
    width = layer_input.shape[-1]
    tokens = layer_input.reshape(-1, width)
    rows = tokens.shape[0]
    vec = query_bias.shape[0]
    vectors = (query_bias, value_bias, output_bias, attn_gain, attn_shift, out_bias, out_gain, out_shift)
    fan = in_bias.shape[0] // vec
    small = jnp.concatenate(
        [v.reshape(1, vec) for v in vectors]
        + [in_bias.reshape(fan, vec), jnp.zeros((16 - len(vectors) - fan, vec), bf16)]
    )
    (xfull, wqkv, smalls, q, k, v, qt, kt, ot, lse, mixed, wo, w1, w2) = forward(
        S, F, tokens, query_weight, key_weight, value_weight, small, output_weight, in_weight, out_weight
    )
    smalls = smalls.reshape(F, 16, vec).astype(f32)
    bias_output, gain_one, shift_one, bias_out, gain_two, shift_two = (
        smalls[:, i].reshape(width) for i in range(2, 8)
    )
    bias_in = smalls[:, 8 : 8 + fan].reshape(-1)
    tokens_single = tokens.astype(f32)
    attn_out = jnp.dot(mixed, wo, preferred_element_type=f32) + bias_output
    normed, pull_first = jax.vjp(layer_norm, tokens_single + attn_out, gain_one, shift_one)
    normed_low = normed.astype(bf16)
    hidden_pre = jnp.dot(normed_low, w1, preferred_element_type=f32) + bias_in
    hidden_single, pull_gelu = jax.vjp(gelu_exact, hidden_pre)
    hidden = hidden_single.astype(bf16)
    branch = jnp.dot(hidden, w2, preferred_element_type=f32) + bias_out
    layer_out, pull_second = jax.vjp(layer_norm, normed + branch, gain_two, shift_two)
    squares = jnp.stack(
        [jnp.sum(t * t) for t in (tokens_single, attn_out, normed, branch, layer_out)]
    )
    cotangent = out_cotangent.reshape(rows, width).astype(f32)
    grad_stream, grad_gain_two, grad_shift_two = pull_second(cotangent)
    grad_branch = grad_stream.astype(bf16)
    grad_bias_out = column_sums(grad_branch)
    grad_out = jnp.dot(hidden.T, grad_branch, preferred_element_type=f32)
    grad_hidden = jnp.dot(grad_branch, w2.T, preferred_element_type=f32)
    grad_pre = pull_gelu(grad_hidden)[0].astype(bf16)
    grad_bias_in = column_sums(grad_pre)
    grad_in = jnp.dot(normed_low.T, grad_pre, preferred_element_type=f32)
    grad_normed = grad_stream + jnp.dot(grad_pre, w1.T, preferred_element_type=f32)
    grad_h, grad_gain_one, grad_shift_one = pull_first(grad_normed)
    grad_attn = grad_h.astype(bf16)
    grad_bias_output = column_sums(grad_attn)
    grad_output = jnp.dot(mixed.T, grad_attn, preferred_element_type=f32)
    grad_mixed = jnp.dot(grad_attn, wo.T, preferred_element_type=f32).astype(bf16)
    grad_mixed = lax.all_to_all(grad_mixed, "seq", split_axis=1, concat_axis=0, tiled=True)
    length, wide = q.shape
    heads = wide // HD
    blocks = length // min(512, length)
    split = lambda t: t.reshape(length, heads, HD)
    keys, values = split(k), split(v)
    lse = lse[:heads].reshape(heads, blocks, length // blocks).swapaxes(0, 1)

    def backward_block(carry, parts):
        grad_keys, grad_values = carry
        query_block, total, grad_block = parts
        scores = jnp.einsum("qhd,khd->hqk", query_block, keys, preferred_element_type=f32)
        probs = jnp.exp(scores - total[..., None])
        grad_probs = jnp.einsum("qhd,khd->hqk", grad_block, values, preferred_element_type=f32)
        delta = jnp.sum(probs * grad_probs, axis=-1, keepdims=True)
        grad_scores = (probs * (grad_probs - delta)).astype(bf16)
        grad_query = jnp.einsum("hqk,khd->qhd", grad_scores, keys, preferred_element_type=f32) * 0.125
        grad_keys += jnp.einsum("hqk,qhd->khd", grad_scores, query_block, preferred_element_type=f32)
        grad_values += jnp.einsum("hqk,qhd->khd", probs.astype(bf16), grad_block, preferred_element_type=f32)
        return ((grad_keys, grad_values), grad_query.astype(bf16))

    in_blocks = lambda t: t.reshape(blocks, length // blocks, heads, HD)
    zero = jnp.zeros((length, heads, HD), f32)
    (grad_keys, grad_values), grad_queries = lax.scan(
        backward_block, (zero, zero), (in_blocks(q), lse, in_blocks(grad_mixed))
    )
    grad_q = grad_queries.reshape(length, wide)
    grad_k = grad_keys.reshape(length, wide).astype(bf16)
    grad_v = grad_values.reshape(length, wide).astype(bf16)
    grads = jnp.concatenate([grad_q, grad_k, grad_v], axis=1)
    input_part = jnp.dot(grads, wqkv.T, preferred_element_type=f32)
    input_grad = grad_h + lax.psum_scatter(input_part, "seq", scatter_dimension=0, tiled=True)
    grad_qkv = jnp.dot(xfull.T, grads, preferred_element_type=f32)

    def over_fsdp(t):
        return lax.psum_scatter(t, "fsdp", scatter_dimension=0, tiled=True)

    wide_sums = over_fsdp(grad_qkv.astype(bf16))
    wide_sums = lax.all_gather(wide_sums, "seq", axis=0, tiled=False).astype(f32)
    grad_query, grad_key, grad_value = (
        wide_sums[:, :, i * wide : (i + 1) * wide].swapaxes(0, 1).reshape(-1, width) for i in range(3)
    )
    weights = [
        lax.psum(over_fsdp(t.astype(bf16)), "seq").astype(f32) for t in (grad_output, grad_in, grad_out)
    ]
    bias_q = lax.all_gather(column_sums(grad_q), "seq", axis=0, tiled=True)
    bias_v = lax.all_gather(column_sums(grad_v), "seq", axis=0, tiled=True)
    sums = jnp.stack(
        [
            bias_q / S,
            bias_v / S,
            grad_bias_output,
            grad_gain_one,
            grad_shift_one,
            grad_bias_out,
            grad_gain_two,
            grad_shift_two,
        ]
    )
    f = lax.axis_index("fsdp")
    extra = jnp.zeros((1, width), f32).at[0, :5].set(squares)
    table = jnp.concatenate([sums, grad_bias_in.reshape(fan, width), extra])
    table = lax.psum(table, ("seq", "fsdp"))
    small_grads = lax.dynamic_slice_in_dim(table[:8], f * vec, vec, 1)
    grad_bias_in = lax.dynamic_slice_in_dim(table[8 : 8 + fan].reshape(-1), f * vec * fan, vec * fan, 0)
    rms = jnp.sqrt(table[8 + fan, :5] / f32(rows * width * S * F))
    return (
        layer_out.astype(bf16).reshape(layer_input.shape),
        input_grad.reshape(layer_input.shape),
        grad_query,
        grad_key,
        grad_value,
        weights[0],
        small_grads[0],
        small_grads[1],
        small_grads[2],
        small_grads[3],
        small_grads[4],
        weights[1],
        grad_bias_in,
        weights[2],
        small_grads[5],
        small_grads[6],
        small_grads[7],
        rms,
    )


def solution(mesh):
    placed = (
        P("fsdp", "seq", None),
        P("fsdp", None),
        P("fsdp", None),
        P("fsdp", None),
        P("fsdp", None),
        P("fsdp"),
        P("fsdp"),
        P("fsdp"),
        P("fsdp"),
        P("fsdp"),
        P("fsdp", None),
        P("fsdp"),
        P("fsdp", None),
        P("fsdp"),
        P("fsdp"),
        P("fsdp"),
        P("fsdp", "seq", None),
    )
    return jax.shard_map(
        local,
        mesh=mesh,
        in_specs=placed,
        out_specs=(
            P("fsdp", "seq", None),
            P("fsdp", "seq", None),
            P("fsdp", None),
            P("fsdp", None),
            P("fsdp", None),
            P("fsdp", None),
            P("fsdp"),
            P("fsdp"),
            P("fsdp"),
            P("fsdp"),
            P("fsdp"),
            P("fsdp", None),
            P("fsdp"),
            P("fsdp", None),
            P("fsdp"),
            P("fsdp"),
            P("fsdp"),
            P(),
        ),
        check_vma=False,
    )
```

```python
import functools
import jax
import jax.numpy as jnp
from jax import lax
from jax.experimental import pallas as pl
from jax.experimental.pallas import tpu as pltpu
from jax.sharding import PartitionSpec as P

HD = 64
MESH = pl.DeviceIdType.MESH
bf16 = jnp.bfloat16
f32 = jnp.float32


def each(lo, hi, body):
    if hi - lo <= 8:
        for i in range(lo, hi):
            body(i)
    else:
        pl.loop(lo, hi)(body)


class Grid:
    def __init__(self, seq_count, fsdp_count):
        self.S, self.F = seq_count, fsdp_count
        self.H = seq_count // 2
        self.Y = 2 if fsdp_count % 2 == 0 and fsdp_count <= 8 else 4
        self.Z = fsdp_count // self.Y
        self.s = lax.axis_index("seq")
        self.f = lax.axis_index("fsdp")
        self.c = self.s % 2
        self.hi = self.s // 2
        self.z = self.f // self.Y
        self.y = self.f % self.Y

    def zp(self, k):
        return ((self.z + k) % self.Z) * self.Y + self.y

    def yp(self, j):
        return self.z * self.Y + (self.y + j) % self.Y

    def xp(self, m):
        return ((self.hi + m) % self.H) * 2 + self.c

    def sib(self):
        return self.hi * 2 + 1 - self.c

    def origin(self, r):
        j, k = r // self.Z, r % self.Z
        return ((self.z + self.Z - k) % self.Z) * self.Y + (self.y + self.Y - j) % self.Y

    def greet(self, barrier):
        count = 0
        for m in range(self.H):
            for flip in range(2):
                if m or flip:
                    to = ((self.hi + m) % self.H) * 2 + (self.c + flip) % 2
                    pl.semaphore_signal(barrier, inc=1, device_id=(to, self.f), device_id_type=MESH)
                    count += 1
        for k in range(1, self.Z):
            pl.semaphore_signal(barrier, inc=1, device_id=(self.s, self.zp(k)), device_id_type=MESH)
            count += 1
        for j in range(1, self.Y):
            pl.semaphore_signal(barrier, inc=1, device_id=(self.s, self.yp(j)), device_id_type=MESH)
            count += 1
        pl.semaphore_wait(barrier, count)


class Sems:
    def __init__(self):
        self.n = 0

    def take(self, n):
        at = self.n
        self.n += n
        return at


def rcopy(sems, src, dst, send, recv, to):
    return pltpu.make_async_remote_copy(
        src_ref=src,
        dst_ref=dst,
        send_sem=sems.at[send],
        recv_sem=sems.at[recv],
        device_id=to,
        device_id_type=MESH,
    )


class Gather:
    def __init__(self, alloc, S, F, Y, kind):
        self.kind = kind
        Z = F // Y
        self.zs = alloc.take(Z)
        self.ys = alloc.take(Y * Z)
        self.ir = alloc.take(F)
        if kind != "own":
            self.ss, self.sr = alloc.take(F), alloc.take(F)
        if kind == "quarter":
            H = S // 2
            self.xs, self.xr = alloc.take(H * F), alloc.take(H * F)
            self.ts, self.tr = alloc.take(H * F), alloc.take(H * F)

    def bind(self, g, sems, piece, place):
        self.g, self.sems, self.piece, self.place = g, sems, piece, place

    def part(self, hi=None, c=None):
        g = self.g
        c = g.c if c is None else c
        hi = g.hi if hi is None else hi
        return {"own": g.s, "half": c, "quarter": hi * 2 + c}[self.kind]

    def start(self):
        g, p = self.g, self.part()
        src, dst = self.piece(p), self.place(g.f, p)
        for k in range(1, g.Z):
            rcopy(self.sems, src, dst, self.zs + k, self.ir + k, (g.s, g.zp(k))).start()
        for j in range(1, g.Y):
            rcopy(self.sems, src, dst, self.ys + j * g.Z, self.ir + j * g.Z, (g.s, g.yp(j))).start()

    def wait_in(self, r):
        ref = self.place(self.g.origin(r), self.part())
        rcopy(self.sems, ref, ref, self.ir + r, self.ir + r, (self.g.sib(), self.g.f)).wait_recv()

    def pass_on(self, r):
        g = self.g
        ref = self.place(g.origin(r), self.part())
        if self.kind == "quarter":
            for m in range(1, g.H):
                rcopy(self.sems, ref, ref, self.xs + m * g.F + r, self.xr + m * g.F + r, (g.xp(m), g.f)).start()
        if self.kind != "own":
            rcopy(self.sems, ref, ref, self.ss + r, self.sr + r, (g.sib(), g.f)).start()

    def on_z(self):
        g = self.g

        def body(k):
            self.wait_in(k)
            ref = self.place(g.origin(k), self.part())
            for j in range(1, g.Y):
                at = j * g.Z + k
                rcopy(self.sems, ref, ref, self.ys + at, self.ir + at, (g.s, g.yp(j))).start()
            self.pass_on(k)

        each(1, g.Z, body)

    def on_y(self):
        def body(r):
            self.wait_in(r)
            self.pass_on(r)

        each(self.g.Z, self.g.F, body)

    def on_x(self):
        if self.kind != "quarter":
            return
        g = self.g
        for m in range(1, g.H):
            part = self.part(hi=(g.hi + g.H - m) % g.H)

            def body(r):
                ref = self.place(g.origin(r), part)
                at = m * g.F + r
                rcopy(self.sems, ref, ref, self.xr + at, self.xr + at, (g.sib(), g.f)).wait_recv()
                rcopy(self.sems, ref, ref, self.ts + at, self.tr + at, (g.sib(), g.f)).start()

            each(1, g.F, body)

    def finish(self):
        g = self.g
        other = 1 - g.c

        def sent(ref, at):
            rcopy(self.sems, ref, ref, at, at, (g.sib(), g.f)).wait_send()

        def got(ref, at):
            rcopy(self.sems, ref, ref, at, at, (g.sib(), g.f)).wait_recv()

        if self.kind != "own":
            each(1, g.F, lambda r: got(self.place(g.origin(r), self.part(c=other)), self.sr + r))
        if self.kind == "quarter":
            for m in range(1, g.H):
                part = self.part(hi=(g.hi + g.H - m) % g.H, c=other)
                each(1, g.F, lambda r: got(self.place(g.origin(r), part), self.tr + m * g.F + r))
        mine = self.piece(self.part())
        for k in range(1, g.Z):
            sent(mine, self.zs + k)
        for j in range(1, g.Y):
            each(0, g.Z, lambda k: sent(mine, self.ys + j * g.Z + k))
        if self.kind != "own":
            each(1, g.F, lambda r: sent(mine, self.ss + r))
        if self.kind == "quarter":
            for m in range(1, g.H):
                each(1, g.F, lambda r: sent(mine, self.xs + m * g.F + r))
                each(1, g.F, lambda r: sent(mine, self.ts + m * g.F + r))


def forward_kernel(plan, x, wq, wk, wv, small, wo, w1, w2, *rest):
    (xfull, wqkv, smalls, q_o, k_o, v_o, qt_o, kt_o, ot_o, lse_o, mixed, wo_f, w1_f, w2_f) = rest[:14]
    (xs, ws, sm, qn, kn, vn, qt, kt, vt, ot, lse, oblk, onat, sems) = rest[14:]
    S, F, rows, length, heads, wide, vec = plan.S, plan.F, plan.rows, plan.length, plan.heads, plan.wide, plan.vec
    g = Grid(S, F)
    g.greet(pltpu.get_barrier_semaphore())
    part_rows = wq.shape[0]
    local = []

    def keep(src, dst, at):
        copy = pltpu.make_async_copy(src, dst, sems.at[at])
        copy.start()
        return copy

    mine = xs.at[pl.ds(g.s * rows, rows)]
    x_out = [rcopy(sems, x, mine, plan.x_s, plan.x_r, (g.sib(), g.f))]
    for m in range(1, g.H):
        x_out.append(rcopy(sems, x, mine, plan.x_s + m, plan.x_r + m, (g.xp(m), g.f)))
    for copy in x_out[::-1]:
        copy.start()
    for item, src, col in ((plan.gq, wq, 0), (plan.gk, wk, 1), (plan.gv, wv, 2)):
        item.bind(
            g,
            sems,
            lambda p, src=src: src.at[:, pl.ds(p * wide, wide)],
            lambda o, p, col=col: ws.at[pl.ds(o * part_rows, part_rows), pl.ds(col * wide, wide)],
        )
        item.start()
    plan.gs.bind(g, sems, lambda p: small, lambda o, p: sm.at[pl.ds(o * 16, 16)])
    plan.gs.start()
    local.append(keep(x, mine, plan.l))
    for col, src in enumerate((wq, wk, wv)):
        local.append(
            keep(
                src.at[:, pl.ds(g.s * wide, wide)],
                ws.at[pl.ds(g.f * part_rows, part_rows), pl.ds(col * wide, wide)],
                plan.l + 1 + col,
            )
        )
    local.append(keep(small, sm.at[pl.ds(g.f * 16, 16)], plan.l + 4))
    own = []
    for i, (src, dst) in enumerate(((wo, wo_f), (w1, w1_f), (w2, w2_f))):
        n = src.shape[0]
        own.append(keep(src, dst.at[pl.ds(g.f * n, n)], plan.l + 5 + i))
    for src, dst, (item, lo, width) in [
        (src, dst, entry)
        for src, dst, entries in ((wo, wo_f, plan.go), (w1, w1_f, plan.g1), (w2, w2_f, plan.g2))
        for entry in entries
    ]:
        n = src.shape[0]
        item.bind(
            g,
            sems,
            lambda p, src=src, lo=lo, width=width: src.at[:, pl.ds(lo + p * width, width)],
            lambda o, p, dst=dst, n=n, lo=lo, width=width: dst.at[pl.ds(o * n, n), pl.ds(lo + p * width, width)],
        )
    big = [e[0] for e in plan.g1 + plan.go + plan.g2]
    for item in (plan.gq, plan.gk, plan.gv, plan.gs):
        item.on_z()
    x_pass = []
    for m in range(1, g.H):
        theirs = xs.at[pl.ds(((g.hi + g.H - m) % g.H * 2 + g.c) * rows, rows)]
        rcopy(sems, theirs, theirs, plan.x_s, plan.x_r + m, (g.sib(), g.f)).wait_recv()
        copy = rcopy(sems, theirs, theirs, plan.x_s + g.H + m, plan.x_r + g.H + m, (g.sib(), g.f))
        copy.start()
        x_pass.append(copy)
    for item in (plan.gq, plan.gk, plan.gv, plan.gs):
        item.on_y()
    for item in big:
        item.start()
    rcopy(sems, mine, mine, plan.x_s, plan.x_r, (g.sib(), g.f)).wait_recv()
    for m in range(1, g.H):
        rcopy(sems, mine, mine, plan.x_s, plan.x_r + g.H + m, (g.sib(), g.f)).wait_recv()
    for copy in local:
        copy.wait()

    table = sm[...]
    lane = lax.broadcasted_iota(jnp.int32, (vec, wide), 1)
    spread = (lane % vec == lax.broadcasted_iota(jnp.int32, (vec, wide), 0)).astype(f32).astype(bf16)
    spread = jnp.dot(table, spread, preferred_element_type=f32)
    row = lax.broadcasted_iota(jnp.int32, spread.shape, 0)
    column = lax.broadcasted_iota(jnp.int32, spread.shape, 1)

    def vector(i):
        want = (g.s * (wide // vec) + column // vec) * 16 + i
        return jnp.sum(jnp.where(row == want, spread, 0.0), axis=0, keepdims=True)

    bias_q, bias_v = vector(0), vector(1)

    @pl.loop(0, S)
    def _(b):
        at = pl.multiple_of(b * rows, rows)
        prod = jnp.dot(xs[pl.ds(at, rows), :], ws[...], preferred_element_type=f32)
        q = (prod[:, :wide] + bias_q).astype(bf16).astype(f32) * 0.125
        k = prod[:, wide : 2 * wide]
        v = prod[:, 2 * wide :] + bias_v
        qn[pl.ds(at, rows), :] = q.astype(bf16)
        kn[pl.ds(at, rows), :] = k.astype(bf16)
        vn[pl.ds(at, rows), :] = v.astype(bf16)
        qt[:, pl.ds(at, rows)] = q.T.astype(bf16)
        kt[:, pl.ds(at, rows)] = k.T.astype(bf16)
        vt[:, pl.ds(at, rows)] = v.T.astype(bf16)

    stores = [
        keep(src, dst, plan.l + 8 + i)
        for i, (src, dst) in enumerate(
            ((xs, xfull), (ws, wqkv), (sm, smalls), (qn, q_o), (kn, k_o), (vn, v_o), (qt, qt_o), (kt, kt_o))
        )
    ]
    head_of = lax.broadcasted_iota(jnp.int32, (wide, rows), 0) // HD
    sent = []
    for t in range(S):
        hi = (g.hi + 1 + t // 2) % g.H
        c = (g.c + t + t // (2 * (g.H - 1))) % 2
        to = hi * 2 + c
        at = pl.multiple_of(to * rows, rows)

        @pl.loop(0, heads)
        def _(h):
            q = jnp.where(head_of == h, qt[:, pl.ds(at, rows)], jnp.zeros((), bf16))
            s = jnp.dot(kn[...], q, preferred_element_type=f32)
            m = jnp.max(s, axis=0, keepdims=True)
            e = jnp.exp(s - m)
            l = jnp.sum(e, axis=0, keepdims=True)
            band = pl.ds(pl.multiple_of(h * HD, HD), HD)
            o = jnp.dot(vt[band, :], e.astype(bf16), preferred_element_type=f32) / l
            oblk[band, :] = o
            lse[pl.ds(h, 1), pl.ds(at, rows)] = m + jnp.log(l)

        ot[:, pl.ds(at, rows)] = oblk[...].astype(bf16)
        onat[t] = oblk[...].T.astype(bf16)
        dst = mixed.at[:, pl.ds(g.s * wide, wide)]
        if t < S - 1:
            copy = rcopy(sems, onat.at[t], dst, plan.o_s + t, plan.o_r + g.s, (to, g.f))
            copy.start()
            sent.append(copy)
        else:
            stores.append(keep(onat.at[t], dst, plan.o_s + t))
    stores.append(keep(ot, ot_o, plan.l + 16))
    stores.append(keep(lse, lse_o, plan.l + 17))
    for i, item in enumerate(big):
        if i == 0:
            item.on_z()
        item.on_y()
        if i + 1 < len(big):
            big[i + 1].on_z()
        item.on_x()
    for item in (plan.gq, plan.gk, plan.gv, plan.gs, *big):
        item.finish()
    for i in range(1, S):
        peer = (g.s + i) % S
        ref = mixed.at[:, pl.ds(peer * wide, wide)]
        rcopy(sems, ref, ref, plan.o_r + peer, plan.o_r + peer, (peer, g.f)).wait_recv()
    for copy in sent + x_out + x_pass:
        copy.wait_send()
    for copy in stores + own:
        copy.wait()


class Plan:
    pass


def forward_plan(S, F, rows, width, ff):
    plan = Plan()
    alloc = Sems()
    plan.S, plan.F, plan.rows, plan.length = S, F, rows, rows * S
    plan.wide = width // S
    plan.heads = plan.wide // HD
    plan.vec = width // F
    Y = 2 if F % 2 == 0 and F <= 8 else 4
    plan.x_s, plan.x_r = alloc.take(S), alloc.take(S)
    plan.gq, plan.gk, plan.gv, plan.gs = (Gather(alloc, S, F, Y, "own") for _ in range(4))
    half = width // 2
    plan.go = [(Gather(alloc, S, F, Y, "half"), 0, half)]
    eighth = ff // 2 // S
    plan.g1 = [(Gather(alloc, S, F, Y, "quarter"), i * S * eighth, eighth) for i in range(2)]
    plan.g2 = [(Gather(alloc, S, F, Y, "half"), i * half, half // 2) for i in range(2)]
    plan.o_s, plan.o_r = alloc.take(S), alloc.take(S)
    plan.l = alloc.take(20)
    plan.sems = alloc.n
    return plan


def forward(S, F, x, wq, wk, wv, small, wo, w1, w2):
    rows, width = x.shape
    ff = w1.shape[1]
    plan = forward_plan(S, F, rows, width, ff)
    length, wide, heads = plan.length, plan.wide, plan.heads
    sds = jax.ShapeDtypeStruct
    any_ = pl.BlockSpec(memory_space=pl.ANY)
    return pl.pallas_call(
        functools.partial(forward_kernel, plan),
        out_shape=(
            sds((length, width), bf16),
            sds((width, 3 * wide), bf16),
            sds((F * 16, plan.vec), bf16),
            sds((length, wide), bf16),
            sds((length, wide), bf16),
            sds((length, wide), bf16),
            sds((wide, length), bf16),
            sds((wide, length), bf16),
            sds((wide, length), bf16),
            sds((8, length), f32),
            sds((rows, width), bf16),
            sds((width, width), bf16),
            sds((width, ff), bf16),
            sds((ff, width), bf16),
        ),
        in_specs=[any_] * 8,
        out_specs=(any_,) * 14,
        scratch_shapes=[
            pltpu.VMEM((length, width), bf16),
            pltpu.VMEM((width, 3 * wide), bf16),
            pltpu.VMEM((F * 16, plan.vec), bf16),
            pltpu.VMEM((length, wide), bf16),
            pltpu.VMEM((length, wide), bf16),
            pltpu.VMEM((length, wide), bf16),
            pltpu.VMEM((wide, length), bf16),
            pltpu.VMEM((wide, length), bf16),
            pltpu.VMEM((wide, length), bf16),
            pltpu.VMEM((wide, length), bf16),
            pltpu.VMEM((8, length), f32),
            pltpu.VMEM((wide, rows), f32),
            pltpu.VMEM((S, rows, wide), bf16),
            pltpu.SemaphoreType.DMA((plan.sems,)),
        ],
        compiler_params=pltpu.CompilerParams(collective_id=0, has_side_effects=True, vmem_limit_bytes=48 << 20),
        name="attention_forward_and_weight_gather",
    )(x, wq, wk, wv, small, wo, w1, w2)


class Reduce:
    def __init__(self, alloc, S, F, Y, R, C, kind):
        self.kind, self.R, self.C = kind, R, C
        self.S, self.F, self.Y, self.Z, self.H = S, F, Y, F // Y, S // 2
        Z, H = self.Z, self.H
        self.w = {"half": C // 2, "quarter": C // S, "own": C}[kind]
        w = self.w
        self.n = H if kind == "quarter" else 1
        self.shapes = [(self.n, Z, Y, R, w), (Y - 1, Z, R, w), (Z, R, w)]
        if kind == "own":
            self.shapes += [(S, R, w)]
        else:
            self.shapes += [(self.n, Z, Y, R, w), (R, C)]
            self.shapes += [(H - 1, Z, Y, R, w) if kind == "quarter" else (H - 1, R, w)]
        self.shapes = [pltpu.VMEM(s, bf16) for s in self.shapes]
        self.load = alloc.take(H)
        self.ds, self.dr = alloc.take(H), alloc.take(H)
        self.xs, self.xr = alloc.take(H), alloc.take(H)
        self.ys, self.yr = alloc.take(Y), alloc.take(Y)
        self.zs, self.zr = alloc.take(Z), alloc.take(Z)
        self.fs, self.fr = alloc.take(2 * H), alloc.take(2 * H)
        self.out = alloc.take(1)

    def bind(self, g, sems, refs, source, dest):
        self.g, self.sems, self.source, self.dest = g, sems, source, dest
        if self.kind == "own":
            self.own, self.ry, self.rz, self.fin = refs
        else:
            self.own, self.ry, self.rz, self.rd, self.fin, self.rx = refs
        self.sends = []

    def send(self, src, dst, s, r, to):
        copy = rcopy(self.sems, src, dst, s, r, to)
        copy.start()
        self.sends.append(copy)

    def recv(self, ref, r):
        rcopy(self.sems, ref, ref, r, r, (self.g.sib(), self.g.f)).wait_recv()

    def column(self, hi, c):
        return (hi * 2 + c) * self.w if self.kind == "quarter" else c * self.w

    def start(self):
        g = self.g
        self.loads = []
        for m in range(self.n):
            hi = (g.hi + m) % g.H
            self.send(
                self.source(self.column(hi, 1 - g.c), self.w),
                self.rd.at[m],
                self.ds + m,
                self.dr + m,
                (g.sib(), g.f),
            )
            copy = pltpu.make_async_copy(
                self.source(self.column(hi, g.c), self.w), self.own.at[m], self.sems.at[self.load + m]
            )
            copy.start()
            self.loads.append(copy)

    def add_all(self, m, other):
        @pl.loop(0, self.Z * self.Y)
        def _(i):
            a, b = i // self.Y, i % self.Y
            self.own[m, a, b] = (self.own[m, a, b].astype(f32) + other(a, b).astype(f32)).astype(bf16)

    def over_cores(self):
        for m in list(range(1, self.n)) + [0]:
            self.loads[m].wait()
            self.recv(self.rd.at[m], self.dr + m)
            self.add_all(m, lambda a, b: self.rd[m, a, b])
            if m:
                self.send(self.own.at[m], self.rx.at[m - 1], self.xs + m, self.xr + m, (self.g.xp(m), self.g.f))
        if self.kind == "half":
            self.send_y()

    def over_x_first(self):
        for m in range(1, self.H):
            self.recv(self.rx.at[m - 1], self.xr + m)
            self.add_all(0, lambda a, b: self.rx[m - 1, a, b])
        self.send_y()

    def send_y(self):
        g = self.g
        for j in range(1, g.Y):
            y = (g.y + j) % g.Y
            self.send(self.own.at[0, :, y], self.ry.at[j - 1], self.ys + j, self.yr + j, (g.s, g.yp(j)))

    def over_y(self):
        g = self.g
        for j in range(1, g.Y):
            self.recv(self.ry.at[j - 1], self.yr + j)

        @pl.loop(0, self.Z)
        def _(a):
            total = self.own[0, a, g.y].astype(f32)
            for j in range(1, g.Y):
                total += self.ry[j - 1, a].astype(f32)
            self.own[0, a, g.y] = total.astype(bf16)

        for k in range(1, g.Z):
            z = (g.z + k) % g.Z
            self.send(self.own.at[0, z, g.y], self.rz.at[k], self.zs + k, self.zr + k, (g.s, g.zp(k)))

    def over_z(self):
        g = self.g
        total = self.own[0, g.z, g.y].astype(f32)
        for k in range(1, g.Z):
            self.recv(self.rz.at[k], self.zr + k)
            total += self.rz[k].astype(f32)
        total = total.astype(bf16)
        if self.kind == "half":
            self.rz[0] = total
            for m in range(1, g.H):
                self.send(self.rz.at[0], self.rx.at[m - 1], self.xs + m, self.xr + m, (g.xp(m), g.f))
            return
        if self.kind == "own":
            self.fin[g.s] = total
            ref = self.fin.at[g.s]
        else:
            at = pl.multiple_of(self.column(g.hi, g.c), self.w)
            self.fin[:, pl.ds(at, self.w)] = total
            ref = self.fin.at[:, pl.ds(at, self.w)]
        for m in range(1, g.H):
            self.send(ref, ref, self.fs + m, self.fr + m, (g.xp(m), g.f))
        self.send(ref, ref, self.fs, self.fr, (g.sib(), g.f))

    def over_x_last(self):
        g = self.g
        if self.kind == "half":
            total = self.rz[0].astype(f32)
            for m in range(1, g.H):
                self.recv(self.rx.at[m - 1], self.xr + m)
                total += self.rx[m - 1].astype(f32)
            at = pl.multiple_of(g.c * self.w, self.w)
            self.fin[:, pl.ds(at, self.w)] = total.astype(bf16)
            ref = self.fin.at[:, pl.ds(at, self.w)]
            self.send(ref, ref, self.fs, self.fr, (g.sib(), g.f))
            return
        for m in range(1, g.H):
            hi = (g.hi + g.H - m) % g.H
            if self.kind == "own":
                ref = self.fin.at[hi * 2 + g.c]
            else:
                ref = self.fin.at[:, pl.ds(self.column(hi, g.c), self.w)]
            self.recv(ref, self.fr + m)
            self.send(ref, ref, self.fs + g.H + m, self.fr + g.H + m, (g.sib(), g.f))

    def finish(self):
        g = self.g
        for m in range(g.H if self.kind != "half" else 1):
            hi = (g.hi + g.H - m) % g.H
            if self.kind == "own":
                ref = self.fin.at[hi * 2 + 1 - g.c]
            else:
                ref = self.fin.at[:, pl.ds(self.column(hi, 1 - g.c), self.w)]
            self.recv(ref, self.fr + (g.H + m if m else 0))
        self.copy_out = pltpu.make_async_copy(self.fin, self.dest, self.sems.at[self.out])
        self.copy_out.start()

    def done(self):
        for copy in self.sends:
            copy.wait_send()
        self.copy_out.wait()

    def steps(self):
        if self.kind == "half":
            return [self.over_y, self.over_z, self.over_x_last, self.finish]
        if self.kind == "quarter":
            return [self.over_x_first, self.over_y, self.over_z, self.over_x_last, self.finish]
        return [self.over_y, self.over_z, self.over_x_last, self.finish]


def backward_kernel(plan, g_o, q_i, k_i, v_i, qt_i, kt_i, ot_i, lse_i, x_i, w_i, gh, table_i, dwo, dw1, dw2, *rest):
    dx_o, dqkv_o, dwo_o, dw1_o, dw2_o, table_o = rest[:6]
    (go, qn, kn, vn, qt, kt, ot, lse, xs, ws, dk, dv, dqt, dt, delta, grads) = rest[6:22]
    (dx, dx_send, dx_core, dx_out, dx_x, tab, tab_core, tab_x, tab_y, tab_s, tab_z, sems) = rest[22:34]
    pools = rest[34:]
    S, F, rows, heads, wide, vec = plan.S, plan.F, plan.rows, plan.heads, plan.wide, plan.vec
    g = Grid(S, F)
    g.greet(pltpu.get_barrier_semaphore())

    def keep(src, dst, at):
        copy = pltpu.make_async_copy(src, dst, sems.at[at])
        copy.start()
        return copy

    sent = []

    def send(src, dst, s, r, to):
        copy = rcopy(sems, src, dst, s, r, to)
        copy.start()
        sent.append(copy)

    def recv(ref, r):
        rcopy(sems, ref, ref, r, r, (g.sib(), g.f)).wait_recv()

    for m in [*range(1, g.H), 0]:
        for flip in range(2):
            if m or flip:
                to = ((g.hi + m) % g.H) * 2 + (g.c + flip) % 2
                send(
                    g_o.at[:, pl.ds(to * wide, wide)],
                    go.at[g.s],
                    plan.o_s + m * 2 + flip,
                    plan.o_r + g.s,
                    (to, g.f),
                )
    used = 0
    for item, which, col, row in plan.items:
        n = len(item.shapes)
        src, dst = {"o": (dwo, dwo_o), "1": (dw1, dw1_o), "2": (dw2, dw2_o)}[which]
        item.bind(
            g,
            sems,
            pools[used : used + n],
            lambda lo, width, src=src, item=item, col=col, row=row: src.at[
                :, :, pl.ds(row, item.R), pl.ds(col + lo, width)
            ],
            dst.at[pl.ds(row, item.R), pl.ds(col, item.C)],
        )
        used += n
        item.start()
    plan.qkv.bind(g, sems, pools[used : used + 4], None, dqkv_o)
    loads = [
        keep(src, dst, plan.l + i)
        for i, (src, dst) in enumerate(
            (
                (g_o.at[:, pl.ds(g.s * wide, wide)], go.at[g.s]),
                (q_i, qn),
                (k_i, kn),
                (v_i, vn),
                (qt_i, qt),
                (kt_i, kt),
                (ot_i, ot),
                (lse_i, lse),
                (x_i, xs),
                (w_i, ws),
                (gh, dx),
                (table_i, tab),
            )
        )
    ]
    items = [entry[0] for entry in plan.items]
    for item in items:
        item.over_cores()
    waves = []
    for tick in range(len(items) + 5):
        for i, item in enumerate(items):
            steps = item.steps()
            if 0 <= tick - i < len(steps):
                waves.append((tick, steps[tick - i]))

    def run(upto):
        while waves and waves[0][0] <= upto:
            waves.pop(0)[1]()

    dk[...] = jnp.zeros_like(dk)
    dv[...] = jnp.zeros_like(dv)
    for copy in loads:
        copy.wait()
    for i in range(1, S):
        peer = (g.s + i) % S
        recv(go.at[peer], plan.o_r + peer)
    head_of = lax.broadcasted_iota(jnp.int32, (wide, rows), 0) // HD
    head_at = lax.broadcasted_iota(jnp.int32, (rows, wide), 1) // HD
    none = jnp.zeros((), bf16)
    for t in range(S):
        span = pl.ds(t * rows, rows)
        turned = go[t].astype(f32).T
        dt[...] = turned.astype(bf16)
        weighed = turned * ot[:, span].astype(f32)
        for h in range(heads):
            delta[pl.ds(h, 1), :] = jnp.sum(weighed[h * HD : (h + 1) * HD], axis=0, keepdims=True)

        @pl.loop(0, heads)
        def _(h):
            band = pl.ds(pl.multiple_of(h * HD, HD), HD)
            s = jnp.dot(kn[...], jnp.where(head_of == h, qt[:, span], none), preferred_element_type=f32)
            p = jnp.exp(s - lse[pl.ds(h, 1), span])
            dp = jnp.dot(vn[...], jnp.where(head_of == h, dt[...], none), preferred_element_type=f32)
            ds = (p * (dp - delta[pl.ds(h, 1), :])).astype(bf16)
            dv[...] += jnp.dot(p.astype(bf16), jnp.where(head_at == h, go[t], none), preferred_element_type=f32)
            dk[...] += jnp.dot(ds, jnp.where(head_at == h, qn[span, :], none), preferred_element_type=f32)
            dqt[band, span] = jnp.dot(kt[band, :], ds, preferred_element_type=f32) * 0.125

        run(plan.ticks[t])

    sum_q = jnp.zeros((1, wide), f32)
    sum_v = jnp.zeros((1, wide), f32)
    for t in range(S):
        span = pl.ds(t * rows, rows)
        q = dqt[:, span].T.astype(bf16)
        v = dv[span, :].astype(bf16)
        grads[span, pl.ds(0, wide)] = q
        grads[span, pl.ds(wide, wide)] = dk[span, :].astype(bf16)
        grads[span, pl.ds(2 * wide, wide)] = v
        sum_q += jnp.sum(q.astype(f32), axis=0, keepdims=True)
        sum_v += jnp.sum(v.astype(f32), axis=0, keepdims=True)
    Y, part_rows, width = g.Y, plan.qkv.R, xs.shape[1]
    step = max(part_rows, 256)
    for lo in range(0, width, step):
        prod = lax.dot_general(
            xs[:, pl.ds(lo, step)], grads[...], (((0,), (0,)), ((), ())), preferred_element_type=f32
        ).astype(bf16)
        for i in range(step // part_rows):
            to = lo // part_rows + i
            plan.qkv.own[0, to // Y, to % Y] = prod[i * part_rows : (i + 1) * part_rows]
    plan.qkv.send_y()
    def part(to):
        return lax.dot_general(
            grads[pl.ds(pl.multiple_of(to * rows, rows), rows), :],
            ws[...],
            (((1,), (1,)), ((), ())),
            preferred_element_type=f32,
        )

    for m in [*range(1, g.H), 0]:
        hi = (g.hi + m) % g.H
        dx_send[m] = part(hi * 2 + 1 - g.c).astype(bf16)
        send(dx_send.at[m], dx_core.at[m], plan.dx + m, plan.dx + g.H + m, (g.sib(), g.f))
    for m in [*range(1, g.H), 0]:
        hi = (g.hi + m) % g.H
        value = part(hi * 2 + g.c)
        recv(dx_core.at[m], plan.dx + g.H + m)
        value += dx_core[m].astype(f32)
        if m:
            dx_out[m - 1] = value.astype(bf16)
            send(dx_out.at[m - 1], dx_x.at[m - 1], plan.dx + 2 * g.H + m, plan.dx + 3 * g.H + m, (g.xp(m), g.f))
        else:
            dx[...] += value
    base = g.s * (wide // vec)
    for i in range(wide // vec):
        to = base + i
        for row, value in ((0, sum_q), (1, sum_v)):
            tab[to // Y, to % Y, pl.ds(row, 1), :] = value[:, i * vec : (i + 1) * vec]
    send(tab, tab_core, plan.t, plan.t + 1, (g.sib(), g.f))
    recv(tab_core, plan.t + 1)
    tab_x[g.hi] = tab[...] + tab_core[...]
    for m in range(1, g.H):
        send(tab_x.at[g.hi], tab_x.at[g.hi], plan.tx + m, plan.tx + g.H + g.hi, (g.xp(m), g.f))
    for m in range(1, g.H):
        hi = (g.hi + m) % g.H
        recv(tab_x.at[hi], plan.tx + g.H + hi)
    total = tab_x[0]
    for m in range(1, g.H):
        total += tab_x[m]
    tab_core[...] = total
    tab_y[g.y] = tab_core[:, g.y]
    for j in range(1, Y):
        y = (g.y + j) % Y
        send(tab_core.at[:, y], tab_y.at[g.y], plan.ty + j, plan.ty + Y + g.y, (g.s, g.yp(j)))
    for j in range(1, Y):
        y = (g.y + j) % Y
        recv(tab_y.at[y], plan.ty + Y + y)
    total = tab_y[0]
    for j in range(1, Y):
        total += tab_y[j]
    tab_s[...] = total
    tab_z[g.z] = tab_s[g.z]
    for k in range(1, g.Z):
        z = (g.z + k) % g.Z
        send(tab_s.at[z], tab_z.at[g.z], plan.tz + k, plan.tz + g.Z + g.z, (g.s, g.zp(k)))
    run(plan.ticks[S])
    for k in range(1, g.Z):
        z = (g.z + k) % g.Z
        recv(tab_z.at[z], plan.tz + g.Z + z)
    total = tab_z[0]
    for k in range(1, g.Z):
        total += tab_z[k]
    tab_y[0, 0] = total
    out = [keep(tab_y.at[0, 0], table_o, plan.l + 12)]
    ending = plan.qkv.steps()
    for i, step_of in enumerate(ending):
        run(plan.ticks[S] + 1 + i)
        step_of()
    run(1000)
    for m in range(1, g.H):
        recv(dx_x.at[m - 1], plan.dx + 3 * g.H + m)
        dx[...] += dx_x[m - 1].astype(f32)
    out.append(keep(dx, dx_o, plan.l + 13))
    for item in (*items, plan.qkv):
        item.done()
    for copy in sent:
        copy.wait_send()
    for copy in out:
        copy.wait()


def backward_plan(S, F, rows, width, ff):
    plan = Plan()
    alloc = Sems()
    plan.S, plan.F, plan.rows = S, F, rows
    plan.wide = width // S
    plan.heads = plan.wide // HD
    plan.vec = width // F
    Y = 2 if F % 2 == 0 and F <= 8 else 4
    R, R2 = width // F, ff // F
    ones = [(Reduce(alloc, S, F, Y, R, width, "quarter"), "1", i * width, 0) for i in range(ff // width)]
    twos = [(Reduce(alloc, S, F, Y, R2 // 4, width, "half"), "2", 0, i * (R2 // 4)) for i in range(4)]
    plan.items = [e for pair in zip(twos, ones) for e in pair]
    plan.items.append((Reduce(alloc, S, F, Y, R, width, "half"), "o", 0, 0))
    plan.qkv = Reduce(alloc, S, F, Y, R, 3 * plan.wide, "own")
    plan.o_s, plan.o_r = alloc.take(S), alloc.take(S)
    plan.dx = alloc.take(4 * S)
    plan.t, plan.tx, plan.ty, plan.tz = alloc.take(2), alloc.take(S), alloc.take(2 * Y), alloc.take(2 * F // Y)
    plan.l = alloc.take(14)
    plan.ticks = [1, 3, 5, 7, 9]
    plan.sems = alloc.n
    return plan


def backward(S, F, g_o, q, k, v, qt, kt, ot, lse, x, w, gh, table, dwo, dw1, dw2):
    rows, width = g_o.shape
    ff = dw1.shape[-1]
    plan = backward_plan(S, F, rows, width, ff)
    wide, vec = plan.wide, plan.vec
    length = rows * S
    Z, Y = table.shape[:2]
    H = S // 2
    R, R2 = width // F, ff // F
    sds = jax.ShapeDtypeStruct
    any_ = pl.BlockSpec(memory_space=pl.ANY)
    pools = [s for e in plan.items for s in e[0].shapes] + plan.qkv.shapes
    return pl.pallas_call(
        functools.partial(backward_kernel, plan),
        out_shape=(
            sds((rows, width), f32),
            sds((S, R, 3 * wide), bf16),
            sds((R, width), bf16),
            sds((R, ff), bf16),
            sds((R2, width), bf16),
            sds((16, vec), f32),
        ),
        in_specs=[any_] * 15,
        out_specs=(any_,) * 6,
        scratch_shapes=[
            pltpu.VMEM((S, rows, wide), bf16),
            pltpu.VMEM((length, wide), bf16),
            pltpu.VMEM((length, wide), bf16),
            pltpu.VMEM((length, wide), bf16),
            pltpu.VMEM((wide, length), bf16),
            pltpu.VMEM((wide, length), bf16),
            pltpu.VMEM((wide, length), bf16),
            pltpu.VMEM((8, length), f32),
            pltpu.VMEM((length, width), bf16),
            pltpu.VMEM((width, 3 * wide), bf16),
            pltpu.VMEM((length, wide), f32),
            pltpu.VMEM((length, wide), f32),
            pltpu.VMEM((wide, length), f32),
            pltpu.VMEM((wide, rows), bf16),
            pltpu.VMEM((8, rows), f32),
            pltpu.VMEM((length, 3 * wide), bf16),
            pltpu.VMEM((rows, width), f32),
            pltpu.VMEM((H, rows, width), bf16),
            pltpu.VMEM((H, rows, width), bf16),
            pltpu.VMEM((H - 1, rows, width), bf16),
            pltpu.VMEM((H - 1, rows, width), bf16),
            pltpu.VMEM((Z, Y, 16, vec), f32),
            pltpu.VMEM((Z, Y, 16, vec), f32),
            pltpu.VMEM((H, Z, Y, 16, vec), f32),
            pltpu.VMEM((Y, Z, 16, vec), f32),
            pltpu.VMEM((Z, 16, vec), f32),
            pltpu.VMEM((Z, 16, vec), f32),
            pltpu.SemaphoreType.DMA((plan.sems,)),
            *pools,
        ],
        compiler_params=pltpu.CompilerParams(collective_id=1, has_side_effects=True, vmem_limit_bytes=63 << 20),
        name="attention_backward_and_gradient_sums",
    )(g_o, q, k, v, qt, kt, ot, lse, x, w, gh, table, dwo, dw1, dw2)


def layer_norm(stream, gain, shift):
    centre = stream - jnp.mean(stream, axis=-1, keepdims=True)
    variance = jnp.mean(centre * centre, axis=-1, keepdims=True)
    return centre * lax.rsqrt(variance + 1e-05) * gain + shift


def gelu_exact(inputs):
    return jax.nn.gelu(inputs, approximate=False)


def column_sums(matrix):
    return jnp.sum(matrix.astype(f32), axis=0)


def local(
    layer_input,
    query_weight,
    key_weight,
    value_weight,
    output_weight,
    query_bias,
    value_bias,
    output_bias,
    attn_gain,
    attn_shift,
    in_weight,
    in_bias,
    out_weight,
    out_bias,
    out_gain,
    out_shift,
    out_cotangent,
):
    F = lax.axis_size("fsdp")
    S = lax.axis_size("seq")
    width = layer_input.shape[-1]
    tokens = layer_input.reshape(-1, width)
    rows = tokens.shape[0]
    vec = query_bias.shape[0]
    vectors = (query_bias, value_bias, output_bias, attn_gain, attn_shift, out_bias, out_gain, out_shift)
    fan = in_bias.shape[0] // vec
    small = jnp.concatenate(
        [v.reshape(1, vec) for v in vectors]
        + [in_bias.reshape(fan, vec), jnp.zeros((16 - len(vectors) - fan, vec), bf16)]
    )
    (xfull, wqkv, smalls, q, k, v, qt, kt, ot, lse, mixed, wo, w1, w2) = forward(
        S, F, tokens, query_weight, key_weight, value_weight, small, output_weight, in_weight, out_weight
    )
    smalls = smalls.reshape(F, 16, vec).astype(f32)
    bias_output, gain_one, shift_one, bias_out, gain_two, shift_two = (
        smalls[:, i].reshape(width) for i in range(2, 8)
    )
    bias_in = smalls[:, 8 : 8 + fan].reshape(-1)
    tokens_single = tokens.astype(f32)
    attn_out = jnp.dot(mixed, wo, preferred_element_type=f32) + bias_output
    normed, pull_first = jax.vjp(layer_norm, tokens_single + attn_out, gain_one, shift_one)
    normed_low = normed.astype(bf16)
    hidden_pre = jnp.dot(normed_low, w1, preferred_element_type=f32) + bias_in
    hidden_single, pull_gelu = jax.vjp(gelu_exact, hidden_pre)
    hidden = hidden_single.astype(bf16)
    branch = jnp.dot(hidden, w2, preferred_element_type=f32) + bias_out
    layer_out, pull_second = jax.vjp(layer_norm, normed + branch, gain_two, shift_two)
    squares = jnp.stack(
        [jnp.sum(t * t) for t in (tokens_single, attn_out, normed, branch, layer_out)]
    )
    cotangent = out_cotangent.reshape(rows, width).astype(f32)
    grad_stream, grad_gain_two, grad_shift_two = pull_second(cotangent)
    grad_branch = grad_stream.astype(bf16)
    grad_bias_out = column_sums(grad_branch)
    grad_out = jnp.dot(hidden.T, grad_branch, preferred_element_type=f32)
    grad_hidden = jnp.dot(grad_branch, w2.T, preferred_element_type=f32)
    grad_pre = pull_gelu(grad_hidden)[0].astype(bf16)
    grad_bias_in = column_sums(grad_pre)
    grad_in = jnp.dot(normed_low.T, grad_pre, preferred_element_type=f32)
    grad_normed = grad_stream + jnp.dot(grad_pre, w1.T, preferred_element_type=f32)
    grad_h, grad_gain_one, grad_shift_one = pull_first(grad_normed)
    grad_attn = grad_h.astype(bf16)
    grad_bias_output = column_sums(grad_attn)
    grad_output = jnp.dot(mixed.T, grad_attn, preferred_element_type=f32)
    grad_mixed = jnp.dot(grad_attn, wo.T, preferred_element_type=f32).astype(bf16)
    f_y = 2 if F % 2 == 0 and F <= 8 else 4
    parts = [jnp.zeros((width,), f32)] * 2 + [
        grad_bias_output,
        grad_gain_one,
        grad_shift_one,
        grad_bias_out,
        grad_gain_two,
        grad_shift_two,
    ]
    table = jnp.stack(parts).reshape(8, F, vec).swapaxes(0, 1)
    extra = jnp.zeros((F, 16 - 8 - fan, vec), f32).at[:, 0, :5].set(squares)
    table = jnp.concatenate([table, grad_bias_in.reshape(F, fan, vec), extra], axis=1)
    by_rows = lambda t: t.astype(bf16).reshape(F // f_y, f_y, t.shape[0] // F, t.shape[1])
    input_grad, grad_qkv, grad_output, grad_in, grad_out, sums = backward(
        S,
        F,
        grad_mixed,
        q,
        k,
        v,
        qt,
        kt,
        ot,
        lse,
        xfull,
        wqkv,
        grad_h,
        table.reshape(F // f_y, f_y, 16, vec),
        by_rows(grad_output),
        by_rows(grad_in),
        by_rows(grad_out),
    )
    wide = q.shape[1]
    grad_query, grad_key, grad_value = (
        grad_qkv[:, :, i * wide : (i + 1) * wide].astype(f32).swapaxes(0, 1).reshape(-1, width) for i in range(3)
    )
    weights = [t.astype(f32) for t in (grad_output, grad_in, grad_out)]
    small_grads = sums
    grad_bias_in = sums[8 : 8 + fan].reshape(-1)
    rms = jnp.sqrt(sums[8 + fan, :5] / f32(rows * width * S * F))
    return (
        layer_out.astype(bf16).reshape(layer_input.shape),
        input_grad.reshape(layer_input.shape),
        grad_query,
        grad_key,
        grad_value,
        weights[0],
        small_grads[0],
        small_grads[1],
        small_grads[2],
        small_grads[3],
        small_grads[4],
        weights[1],
        grad_bias_in,
        weights[2],
        small_grads[5],
        small_grads[6],
        small_grads[7],
        rms,
    )


def solution(mesh):
    placed = (
        P("fsdp", "seq", None),
        P("fsdp", None),
        P("fsdp", None),
        P("fsdp", None),
        P("fsdp", None),
        P("fsdp"),
        P("fsdp"),
        P("fsdp"),
        P("fsdp"),
        P("fsdp"),
        P("fsdp", None),
        P("fsdp"),
        P("fsdp", None),
        P("fsdp"),
        P("fsdp"),
        P("fsdp"),
        P("fsdp", "seq", None),
    )
    return jax.shard_map(
        local,
        mesh=mesh,
        in_specs=placed,
        out_specs=(
            P("fsdp", "seq", None),
            P("fsdp", "seq", None),
            P("fsdp", None),
            P("fsdp", None),
            P("fsdp", None),
            P("fsdp", None),
            P("fsdp"),
            P("fsdp"),
            P("fsdp"),
            P("fsdp"),
            P("fsdp"),
            P("fsdp", None),
            P("fsdp"),
            P("fsdp", None),
            P("fsdp"),
            P("fsdp"),
            P("fsdp"),
            P(),
        ),
        check_vma=False,
    )
```

```python
import functools
import jax
import jax.numpy as jnp
from jax import lax
from jax.experimental import pallas as pl
from jax.experimental.pallas import tpu as pltpu
from jax.sharding import PartitionSpec as P

HD = 64
MESH = pl.DeviceIdType.MESH
bf16 = jnp.bfloat16
f32 = jnp.float32


def each(lo, hi, body):
    if hi - lo <= 8:
        for i in range(lo, hi):
            body(i)
    else:
        pl.loop(lo, hi)(body)


class Grid:
    def __init__(self, seq_count, fsdp_count):
        self.S, self.F = seq_count, fsdp_count
        self.H = seq_count // 2
        self.Y = 2 if fsdp_count % 2 == 0 and fsdp_count <= 8 else 4
        self.Z = fsdp_count // self.Y
        self.s = lax.axis_index("seq")
        self.f = lax.axis_index("fsdp")
        self.c = self.s % 2
        self.hi = self.s // 2
        self.z = self.f // self.Y
        self.y = self.f % self.Y

    def zp(self, k):
        return ((self.z + k) % self.Z) * self.Y + self.y

    def yp(self, j):
        return self.z * self.Y + (self.y + j) % self.Y

    def xp(self, m):
        return ((self.hi + m) % self.H) * 2 + self.c

    def sib(self):
        return self.hi * 2 + 1 - self.c

    def origin(self, r):
        j, k = r // self.Z, r % self.Z
        return ((self.z + self.Z - k) % self.Z) * self.Y + (self.y + self.Y - j) % self.Y

    def greet(self, barrier):
        count = 0
        for m in range(self.H):
            for flip in range(2):
                if m or flip:
                    to = ((self.hi + m) % self.H) * 2 + (self.c + flip) % 2
                    pl.semaphore_signal(barrier, inc=1, device_id=(to, self.f), device_id_type=MESH)
                    count += 1
        for k in range(1, self.Z):
            pl.semaphore_signal(barrier, inc=1, device_id=(self.s, self.zp(k)), device_id_type=MESH)
            count += 1
        for j in range(1, self.Y):
            pl.semaphore_signal(barrier, inc=1, device_id=(self.s, self.yp(j)), device_id_type=MESH)
            count += 1
        pl.semaphore_wait(barrier, count)


class Sems:
    def __init__(self):
        self.n = 0

    def take(self, n):
        at = self.n
        self.n += n
        return at


def rcopy(sems, src, dst, send, recv, to):
    return pltpu.make_async_remote_copy(
        src_ref=src,
        dst_ref=dst,
        send_sem=sems.at[send],
        recv_sem=sems.at[recv],
        device_id=to,
        device_id_type=MESH,
    )


class Gather:
    def __init__(self, alloc, S, F, Y, kind):
        self.kind = kind
        Z = F // Y
        self.zs = alloc.take(Z)
        self.ys = alloc.take(Y * Z)
        self.ir = alloc.take(F)
        if kind != "own":
            self.ss, self.sr = alloc.take(F), alloc.take(F)
        if kind == "quarter":
            H = S // 2
            self.xs, self.xr = alloc.take(H * F), alloc.take(H * F)
            self.ts, self.tr = alloc.take(H * F), alloc.take(H * F)

    def bind(self, g, sems, piece, place):
        self.g, self.sems, self.piece, self.place = g, sems, piece, place

    def part(self, hi=None, c=None):
        g = self.g
        c = g.c if c is None else c
        hi = g.hi if hi is None else hi
        return {"own": g.s, "half": c, "quarter": hi * 2 + c}[self.kind]

    def start_z(self):
        g, p = self.g, self.part()
        src, dst = self.piece(p), self.place(g.f, p)
        for k in range(1, g.Z):
            rcopy(self.sems, src, dst, self.zs + k, self.ir + k, (g.s, g.zp(k))).start()

    def start_y(self):
        g, p = self.g, self.part()
        src, dst = self.piece(p), self.place(g.f, p)
        for j in range(1, g.Y):
            rcopy(self.sems, src, dst, self.ys + j * g.Z, self.ir + j * g.Z, (g.s, g.yp(j))).start()

    def wait_in(self, r):
        ref = self.place(self.g.origin(r), self.part())
        rcopy(self.sems, ref, ref, self.ir + r, self.ir + r, (self.g.sib(), self.g.f)).wait_recv()

    def pass_on(self, r):
        g = self.g
        ref = self.place(g.origin(r), self.part())
        if self.kind == "quarter":
            for m in range(1, g.H):
                rcopy(self.sems, ref, ref, self.xs + m * g.F + r, self.xr + m * g.F + r, (g.xp(m), g.f)).start()
        if self.kind != "own":
            rcopy(self.sems, ref, ref, self.ss + r, self.sr + r, (g.sib(), g.f)).start()

    def on_z(self):
        g = self.g

        def body(k):
            self.wait_in(k)
            ref = self.place(g.origin(k), self.part())
            for j in range(1, g.Y):
                at = j * g.Z + k
                rcopy(self.sems, ref, ref, self.ys + at, self.ir + at, (g.s, g.yp(j))).start()
            self.pass_on(k)

        each(1, g.Z, body)

    def on_y(self):
        def body(r):
            self.wait_in(r)
            self.pass_on(r)

        each(self.g.Z, self.g.F, body)

    def on_x(self):
        if self.kind != "quarter":
            return
        g = self.g
        for m in range(1, g.H):
            part = self.part(hi=(g.hi + g.H - m) % g.H)

            def body(r):
                ref = self.place(g.origin(r), part)
                at = m * g.F + r
                rcopy(self.sems, ref, ref, self.xr + at, self.xr + at, (g.sib(), g.f)).wait_recv()
                rcopy(self.sems, ref, ref, self.ts + at, self.tr + at, (g.sib(), g.f)).start()

            each(1, g.F, body)

    def finish(self):
        g = self.g
        other = 1 - g.c

        def sent(ref, at):
            rcopy(self.sems, ref, ref, at, at, (g.sib(), g.f)).wait_send()

        def got(ref, at):
            rcopy(self.sems, ref, ref, at, at, (g.sib(), g.f)).wait_recv()

        if self.kind != "own":
            each(1, g.F, lambda r: got(self.place(g.origin(r), self.part(c=other)), self.sr + r))
        if self.kind == "quarter":
            for m in range(1, g.H):
                part = self.part(hi=(g.hi + g.H - m) % g.H, c=other)
                each(1, g.F, lambda r: got(self.place(g.origin(r), part), self.tr + m * g.F + r))
        mine = self.piece(self.part())
        for k in range(1, g.Z):
            sent(mine, self.zs + k)
        for j in range(1, g.Y):
            each(0, g.Z, lambda k: sent(mine, self.ys + j * g.Z + k))
        if self.kind != "own":
            each(1, g.F, lambda r: sent(mine, self.ss + r))
        if self.kind == "quarter":
            for m in range(1, g.H):
                each(1, g.F, lambda r: sent(mine, self.xs + m * g.F + r))
                each(1, g.F, lambda r: sent(mine, self.ts + m * g.F + r))


def forward_kernel(plan, x, wq, wk, wv, small, wo, w1, w2, *rest):
    (xfull, wqkv, smalls, q_o, k_o, v_o, qt_o, kt_o, ot_o, lse_o, mixed, wo_f, w1_f, w2_f) = rest[:14]
    (xs, ws, sm, qn, kn, vn, qt, kt, vt, ot, lse, oblk, onat, own_o, own_1, own_2, sems) = rest[14:]
    stage = (own_o, own_1, own_2)
    S, F, rows, length, heads, wide, vec = plan.S, plan.F, plan.rows, plan.length, plan.heads, plan.wide, plan.vec
    g = Grid(S, F)
    g.greet(pltpu.get_barrier_semaphore())
    part_rows = wq.shape[0]
    local = []

    def keep(src, dst, at):
        copy = pltpu.make_async_copy(src, dst, sems.at[at])
        copy.start()
        return copy

    mine = xs.at[pl.ds(g.s * rows, rows)]
    x_out = [rcopy(sems, x, mine, plan.x_s, plan.x_r, (g.sib(), g.f))]
    for m in range(1, g.H):
        x_out.append(rcopy(sems, x, mine, plan.x_s + m, plan.x_r + m, (g.xp(m), g.f)))
    for copy in x_out[::-1]:
        copy.start()
    for item, src, col in ((plan.gq, wq, 0), (plan.gk, wk, 1), (plan.gv, wv, 2)):
        item.bind(
            g,
            sems,
            lambda p, src=src: src.at[:, pl.ds(p * wide, wide)],
            lambda o, p, col=col: ws.at[pl.ds(o * part_rows, part_rows), pl.ds(col * wide, wide)],
        )
    plan.gs.bind(g, sems, lambda p: small, lambda o, p: sm.at[pl.ds(o * 16, 16)])
    first = (plan.gs, plan.gq, plan.gk, plan.gv)
    for item in first:
        item.start_z()
        item.start_y()
    local.append(keep(x, mine, plan.l))
    for col, src in enumerate((wq, wk, wv)):
        local.append(
            keep(
                src.at[:, pl.ds(g.s * wide, wide)],
                ws.at[pl.ds(g.f * part_rows, part_rows), pl.ds(col * wide, wide)],
                plan.l + 1 + col,
            )
        )
    local.append(keep(small, sm.at[pl.ds(g.f * 16, 16)], plan.l + 4))
    own = []
    for i, (src, dst) in enumerate(((wo, wo_f), (w1, w1_f), (w2, w2_f))):
        n = src.shape[0]
        own.append(keep(src, stage[i], plan.l + 5 + i))
    for src, dst, (item, lo, width) in [
        (src, dst, entry)
        for src, dst, entries in ((wo, wo_f, plan.go), (w1, w1_f, plan.g1), (w2, w2_f, plan.g2))
        for entry in entries
    ]:
        n = src.shape[0]
        item.bind(
            g,
            sems,
            lambda p, src=src, lo=lo, width=width: src.at[:, pl.ds(lo + p * width, width)],
            lambda o, p, dst=dst, n=n, lo=lo, width=width: dst.at[pl.ds(o * n, n), pl.ds(lo + p * width, width)],
        )
    big = [e[0] for e in plan.g1 + plan.g2[:1] + plan.go + plan.g2[1:]]
    for item in big:
        item.start_z()
    for item in first:
        item.on_z()
    x_pass = []
    for m in range(1, g.H):
        theirs = xs.at[pl.ds(((g.hi + g.H - m) % g.H * 2 + g.c) * rows, rows)]
        rcopy(sems, theirs, theirs, plan.x_s, plan.x_r + m, (g.sib(), g.f)).wait_recv()
        copy = rcopy(sems, theirs, theirs, plan.x_s + g.H + m, plan.x_r + g.H + m, (g.sib(), g.f))
        copy.start()
        x_pass.append(copy)
    for item in big:
        item.start_y()
    for item in first:
        item.on_y()
    rcopy(sems, mine, mine, plan.x_s, plan.x_r, (g.sib(), g.f)).wait_recv()
    for m in range(1, g.H):
        rcopy(sems, mine, mine, plan.x_s, plan.x_r + g.H + m, (g.sib(), g.f)).wait_recv()
    for copy in local:
        copy.wait()

    table = sm[...]
    lane = lax.broadcasted_iota(jnp.int32, (vec, wide), 1)
    spread = (lane % vec == lax.broadcasted_iota(jnp.int32, (vec, wide), 0)).astype(f32).astype(bf16)
    spread = jnp.dot(table, spread, preferred_element_type=f32)
    row = lax.broadcasted_iota(jnp.int32, spread.shape, 0)
    column = lax.broadcasted_iota(jnp.int32, spread.shape, 1)

    def vector(i):
        want = (g.s * (wide // vec) + column // vec) * 16 + i
        return jnp.sum(jnp.where(row == want, spread, 0.0), axis=0, keepdims=True)

    bias_q, bias_v = vector(0), vector(1)

    @pl.loop(0, S)
    def _(b):
        at = pl.multiple_of(b * rows, rows)
        prod = jnp.dot(xs[pl.ds(at, rows), :], ws[...], preferred_element_type=f32)
        q = (prod[:, :wide] + bias_q).astype(bf16).astype(f32) * 0.125
        k = prod[:, wide : 2 * wide]
        v = prod[:, 2 * wide :] + bias_v
        qn[pl.ds(at, rows), :] = q.astype(bf16)
        kn[pl.ds(at, rows), :] = k.astype(bf16)
        vn[pl.ds(at, rows), :] = v.astype(bf16)
        qt[:, pl.ds(at, rows)] = q.T.astype(bf16)
        kt[:, pl.ds(at, rows)] = k.T.astype(bf16)
        vt[:, pl.ds(at, rows)] = v.T.astype(bf16)

    for i, dst in enumerate((wo_f, w1_f, w2_f)):
        own[i].wait()
        n = stage[i].shape[0]
        own[i] = keep(stage[i], dst.at[pl.ds(g.f * n, n)], plan.l + 5 + i)
    stores = [
        keep(src, dst, plan.l + 8 + i)
        for i, (src, dst) in enumerate(
            ((xs, xfull), (ws, wqkv), (sm, smalls), (qn, q_o), (kn, k_o), (vn, v_o), (qt, qt_o), (kt, kt_o))
        )
    ]
    head_of = lax.broadcasted_iota(jnp.int32, (wide, rows), 0) // HD
    sent = []

    def attend(t):
        hi = (g.hi + 1 + t // 2) % g.H
        c = (g.c + t + t // (2 * (g.H - 1))) % 2
        to = hi * 2 + c
        at = pl.multiple_of(to * rows, rows)

        @pl.loop(0, heads)
        def _(h):
            q = jnp.where(head_of == h, qt[:, pl.ds(at, rows)], jnp.zeros((), bf16))
            s = jnp.dot(kn[...], q, preferred_element_type=f32)
            m = jnp.max(s, axis=0, keepdims=True)
            e = jnp.exp(s - m)
            l = jnp.sum(e, axis=0, keepdims=True)
            band = pl.ds(pl.multiple_of(h * HD, HD), HD)
            o = jnp.dot(vt[band, :], e.astype(bf16), preferred_element_type=f32) / l
            oblk[band, :] = o
            lse[pl.ds(h, 1), pl.ds(at, rows)] = m + jnp.log(l)

        ot[:, pl.ds(at, rows)] = oblk[...].astype(bf16)
        onat[t] = oblk[...].T.astype(bf16)
        dst = mixed.at[:, pl.ds(g.s * wide, wide)]
        if t < S - 1:
            copy = rcopy(sems, onat.at[t], dst, plan.o_s + t, plan.o_r + g.s, (to, g.f))
            copy.start()
            sent.append(copy)
        else:
            stores.append(keep(onat.at[t], dst, plan.o_s + t))

    turn = 0
    for op in plan.order:
        if op == "T":
            attend(turn)
            turn += 1
        else:
            item = big[int(op[1:])]
            {"z": item.on_z, "y": item.on_y, "x": item.on_x}[op[0]]()
    stores.append(keep(ot, ot_o, plan.l + 16))
    stores.append(keep(lse, lse_o, plan.l + 17))
    for item in (*first, *big):
        item.finish()
    for i in range(1, S):
        peer = (g.s + i) % S
        ref = mixed.at[:, pl.ds(peer * wide, wide)]
        rcopy(sems, ref, ref, plan.o_r + peer, plan.o_r + peer, (peer, g.f)).wait_recv()
    for copy in sent + x_out + x_pass:
        copy.wait_send()
    for copy in stores + own:
        copy.wait()


class Plan:
    pass


def forward_plan(S, F, rows, width, ff):
    plan = Plan()
    alloc = Sems()
    plan.S, plan.F, plan.rows, plan.length = S, F, rows, rows * S
    plan.wide = width // S
    plan.heads = plan.wide // HD
    plan.vec = width // F
    Y = 2 if F % 2 == 0 and F <= 8 else 4
    plan.x_s, plan.x_r = alloc.take(S), alloc.take(S)
    plan.gq, plan.gk, plan.gv, plan.gs = (Gather(alloc, S, F, Y, "own") for _ in range(4))
    half = width // 2
    plan.go = [(Gather(alloc, S, F, Y, "half"), 0, half)]
    eighth = ff // 2 // S
    plan.g1 = [(Gather(alloc, S, F, Y, "quarter"), i * S * eighth, eighth) for i in range(2)]
    plan.g2 = [(Gather(alloc, S, F, Y, "quarter"), 0, half // S)]
    plan.g2 += [(Gather(alloc, S, F, Y, "half"), half + i * half // 2, half // 4) for i in range(2)]
    plan.order = (
        "z0", "T", "y0", "T", "z1", "T", "y1", "T", "z2", "y2", "x0", "z3", "y3", "x1", "z4", "y4",
        "z5", "y5", "x2",
    )
    plan.o_s, plan.o_r = alloc.take(S), alloc.take(S)
    plan.l = alloc.take(20)
    plan.sems = alloc.n
    return plan


def forward(S, F, x, wq, wk, wv, small, wo, w1, w2):
    rows, width = x.shape
    ff = w1.shape[1]
    plan = forward_plan(S, F, rows, width, ff)
    length, wide, heads = plan.length, plan.wide, plan.heads
    sds = jax.ShapeDtypeStruct
    any_ = pl.BlockSpec(memory_space=pl.ANY)
    return pl.pallas_call(
        functools.partial(forward_kernel, plan),
        out_shape=(
            sds((length, width), bf16),
            sds((width, 3 * wide), bf16),
            sds((F * 16, plan.vec), bf16),
            sds((length, wide), bf16),
            sds((length, wide), bf16),
            sds((length, wide), bf16),
            sds((wide, length), bf16),
            sds((wide, length), bf16),
            sds((wide, length), bf16),
            sds((8, length), f32),
            sds((rows, width), bf16),
            sds((width, width), bf16),
            sds((width, ff), bf16),
            sds((ff, width), bf16),
        ),
        in_specs=[any_] * 8,
        out_specs=(any_,) * 14,
        scratch_shapes=[
            pltpu.VMEM((length, width), bf16),
            pltpu.VMEM((width, 3 * wide), bf16),
            pltpu.VMEM((F * 16, plan.vec), bf16),
            pltpu.VMEM((length, wide), bf16),
            pltpu.VMEM((length, wide), bf16),
            pltpu.VMEM((length, wide), bf16),
            pltpu.VMEM((wide, length), bf16),
            pltpu.VMEM((wide, length), bf16),
            pltpu.VMEM((wide, length), bf16),
            pltpu.VMEM((wide, length), bf16),
            pltpu.VMEM((8, length), f32),
            pltpu.VMEM((wide, rows), f32),
            pltpu.VMEM((S, rows, wide), bf16),
            pltpu.VMEM(wo.shape, bf16),
            pltpu.VMEM(w1.shape, bf16),
            pltpu.VMEM(w2.shape, bf16),
            pltpu.SemaphoreType.DMA((plan.sems,)),
        ],
        compiler_params=pltpu.CompilerParams(collective_id=0, has_side_effects=True, vmem_limit_bytes=48 << 20),
        name="attention_forward_and_weight_gather",
    )(x, wq, wk, wv, small, wo, w1, w2)


class Reduce:
    def __init__(self, alloc, S, F, Y, R, C, kind):
        self.kind, self.R, self.C = kind, R, C
        self.S, self.F, self.Y, self.Z, self.H = S, F, Y, F // Y, S // 2
        Z, H = self.Z, self.H
        self.w = {"half": C // 2, "quarter": C // S, "own": C}[kind]
        w = self.w
        self.n = H if kind == "quarter" else 1
        self.shapes = [(self.n, Z, Y, R, w), (Y - 1, Z, R, w), (Z, R, w)]
        if kind == "own":
            self.shapes += [(S, R, w)]
        else:
            self.shapes += [(self.n, Z, Y, R, w), (R, C)]
            self.shapes += [(H - 1, Z, Y, R, w) if kind == "quarter" else (H - 1, R, w)]
        self.shapes = [pltpu.VMEM(s, bf16) for s in self.shapes]
        self.load = alloc.take(H)
        self.ds, self.dr = alloc.take(H), alloc.take(H)
        self.xs, self.xr = alloc.take(H), alloc.take(H)
        self.ys, self.yr = alloc.take(Y), alloc.take(Y)
        self.zs, self.zr = alloc.take(Z), alloc.take(Z)
        self.fs, self.fr = alloc.take(2 * H), alloc.take(2 * H)
        self.out = alloc.take(1)

    def bind(self, g, sems, refs, source, dest):
        self.g, self.sems, self.source, self.dest = g, sems, source, dest
        if self.kind == "own":
            self.own, self.ry, self.rz, self.fin = refs
        else:
            self.own, self.ry, self.rz, self.rd, self.fin, self.rx = refs
        self.sends = []

    def send(self, src, dst, s, r, to):
        copy = rcopy(self.sems, src, dst, s, r, to)
        copy.start()
        self.sends.append(copy)

    def recv(self, ref, r):
        rcopy(self.sems, ref, ref, r, r, (self.g.sib(), self.g.f)).wait_recv()

    def column(self, hi, c):
        return (hi * 2 + c) * self.w if self.kind == "quarter" else c * self.w

    def start(self):
        g = self.g
        self.loads = []
        for m in range(self.n):
            hi = (g.hi + m) % g.H
            self.send(
                self.source(self.column(hi, 1 - g.c), self.w),
                self.rd.at[m],
                self.ds + m,
                self.dr + m,
                (g.sib(), g.f),
            )
            copy = pltpu.make_async_copy(
                self.source(self.column(hi, g.c), self.w), self.own.at[m], self.sems.at[self.load + m]
            )
            copy.start()
            self.loads.append(copy)

    def add_all(self, m, other):
        @pl.loop(0, self.Z * self.Y)
        def _(i):
            a, b = i // self.Y, i % self.Y
            self.own[m, a, b] = (self.own[m, a, b].astype(f32) + other(a, b).astype(f32)).astype(bf16)

    def over_cores(self):
        for m in list(range(1, self.n)) + [0]:
            self.loads[m].wait()
            self.recv(self.rd.at[m], self.dr + m)
            self.add_all(m, lambda a, b: self.rd[m, a, b])
            if m:
                self.send(self.own.at[m], self.rx.at[m - 1], self.xs + m, self.xr + m, (self.g.xp(m), self.g.f))
        if self.kind == "half":
            self.send_y()

    def over_x_first(self):
        for m in range(1, self.H):
            self.recv(self.rx.at[m - 1], self.xr + m)
            self.add_all(0, lambda a, b: self.rx[m - 1, a, b])
        self.send_y()

    def send_y(self):
        g = self.g
        for j in range(1, g.Y):
            y = (g.y + j) % g.Y
            self.send(self.own.at[0, :, y], self.ry.at[j - 1], self.ys + j, self.yr + j, (g.s, g.yp(j)))

    def over_y(self):
        g = self.g
        for j in range(1, g.Y):
            self.recv(self.ry.at[j - 1], self.yr + j)

        @pl.loop(0, self.Z)
        def _(a):
            total = self.own[0, a, g.y].astype(f32)
            for j in range(1, g.Y):
                total += self.ry[j - 1, a].astype(f32)
            self.own[0, a, g.y] = total.astype(bf16)

        for k in range(1, g.Z):
            z = (g.z + k) % g.Z
            self.send(self.own.at[0, z, g.y], self.rz.at[k], self.zs + k, self.zr + k, (g.s, g.zp(k)))

    def over_z(self):
        g = self.g
        total = self.own[0, g.z, g.y].astype(f32)
        for k in range(1, g.Z):
            self.recv(self.rz.at[k], self.zr + k)
            total += self.rz[k].astype(f32)
        total = total.astype(bf16)
        if self.kind == "half":
            self.rz[0] = total
            for m in range(1, g.H):
                self.send(self.rz.at[0], self.rx.at[m - 1], self.xs + m, self.xr + m, (g.xp(m), g.f))
            return
        if self.kind == "own":
            self.fin[g.s] = total
            ref = self.fin.at[g.s]
        else:
            at = pl.multiple_of(self.column(g.hi, g.c), self.w)
            self.fin[:, pl.ds(at, self.w)] = total
            ref = self.fin.at[:, pl.ds(at, self.w)]
        for m in range(1, g.H):
            self.send(ref, ref, self.fs + m, self.fr + m, (g.xp(m), g.f))
        self.send(ref, ref, self.fs, self.fr, (g.sib(), g.f))

    def over_x_last(self):
        g = self.g
        if self.kind == "half":
            total = self.rz[0].astype(f32)
            for m in range(1, g.H):
                self.recv(self.rx.at[m - 1], self.xr + m)
                total += self.rx[m - 1].astype(f32)
            at = pl.multiple_of(g.c * self.w, self.w)
            self.fin[:, pl.ds(at, self.w)] = total.astype(bf16)
            ref = self.fin.at[:, pl.ds(at, self.w)]
            self.send(ref, ref, self.fs, self.fr, (g.sib(), g.f))
            return
        for m in range(1, g.H):
            hi = (g.hi + g.H - m) % g.H
            if self.kind == "own":
                ref = self.fin.at[hi * 2 + g.c]
            else:
                ref = self.fin.at[:, pl.ds(self.column(hi, g.c), self.w)]
            self.recv(ref, self.fr + m)
            self.send(ref, ref, self.fs + g.H + m, self.fr + g.H + m, (g.sib(), g.f))

    def finish(self):
        g = self.g
        for m in range(g.H if self.kind != "half" else 1):
            hi = (g.hi + g.H - m) % g.H
            if self.kind == "own":
                ref = self.fin.at[hi * 2 + 1 - g.c]
            else:
                ref = self.fin.at[:, pl.ds(self.column(hi, 1 - g.c), self.w)]
            self.recv(ref, self.fr + (g.H + m if m else 0))
        self.copy_out = pltpu.make_async_copy(self.fin, self.dest, self.sems.at[self.out])
        self.copy_out.start()

    def done(self):
        for copy in self.sends:
            copy.wait_send()
        self.copy_out.wait()

    def step(self, name):
        {
            "D": self.over_cores,
            "X": self.over_x_first if self.kind == "quarter" else self.over_x_last,
            "Y": self.over_y,
            "Z": self.over_z,
            "L": self.over_x_last,
            "F": self.finish,
        }[name]()


def backward_kernel(plan, g_o, q_i, k_i, v_i, qt_i, kt_i, ot_i, lse_i, x_i, w_i, gh, table_i, dwo, dw1, dw2, *rest):
    dx_o, dqkv_o, dwo_o, dw1_o, dw2_o, table_o = rest[:6]
    (go, qn, kn, vn, qt, kt, ot, lse, xs, ws, dk, dv, dqt, dt, delta, grads) = rest[6:22]
    (dx, dx_send, dx_core, dx_out, dx_x, tab, tab_core, tab_x, tab_y, tab_s, tab_z, sems) = rest[22:34]
    pools = rest[34:]
    S, F, rows, heads, wide, vec = plan.S, plan.F, plan.rows, plan.heads, plan.wide, plan.vec
    g = Grid(S, F)
    g.greet(pltpu.get_barrier_semaphore())

    def keep(src, dst, at):
        copy = pltpu.make_async_copy(src, dst, sems.at[at])
        copy.start()
        return copy

    sent = []

    def send(src, dst, s, r, to):
        copy = rcopy(sems, src, dst, s, r, to)
        copy.start()
        sent.append(copy)

    def recv(ref, r):
        rcopy(sems, ref, ref, r, r, (g.sib(), g.f)).wait_recv()

    for m in [*range(1, g.H), 0]:
        for flip in range(2):
            if m or flip:
                to = ((g.hi + m) % g.H) * 2 + (g.c + flip) % 2
                send(
                    g_o.at[:, pl.ds(to * wide, wide)],
                    go.at[g.s],
                    plan.o_s + m * 2 + flip,
                    plan.o_r + g.s,
                    (to, g.f),
                )
    used = 0
    for item, which, col, row in plan.items:
        n = len(item.shapes)
        src, dst = {"o": (dwo, dwo_o), "1": (dw1, dw1_o), "2": (dw2, dw2_o)}[which]
        item.bind(
            g,
            sems,
            pools[used : used + n],
            lambda lo, width, src=src, item=item, col=col, row=row: src.at[
                :, :, pl.ds(row, item.R), pl.ds(col + lo, width)
            ],
            dst.at[pl.ds(row, item.R), pl.ds(col, item.C)],
        )
        used += n
        item.start()
    for i, item in enumerate(plan.qkv):
        item.bind(g, sems, pools[used : used + 4], None, dqkv_o.at[i])
        used += 4
    loads = [
        keep(src, dst, plan.l + i)
        for i, (src, dst) in enumerate(
            (
                (g_o.at[:, pl.ds(g.s * wide, wide)], go.at[g.s]),
                (q_i, qn),
                (k_i, kn),
                (v_i, vn),
                (qt_i, qt),
                (kt_i, kt),
                (ot_i, ot),
                (lse_i, lse),
                (x_i, xs),
                (w_i, ws),
                (gh, dx),
                (table_i, tab),
            )
        )
    ]
    items = [entry[0] for entry in plan.items]
    dk[...] = jnp.zeros_like(dk)
    dv[...] = jnp.zeros_like(dv)
    for copy in loads:
        copy.wait()
    head_of = lax.broadcasted_iota(jnp.int32, (wide, rows), 0) // HD
    head_at = lax.broadcasted_iota(jnp.int32, (rows, wide), 1) // HD
    none = jnp.zeros((), bf16)

    def attend(t):
        if t == 0:
            for i in range(1, S):
                peer = (g.s + i) % S
                recv(go.at[peer], plan.o_r + peer)
        span = pl.ds(t * rows, rows)
        turned = go[t].astype(f32).T
        dt[...] = turned.astype(bf16)
        weighed = turned * ot[:, span].astype(f32)
        for h in range(heads):
            delta[pl.ds(h, 1), :] = jnp.sum(weighed[h * HD : (h + 1) * HD], axis=0, keepdims=True)

        @pl.loop(0, heads)
        def _(h):
            band = pl.ds(pl.multiple_of(h * HD, HD), HD)
            s = jnp.dot(kn[...], jnp.where(head_of == h, qt[:, span], none), preferred_element_type=f32)
            p = jnp.exp(s - lse[pl.ds(h, 1), span])
            dp = jnp.dot(vn[...], jnp.where(head_of == h, dt[...], none), preferred_element_type=f32)
            ds = (p * (dp - delta[pl.ds(h, 1), :])).astype(bf16)
            dv[...] += jnp.dot(p.astype(bf16), jnp.where(head_at == h, go[t], none), preferred_element_type=f32)
            dk[...] += jnp.dot(ds, jnp.where(head_at == h, qn[span, :], none), preferred_element_type=f32)
            dqt[band, span] = jnp.dot(kt[band, :], ds, preferred_element_type=f32) * 0.125

    totals = []

    def projections(i):
        if i == 0:
            sum_q = jnp.zeros((1, wide), f32)
            sum_v = jnp.zeros((1, wide), f32)
            for t in range(S):
                span = pl.ds(t * rows, rows)
                q = dqt[:, span].T.astype(bf16)
                v = dv[span, :].astype(bf16)
                grads[span, pl.ds(0, wide)] = q
                grads[span, pl.ds(wide, wide)] = dk[span, :].astype(bf16)
                grads[span, pl.ds(2 * wide, wide)] = v
                sum_q += jnp.sum(q.astype(f32), axis=0, keepdims=True)
                sum_v += jnp.sum(v.astype(f32), axis=0, keepdims=True)
            totals.extend((sum_q, sum_v))
        item = plan.qkv[i]
        part_rows, width = item.R, xs.shape[1]
        step = max(part_rows, 256)
        for lo in range(0, width, step):
            prod = lax.dot_general(
                xs[:, pl.ds(lo, step)],
                grads[:, pl.ds(i * wide, wide)],
                (((0,), (0,)), ((), ())),
                preferred_element_type=f32,
            ).astype(bf16)
            for j in range(step // part_rows):
                to = lo // part_rows + j
                item.own[0, to // g.Y, to % g.Y] = prod[j * part_rows : (j + 1) * part_rows]
        item.send_y()

    def part(to):
        return lax.dot_general(
            grads[pl.ds(pl.multiple_of(to * rows, rows), rows), :],
            ws[...],
            (((1,), (1,)), ((), ())),
            preferred_element_type=f32,
        )

    def input_parts():
        for m in [*range(1, g.H), 0]:
            hi = (g.hi + m) % g.H
            dx_send[m] = part(hi * 2 + 1 - g.c).astype(bf16)
            send(dx_send.at[m], dx_core.at[m], plan.dx + m, plan.dx + g.H + m, (g.sib(), g.f))
        for m in [*range(1, g.H), 0]:
            hi = (g.hi + m) % g.H
            value = part(hi * 2 + g.c)
            recv(dx_core.at[m], plan.dx + g.H + m)
            value += dx_core[m].astype(f32)
            if m:
                dx_out[m - 1] = value.astype(bf16)
                send(dx_out.at[m - 1], dx_x.at[m - 1], plan.dx + 2 * g.H + m, plan.dx + 3 * g.H + m, (g.xp(m), g.f))
            else:
                dx[...] += value

    out = []

    def input_done():
        for m in range(1, g.H):
            recv(dx_x.at[m - 1], plan.dx + 3 * g.H + m)
            dx[...] += dx_x[m - 1].astype(f32)
        out.append(keep(dx, dx_o, plan.l + 13))

    def vectors(stage):
        Y = g.Y
        if stage == 0:
            base = g.s * (wide // vec)
            for i in range(wide // vec):
                to = base + i
                for row, value in enumerate(totals):
                    tab[to // Y, to % Y, pl.ds(row, 1), :] = value[:, i * vec : (i + 1) * vec]
            send(tab, tab_core, plan.t, plan.t + 1, (g.sib(), g.f))
        if stage == 1:
            recv(tab_core, plan.t + 1)
            tab_x[g.hi] = tab[...] + tab_core[...]
            for m in range(1, g.H):
                send(tab_x.at[g.hi], tab_x.at[g.hi], plan.tx + m, plan.tx + g.H + g.hi, (g.xp(m), g.f))
        if stage == 2:
            for m in range(1, g.H):
                hi = (g.hi + m) % g.H
                recv(tab_x.at[hi], plan.tx + g.H + hi)
            total = tab_x[0]
            for m in range(1, g.H):
                total += tab_x[m]
            tab_core[...] = total
            tab_y[g.y] = tab_core[:, g.y]
            for j in range(1, Y):
                y = (g.y + j) % Y
                send(tab_core.at[:, y], tab_y.at[g.y], plan.ty + j, plan.ty + Y + g.y, (g.s, g.yp(j)))
        if stage == 3:
            for j in range(1, Y):
                y = (g.y + j) % Y
                recv(tab_y.at[y], plan.ty + Y + y)
            total = tab_y[0]
            for j in range(1, Y):
                total += tab_y[j]
            tab_s[...] = total
            tab_z[g.z] = tab_s[g.z]
            for k in range(1, g.Z):
                z = (g.z + k) % g.Z
                send(tab_s.at[z], tab_z.at[g.z], plan.tz + k, plan.tz + g.Z + g.z, (g.s, g.zp(k)))
        if stage == 4:
            for k in range(1, g.Z):
                z = (g.z + k) % g.Z
                recv(tab_z.at[z], plan.tz + g.Z + z)
            total = tab_z[0]
            for k in range(1, g.Z):
                total += tab_z[k]
            tab_y[0, 0] = total
            out.append(keep(tab_y.at[0, 0], table_o, plan.l + 12))

    named = {chr(ord("a") + i): item for i, item in enumerate(items)}
    named.update({"q%d" % i: item for i, item in enumerate(plan.qkv)})
    for op in plan.order:
        what, on = op[0], op[1:]
        if what == "T":
            attend(int(on))
        elif what == "G":
            projections(int(on))
        elif what == "I":
            input_parts()
        elif what == "J":
            input_done()
        elif what == "V":
            vectors(int(on))
        else:
            named[on].step(what)
    for item in (*items, *plan.qkv):
        item.done()
    for copy in sent:
        copy.wait_send()
    for copy in out:
        copy.wait()


def backward_plan(S, F, rows, width, ff):
    plan = Plan()
    alloc = Sems()
    plan.S, plan.F, plan.rows = S, F, rows
    plan.wide = width // S
    plan.heads = plan.wide // HD
    plan.vec = width // F
    Y = 2 if F % 2 == 0 and F <= 8 else 4
    R, R2 = width // F, ff // F
    ones = [(Reduce(alloc, S, F, Y, R, width, "quarter"), "1", i * width, 0) for i in range(ff // width)]
    twos = [(Reduce(alloc, S, F, Y, R2 // 4, width, "half"), "2", 0, i * (R2 // 4)) for i in range(4)]
    plan.items = [e for pair in zip(ones, twos) for e in pair]
    plan.items.append((Reduce(alloc, S, F, Y, R, width, "half"), "o", 0, 0))
    plan.qkv = [Reduce(alloc, S, F, Y, R, plan.wide, "own") for _ in range(3)]
    plan.o_s, plan.o_r = alloc.take(S), alloc.take(S)
    plan.dx = alloc.take(4 * S)
    plan.t, plan.tx, plan.ty, plan.tz = alloc.take(2), alloc.take(S), alloc.take(2 * Y), alloc.take(2 * F // Y)
    plan.l = alloc.take(14)
    plan.order = (
        "Da", "Db", "Dc", "Dd", "T0", "Df", "De", "Yb", "T1", "Xa", "T2", "Dg", "Yd", "Dh", "Zb", "Xc",
        "T3", "Yf", "G0", "Xe", "Ya", "Zd", "G1", "G2", "I", "Xg", "V0", "Yh", "Xb", "Zf", "V1", "Fb",
        "Xd", "Fd", "Yc", "Za", "Yq0", "Ye", "Di", "Zh", "J", "Yq1", "Xf", "Zc", "V2", "Ff", "La", "Fa",
        "Yq2", "Xh", "Zq0", "Lc", "Fh", "Fc", "Lq0", "Yg", "Fq0", "Ze", "Le", "Fe", "Zq1", "Lq1", "Yi", "Fq1",
        "V3", "Zq2", "Lq2", "Fq2", "Zg", "Lg", "Fg", "Zi", "V4", "Xi", "Fi",
    )
    plan.sems = alloc.n
    return plan


def backward(S, F, g_o, q, k, v, qt, kt, ot, lse, x, w, gh, table, dwo, dw1, dw2):
    rows, width = g_o.shape
    ff = dw1.shape[-1]
    plan = backward_plan(S, F, rows, width, ff)
    wide, vec = plan.wide, plan.vec
    length = rows * S
    Z, Y = table.shape[:2]
    H = S // 2
    R, R2 = width // F, ff // F
    sds = jax.ShapeDtypeStruct
    any_ = pl.BlockSpec(memory_space=pl.ANY)
    pools = [s for e in plan.items for s in e[0].shapes] + [s for i in plan.qkv for s in i.shapes]
    return pl.pallas_call(
        functools.partial(backward_kernel, plan),
        out_shape=(
            sds((rows, width), f32),
            sds((3, S, R, wide), bf16),
            sds((R, width), bf16),
            sds((R, ff), bf16),
            sds((R2, width), bf16),
            sds((16, vec), f32),
        ),
        in_specs=[any_] * 15,
        out_specs=(any_,) * 6,
        scratch_shapes=[
            pltpu.VMEM((S, rows, wide), bf16),
            pltpu.VMEM((length, wide), bf16),
            pltpu.VMEM((length, wide), bf16),
            pltpu.VMEM((length, wide), bf16),
            pltpu.VMEM((wide, length), bf16),
            pltpu.VMEM((wide, length), bf16),
            pltpu.VMEM((wide, length), bf16),
            pltpu.VMEM((8, length), f32),
            pltpu.VMEM((length, width), bf16),
            pltpu.VMEM((width, 3 * wide), bf16),
            pltpu.VMEM((length, wide), f32),
            pltpu.VMEM((length, wide), f32),
            pltpu.VMEM((wide, length), f32),
            pltpu.VMEM((wide, rows), bf16),
            pltpu.VMEM((8, rows), f32),
            pltpu.VMEM((length, 3 * wide), bf16),
            pltpu.VMEM((rows, width), f32),
            pltpu.VMEM((H, rows, width), bf16),
            pltpu.VMEM((H, rows, width), bf16),
            pltpu.VMEM((H - 1, rows, width), bf16),
            pltpu.VMEM((H - 1, rows, width), bf16),
            pltpu.VMEM((Z, Y, 16, vec), f32),
            pltpu.VMEM((Z, Y, 16, vec), f32),
            pltpu.VMEM((H, Z, Y, 16, vec), f32),
            pltpu.VMEM((Y, Z, 16, vec), f32),
            pltpu.VMEM((Z, 16, vec), f32),
            pltpu.VMEM((Z, 16, vec), f32),
            pltpu.SemaphoreType.DMA((plan.sems,)),
            *pools,
        ],
        compiler_params=pltpu.CompilerParams(collective_id=1, has_side_effects=True, vmem_limit_bytes=63 << 20),
        name="attention_backward_and_gradient_sums",
    )(g_o, q, k, v, qt, kt, ot, lse, x, w, gh, table, dwo, dw1, dw2)


def layer_norm(stream, gain, shift):
    centre = stream - jnp.mean(stream, axis=-1, keepdims=True)
    variance = jnp.mean(centre * centre, axis=-1, keepdims=True)
    return centre * lax.rsqrt(variance + 1e-05) * gain + shift


def gelu_exact(inputs):
    return jax.nn.gelu(inputs, approximate=False)


def column_sums(matrix):
    return jnp.sum(matrix.astype(f32), axis=0)


def local(
    layer_input,
    query_weight,
    key_weight,
    value_weight,
    output_weight,
    query_bias,
    value_bias,
    output_bias,
    attn_gain,
    attn_shift,
    in_weight,
    in_bias,
    out_weight,
    out_bias,
    out_gain,
    out_shift,
    out_cotangent,
):
    F = lax.axis_size("fsdp")
    S = lax.axis_size("seq")
    width = layer_input.shape[-1]
    tokens = layer_input.reshape(-1, width)
    rows = tokens.shape[0]
    vec = query_bias.shape[0]
    vectors = (query_bias, value_bias, output_bias, attn_gain, attn_shift, out_bias, out_gain, out_shift)
    fan = in_bias.shape[0] // vec
    small = jnp.concatenate(
        [v.reshape(1, vec) for v in vectors]
        + [in_bias.reshape(fan, vec), jnp.zeros((16 - len(vectors) - fan, vec), bf16)]
    )
    (xfull, wqkv, smalls, q, k, v, qt, kt, ot, lse, mixed, wo, w1, w2) = forward(
        S, F, tokens, query_weight, key_weight, value_weight, small, output_weight, in_weight, out_weight
    )
    smalls = smalls.reshape(F, 16, vec).astype(f32)
    bias_output, gain_one, shift_one, bias_out, gain_two, shift_two = (
        smalls[:, i].reshape(width) for i in range(2, 8)
    )
    bias_in = smalls[:, 8 : 8 + fan].reshape(-1)
    tokens_single = tokens.astype(f32)
    attn_out = jnp.dot(mixed, wo, preferred_element_type=f32) + bias_output
    normed, pull_first = jax.vjp(layer_norm, tokens_single + attn_out, gain_one, shift_one)
    normed_low = normed.astype(bf16)
    hidden_pre = jnp.dot(normed_low, w1, preferred_element_type=f32) + bias_in
    hidden_single, pull_gelu = jax.vjp(gelu_exact, hidden_pre)
    hidden = hidden_single.astype(bf16)
    branch = jnp.dot(hidden, w2, preferred_element_type=f32) + bias_out
    layer_out, pull_second = jax.vjp(layer_norm, normed + branch, gain_two, shift_two)
    squares = jnp.stack(
        [jnp.sum(t * t) for t in (tokens_single, attn_out, normed, branch, layer_out)]
    )
    cotangent = out_cotangent.reshape(rows, width).astype(f32)
    grad_stream, grad_gain_two, grad_shift_two = pull_second(cotangent)
    grad_branch = grad_stream.astype(bf16)
    grad_bias_out = column_sums(grad_branch)
    grad_out = jnp.dot(hidden.T, grad_branch, preferred_element_type=f32)
    grad_hidden = jnp.dot(grad_branch, w2.T, preferred_element_type=f32)
    grad_pre = pull_gelu(grad_hidden)[0].astype(bf16)
    grad_bias_in = column_sums(grad_pre)
    grad_in = jnp.dot(normed_low.T, grad_pre, preferred_element_type=f32)
    grad_normed = grad_stream + jnp.dot(grad_pre, w1.T, preferred_element_type=f32)
    grad_h, grad_gain_one, grad_shift_one = pull_first(grad_normed)
    grad_attn = grad_h.astype(bf16)
    grad_bias_output = column_sums(grad_attn)
    grad_output = jnp.dot(mixed.T, grad_attn, preferred_element_type=f32)
    grad_mixed = jnp.dot(grad_attn, wo.T, preferred_element_type=f32).astype(bf16)
    f_y = 2 if F % 2 == 0 and F <= 8 else 4
    parts = [jnp.zeros((width,), f32)] * 2 + [
        grad_bias_output,
        grad_gain_one,
        grad_shift_one,
        grad_bias_out,
        grad_gain_two,
        grad_shift_two,
    ]
    table = jnp.stack(parts).reshape(8, F, vec).swapaxes(0, 1)
    extra = jnp.zeros((F, 16 - 8 - fan, vec), f32).at[:, 0, :5].set(squares)
    table = jnp.concatenate([table, grad_bias_in.reshape(F, fan, vec), extra], axis=1)
    by_rows = lambda t: t.astype(bf16).reshape(F // f_y, f_y, t.shape[0] // F, t.shape[1])
    input_grad, grad_qkv, grad_output, grad_in, grad_out, sums = backward(
        S,
        F,
        grad_mixed,
        q,
        k,
        v,
        qt,
        kt,
        ot,
        lse,
        xfull,
        wqkv,
        grad_h,
        table.reshape(F // f_y, f_y, 16, vec),
        by_rows(grad_output),
        by_rows(grad_in),
        by_rows(grad_out),
    )
    wide = q.shape[1]
    grad_query, grad_key, grad_value = (
        t.astype(f32).swapaxes(0, 1).reshape(-1, width) for t in grad_qkv
    )
    weights = [t.astype(f32) for t in (grad_output, grad_in, grad_out)]
    small_grads = sums
    grad_bias_in = sums[8 : 8 + fan].reshape(-1)
    rms = jnp.sqrt(sums[8 + fan, :5] / f32(rows * width * S * F))
    return (
        layer_out.astype(bf16).reshape(layer_input.shape),
        input_grad.reshape(layer_input.shape),
        grad_query,
        grad_key,
        grad_value,
        weights[0],
        small_grads[0],
        small_grads[1],
        small_grads[2],
        small_grads[3],
        small_grads[4],
        weights[1],
        grad_bias_in,
        weights[2],
        small_grads[5],
        small_grads[6],
        small_grads[7],
        rms,
    )


def solution(mesh):
    placed = (
        P("fsdp", "seq", None),
        P("fsdp", None),
        P("fsdp", None),
        P("fsdp", None),
        P("fsdp", None),
        P("fsdp"),
        P("fsdp"),
        P("fsdp"),
        P("fsdp"),
        P("fsdp"),
        P("fsdp", None),
        P("fsdp"),
        P("fsdp", None),
        P("fsdp"),
        P("fsdp"),
        P("fsdp"),
        P("fsdp", "seq", None),
    )
    return jax.shard_map(
        local,
        mesh=mesh,
        in_specs=placed,
        out_specs=(
            P("fsdp", "seq", None),
            P("fsdp", "seq", None),
            P("fsdp", None),
            P("fsdp", None),
            P("fsdp", None),
            P("fsdp", None),
            P("fsdp"),
            P("fsdp"),
            P("fsdp"),
            P("fsdp"),
            P("fsdp"),
            P("fsdp", None),
            P("fsdp"),
            P("fsdp", None),
            P("fsdp"),
            P("fsdp"),
            P("fsdp"),
            P(),
        ),
        check_vma=False,
    )
```

```python
import functools
import jax
import jax.numpy as jnp
from jax import lax
from jax.experimental import pallas as pl
from jax.experimental.pallas import tpu as pltpu
from jax.sharding import PartitionSpec as P

HD = 64
MESH = pl.DeviceIdType.MESH
bf16 = jnp.bfloat16
f32 = jnp.float32


def each(lo, hi, body):
    if hi - lo <= 8:
        for i in range(lo, hi):
            body(i)
    else:
        pl.loop(lo, hi)(body)


class Grid:
    def __init__(self, seq_count, fsdp_count):
        self.S, self.F = seq_count, fsdp_count
        self.H = seq_count // 2
        self.Y = 2 if fsdp_count % 2 == 0 and fsdp_count <= 8 else 4
        self.Z = fsdp_count // self.Y
        self.s = lax.axis_index("seq")
        self.f = lax.axis_index("fsdp")
        self.c = self.s % 2
        self.hi = self.s // 2
        self.z = self.f // self.Y
        self.y = self.f % self.Y

    def zp(self, k):
        return ((self.z + k) % self.Z) * self.Y + self.y

    def yp(self, j):
        return self.z * self.Y + (self.y + j) % self.Y

    def xp(self, m):
        return ((self.hi + m) % self.H) * 2 + self.c

    def sib(self):
        return self.hi * 2 + 1 - self.c

    def origin(self, r):
        j, k = r // self.Z, r % self.Z
        return ((self.z + self.Z - k) % self.Z) * self.Y + (self.y + self.Y - j) % self.Y

    def greet(self, barrier):
        count = 0
        for m in range(self.H):
            for flip in range(2):
                if m or flip:
                    to = ((self.hi + m) % self.H) * 2 + (self.c + flip) % 2
                    pl.semaphore_signal(barrier, inc=1, device_id=(to, self.f), device_id_type=MESH)
                    count += 1
        for k in range(1, self.Z):
            pl.semaphore_signal(barrier, inc=1, device_id=(self.s, self.zp(k)), device_id_type=MESH)
            count += 1
        for j in range(1, self.Y):
            pl.semaphore_signal(barrier, inc=1, device_id=(self.s, self.yp(j)), device_id_type=MESH)
            count += 1
        pl.semaphore_wait(barrier, count)


class Sems:
    def __init__(self):
        self.n = 0

    def take(self, n):
        at = self.n
        self.n += n
        return at


def rcopy(sems, src, dst, send, recv, to):
    return pltpu.make_async_remote_copy(
        src_ref=src,
        dst_ref=dst,
        send_sem=sems.at[send],
        recv_sem=sems.at[recv],
        device_id=to,
        device_id_type=MESH,
    )


class Gather:
    def __init__(self, alloc, S, F, Y, kind):
        self.kind = kind
        Z = F // Y
        self.zs = alloc.take(Z - 1) - 1
        self.ys = alloc.take((Y - 1) * Z)
        self.ir = alloc.take(F - 1) - 1
        if kind != "own":
            self.ss, self.sr = alloc.take(F - 1) - 1, alloc.take(F - 1) - 1
        if kind == "quarter":
            n = (S // 2 - 1) * F
            self.xs, self.xr = alloc.take(n), alloc.take(n)
            self.ts, self.tr = alloc.take(n), alloc.take(n)

    def bind(self, g, sems, piece, place):
        self.g, self.sems, self.piece, self.place = g, sems, piece, place

    def part(self, hi=None, c=None):
        g = self.g
        c = g.c if c is None else c
        hi = g.hi if hi is None else hi
        return {"own": g.s, "half": c, "quarter": hi * 2 + c}[self.kind]

    def start_z(self):
        g, p = self.g, self.part()
        src, dst = self.piece(p), self.place(g.f, p)
        for k in range(1, g.Z):
            rcopy(self.sems, src, dst, self.zs + k, self.ir + k, (g.s, g.zp(k))).start()

    def start_y(self):
        g, p = self.g, self.part()
        src, dst = self.piece(p), self.place(g.f, p)
        for j in range(1, g.Y):
            rcopy(self.sems, src, dst, self.ys + (j - 1) * g.Z, self.ir + j * g.Z, (g.s, g.yp(j))).start()

    def wait_in(self, r):
        ref = self.place(self.g.origin(r), self.part())
        rcopy(self.sems, ref, ref, self.ir + r, self.ir + r, (self.g.sib(), self.g.f)).wait_recv()

    def pass_on(self, r):
        g = self.g
        ref = self.place(g.origin(r), self.part())
        if self.kind == "quarter":
            for m in range(1, g.H):
                rcopy(self.sems, ref, ref, self.xs + (m - 1) * g.F + r, self.xr + (m - 1) * g.F + r, (g.xp(m), g.f)).start()
        if self.kind != "own":
            rcopy(self.sems, ref, ref, self.ss + r, self.sr + r, (g.sib(), g.f)).start()

    def on_z(self):
        g = self.g

        def body(k):
            self.wait_in(k)
            ref = self.place(g.origin(k), self.part())
            for j in range(1, g.Y):
                at = j * g.Z + k
                rcopy(self.sems, ref, ref, self.ys + at - g.Z, self.ir + at, (g.s, g.yp(j))).start()
            self.pass_on(k)

        each(1, g.Z, body)

    def on_y(self):
        def body(r):
            self.wait_in(r)
            self.pass_on(r)

        each(self.g.Z, self.g.F, body)

    def on_x(self):
        if self.kind != "quarter":
            return
        g = self.g
        for m in range(1, g.H):
            part = self.part(hi=(g.hi + g.H - m) % g.H)

            def body(r):
                ref = self.place(g.origin(r), part)
                at = (m - 1) * g.F + r
                rcopy(self.sems, ref, ref, self.xr + at, self.xr + at, (g.sib(), g.f)).wait_recv()
                rcopy(self.sems, ref, ref, self.ts + at, self.tr + at, (g.sib(), g.f)).start()

            each(1, g.F, body)

    def complete(self):
        g = self.g
        other = 1 - g.c

        def got(ref, at):
            rcopy(self.sems, ref, ref, at, at, (g.sib(), g.f)).wait_recv()

        if self.kind != "own":
            each(1, g.F, lambda r: got(self.place(g.origin(r), self.part(c=other)), self.sr + r))
        if self.kind == "quarter":
            for m in range(1, g.H):
                part = self.part(hi=(g.hi + g.H - m) % g.H, c=other)
                each(1, g.F, lambda r: got(self.place(g.origin(r), part), self.tr + (m - 1) * g.F + r))

    def drain(self):
        g = self.g

        def sent(ref, at):
            rcopy(self.sems, ref, ref, at, at, (g.sib(), g.f)).wait_send()

        mine = self.piece(self.part())
        for k in range(1, g.Z):
            sent(mine, self.zs + k)
        for j in range(1, g.Y):
            each(0, g.Z, lambda k: sent(mine, self.ys + (j - 1) * g.Z + k))
        if self.kind != "own":
            each(1, g.F, lambda r: sent(mine, self.ss + r))
        if self.kind == "quarter":
            for m in range(1, g.H):
                each(1, g.F, lambda r: sent(mine, self.xs + (m - 1) * g.F + r))
                each(1, g.F, lambda r: sent(mine, self.ts + (m - 1) * g.F + r))


def forward_kernel(plan, x, wq, wk, wv, small, wo, w1, w2, cot, *rest):
    (xfull, wqkv, q_o, k_o, v_o, qt_o, kt_o, ot_o, lse_o, mixed_o, wo_o, w1_o, w2_o) = rest[:13]
    (nlow_o, nhat_o, inv_o, hidden_o, slope_o, out_o, gs_o, sums_o, vecs_o) = rest[13:22]
    (xs, ws, sm, qn, kn, vn, qt, kt, vt, ot, lse, oblk, onat) = rest[22:35]
    (wo_f, w1_f, w2_f, mixed, spread, vecs, normed, nhat, inv, nlow, hidden, slope) = rest[35:47]
    (branch, cots, outs, gs, sums, sems) = rest[47:]
    S, F, rows, heads, wide, vec = plan.S, plan.F, plan.rows, plan.heads, plan.wide, plan.vec
    width, ff = w1_f.shape
    g = Grid(S, F)
    g.greet(pltpu.get_barrier_semaphore())
    part_rows = wq.shape[0]

    def keep(src, dst, at):
        copy = pltpu.make_async_copy(src, dst, sems.at[at])
        copy.start()
        return copy

    mine = xs.at[pl.ds(g.s * rows, rows)]
    x_out = [rcopy(sems, x, mine, plan.x_s, plan.x_r, (g.sib(), g.f))]
    for m in range(1, g.H):
        x_out.append(rcopy(sems, x, mine, plan.x_s + m, plan.x_r + m, (g.xp(m), g.f)))
    for copy in x_out[::-1]:
        copy.start()
    for item, src, col in ((plan.gq, wq, 0), (plan.gk, wk, 1), (plan.gv, wv, 2)):
        item.bind(
            g,
            sems,
            lambda p, src=src: src.at[:, pl.ds(p * wide, wide)],
            lambda o, p, col=col: ws.at[pl.ds(o * part_rows, part_rows), pl.ds(col * wide, wide)],
        )
    plan.gs.bind(g, sems, lambda p: small, lambda o, p: sm.at[pl.ds(o * 16, 16)])
    first = (plan.gs, plan.gq, plan.gk, plan.gv)
    for item in first:
        item.start_z()
        item.start_y()
    for dst, src, entries in ((wo_f, wo, plan.go), (w1_f, w1, plan.g1), (w2_f, w2, plan.g2)):
        n = src.shape[0]
        for item, lo, part in entries:
            item.bind(
                g,
                sems,
                lambda p, src=src, lo=lo, part=part: src.at[:, pl.ds(lo + p * part, part)],
                lambda o, p, dst=dst, n=n, lo=lo, part=part: dst.at[pl.ds(o * n, n), pl.ds(lo + p * part, part)],
            )
    entries = plan.g1[:3] + plan.go + plan.g1[3:] + plan.g2
    big = [e[0] for e in entries]
    for item in big[:1]:
        item.start_y()
    for item in big[: plan.ahead]:
        item.start_z()
    local = [keep(x, mine, plan.l), keep(small, sm.at[pl.ds(g.f * 16, 16)], plan.l + 1), keep(cot, cots, plan.l + 2)]
    for col, src in enumerate((wq, wk, wv)):
        local.append(
            keep(
                src.at[:, pl.ds(g.s * wide, wide)],
                ws.at[pl.ds(g.f * part_rows, part_rows), pl.ds(col * wide, wide)],
                plan.l + 3 + col,
            )
        )
    for i, (src, dst) in enumerate(((wo, wo_f), (w1, w1_f), (w2, w2_f))):
        n = src.shape[0]
        local.append(keep(src, dst.at[pl.ds(g.f * n, n)], plan.l + 6 + i))
    for item in first:
        item.on_z()
    x_pass = []
    for m in range(1, g.H):
        theirs = xs.at[pl.ds(((g.hi + g.H - m) % g.H * 2 + g.c) * rows, rows)]
        rcopy(sems, theirs, theirs, plan.x_s, plan.x_r + m, (g.sib(), g.f)).wait_recv()
        copy = rcopy(sems, theirs, theirs, plan.x_s + g.H + m, plan.x_r + g.H + m, (g.sib(), g.f))
        copy.start()
        x_pass.append(copy)
    for item in first:
        item.on_y()
    rcopy(sems, mine, mine, plan.x_s, plan.x_r, (g.sib(), g.f)).wait_recv()
    for m in range(1, g.H):
        rcopy(sems, mine, mine, plan.x_s, plan.x_r + g.H + m, (g.sib(), g.f)).wait_recv()
    for copy in local:
        copy.wait()

    lane = lax.broadcasted_iota(jnp.int32, (vec, width), 1)
    pick = (lane % vec == lax.broadcasted_iota(jnp.int32, (vec, width), 0)).astype(f32).astype(bf16)
    spread[...] = jnp.dot(sm[...], pick, preferred_element_type=f32)
    fan = ff // width

    @pl.loop(0, 8 + fan)
    def _(i):
        row = lax.broadcasted_iota(jnp.int32, spread.shape, 0)
        column = lax.broadcasted_iota(jnp.int32, spread.shape, 1)
        at = (i - 8) * width + column
        plain = (column // vec) * 16 + i
        want = jnp.where(i < 8, plain, (at // (fan * vec)) * 16 + 8 + (at // vec) % fan)
        vecs[pl.ds(i, 1), :] = jnp.sum(jnp.where(row == want, spread[...], 0.0), axis=0, keepdims=True)

    own = pl.ds(pl.multiple_of(g.s * wide, wide), wide)

    def queries(b):
        at = pl.multiple_of(b * rows, rows)
        prod = jnp.dot(xs[pl.ds(at, rows), :], ws[...], preferred_element_type=f32)
        q = (prod[:, :wide] + vecs[0:1, own]).astype(bf16).astype(f32) * 0.125
        k = prod[:, wide : 2 * wide]
        v = prod[:, 2 * wide :] + vecs[1:2, own]
        qn[pl.ds(at, rows), :] = q.astype(bf16)
        kn[pl.ds(at, rows), :] = k.astype(bf16)
        vn[pl.ds(at, rows), :] = v.astype(bf16)
        qt[:, pl.ds(at, rows)] = q.T.astype(bf16)
        kt[:, pl.ds(at, rows)] = k.T.astype(bf16)
        vt[:, pl.ds(at, rows)] = v.T.astype(bf16)

    stores = []
    head_of = lax.broadcasted_iota(jnp.int32, (wide, rows), 0) // HD
    sent = []

    def attend(t):
        hi = (g.hi + 1 + t // 2) % g.H
        c = (g.c + t + t // (2 * (g.H - 1))) % 2
        to = hi * 2 + c
        at = pl.multiple_of(to * rows, rows)

        @pl.loop(0, heads)
        def _(h):
            q = jnp.where(head_of == h, qt[:, pl.ds(at, rows)], jnp.zeros((), bf16))
            s = jnp.dot(kn[...], q, preferred_element_type=f32)
            m = jnp.max(s, axis=0, keepdims=True)
            e = jnp.exp(s - m)
            l = jnp.sum(e, axis=0, keepdims=True)
            band = pl.ds(pl.multiple_of(h * HD, HD), HD)
            o = jnp.dot(vt[band, :], e.astype(bf16), preferred_element_type=f32) / l
            oblk[band, :] = o
            lse[pl.ds(h, 1), pl.ds(at, rows)] = m + jnp.log(l)

        ot[:, pl.ds(at, rows)] = oblk[...].astype(bf16)
        onat[t] = oblk[...].T.astype(bf16)
        dst = mixed.at[:, pl.ds(g.s * wide, wide)]
        if t < S - 1:
            copy = rcopy(sems, onat.at[t], dst, plan.o_s + t, plan.o_r + g.s, (to, g.f))
            copy.start()
            sent.append(copy)
        else:
            mixed[:, own] = onat[t]
            stores.append(keep(ot, ot_o, plan.l + 16))
            stores.append(keep(lse, lse_o, plan.l + 17))

    def normalize(stream):
        centre = stream - jnp.mean(stream, axis=1, keepdims=True)
        scale = lax.rsqrt(jnp.mean(centre * centre, axis=1, keepdims=True) + 1e-05)
        return centre * scale, scale

    def count(row, value):
        sums[pl.ds(row, 1), :] += jnp.sum(value, axis=0, keepdims=True)

    chunk = 128 if rows % 128 == 0 else rows

    def project():
        for i in range(1, S):
            peer = (g.s + i) % S
            ref = mixed.at[:, pl.ds(peer * wide, wide)]
            rcopy(sems, ref, ref, plan.o_r + peer, plan.o_r + peer, (peer, g.f)).wait_recv()
        sums[...] = jnp.zeros_like(sums)

        @pl.loop(0, rows // chunk)
        def _(b):
            at = pl.ds(pl.multiple_of(b * chunk, chunk), chunk)
            tokens = xs[pl.ds(pl.multiple_of(g.s * rows + b * chunk, chunk), chunk), :].astype(f32)
            attn = jnp.dot(mixed[at, :], wo_f[...], preferred_element_type=f32) + vecs[2:3, :]
            count(3, tokens * tokens)
            count(4, attn * attn)
            unit, scale = normalize(tokens + attn)
            value = unit * vecs[3:4, :] + vecs[4:5, :]
            count(5, value * value)
            normed[at, :] = value
            nhat[at, :] = unit
            inv[at, :] = jnp.broadcast_to(scale, (chunk, inv.shape[1]))
            nlow[at, :] = value.astype(bf16)

        for i, (src, dst) in enumerate(
            ((mixed, mixed_o), (nhat, nhat_o), (inv, inv_o), (nlow, nlow_o), (wo_f, wo_o))
        ):
            stores.append(keep(src, dst, plan.l + 18 + i))

    def expand(b):
        part = width // 2

        @pl.loop(0, 2)
        def _(i):
            at = pl.ds(pl.multiple_of(b * width + i * part, part), part)
            bias = vecs[8 + b : 9 + b, pl.ds(pl.multiple_of(i * part, part), part)]
            pre = jnp.dot(nlow[...], w1_f[:, at], preferred_element_type=f32) + bias
            below = 0.5 * lax.erf(pre * 0.7071067811865476) + 0.5
            hidden[:, at] = (pre * below).astype(bf16)
            slope[:, at] = (below + pre * (jnp.exp(pre * pre * -0.5) * 0.3989422804014327)).astype(bf16)

    def contract(i):
        lo, part = entries[i][1:]
        n = part * (S if big[i].kind == "quarter" else 2)
        at = pl.ds(lo, n)
        branch[:, at] = jnp.dot(hidden[...], w2_f[:, at], preferred_element_type=f32) + vecs[5:6, at]
        stores.append(keep(w2_f.at[:, at], w2_o.at[:, at], plan.l + 31 + i))

    def close():
        @pl.loop(0, rows // chunk)
        def _(b):
            at = pl.ds(pl.multiple_of(b * chunk, chunk), chunk)
            value = branch[at, :]
            count(6, value * value)
            unit, scale = normalize(normed[at, :] + value)
            gain = vecs[6:7, :]
            value = unit * gain + vecs[7:8, :]
            count(7, value * value)
            outs[at, :] = value.astype(bf16)
            r = cots[at, :].astype(f32)
            count(0, r * unit)
            count(1, r)
            rg = r * gain
            grad = rg - jnp.mean(rg, axis=1, keepdims=True) - unit * jnp.mean(rg * unit, axis=1, keepdims=True)
            grad = grad * scale
            gs[at, :] = grad
            count(2, grad.astype(bf16).astype(f32))

        for i, (src, dst) in enumerate(((outs, out_o), (gs, gs_o), (sums, sums_o), (vecs, vecs_o))):
            stores.append(keep(src, dst, plan.l + 23 + i))

    turn = 0
    for op in plan.order:
        what, on = op[0], int(op[1:] or 0)
        if what == "P":
            pl.loop(0, S)(queries)
            for i, (src, dst) in enumerate(
                ((xs, xfull), (ws, wqkv), (qn, q_o), (kn, k_o), (vn, v_o), (qt, qt_o), (kt, kt_o))
            ):
                stores.append(keep(src, dst, plan.l + 9 + i))
        elif what == "T":
            attend(turn)
            turn += 1
        elif what in "zyxC":
            item = big[on]
            {"z": item.on_z, "y": item.on_y, "x": item.on_x, "C": item.complete}[what]()
            if what == "z" and 1 <= on + 1 < len(big):
                big[on + 1].start_y()
            if what == "z" and on + plan.ahead < len(big):
                big[on + plan.ahead].start_z()
        elif what == "O":
            project()
        elif what == "E":
            expand(on)
            if on == fan - 1:
                for i, (src, dst) in enumerate(((hidden, hidden_o), (slope, slope_o), (w1_f, w1_o))):
                    stores.append(keep(src, dst, plan.l + 28 + i))
        elif what == "B":
            contract(on)
        else:
            close()
    for item in (*first, *big):
        item.drain()
    for copy in sent + x_out + x_pass:
        copy.wait_send()
    for copy in stores:
        copy.wait()


class Plan:
    pass


def forward_plan(S, F, rows, width, ff):
    plan = Plan()
    alloc = Sems()
    plan.S, plan.F, plan.rows = S, F, rows
    plan.wide = width // S
    plan.heads = plan.wide // HD
    plan.vec = width // F
    Y = 2 if F % 2 == 0 and F <= 8 else 4
    plan.x_s, plan.x_r = alloc.take(S), alloc.take(S)
    plan.gq, plan.gk, plan.gv, plan.gs = (Gather(alloc, S, F, Y, "own") for _ in range(4))
    half = width // 2
    plan.go = [(Gather(alloc, S, F, Y, "half"), 0, half)]
    fan = ff // width
    kind, shares = ("quarter", S) if F <= 8 else ("half", 2)
    plan.g1 = [(Gather(alloc, S, F, Y, kind), i * width, width // shares) for i in range(fan)]
    plan.g2 = [(Gather(alloc, S, F, Y, "quarter"), 0, half // S)]
    plan.g2 += [(Gather(alloc, S, F, Y, "half"), half + i * half // 2, half // 4) for i in range(2)]
    plan.ahead = 2
    plan.order = (
        *("z0", "y0", "z1", "z2", "y1", "P", "z3", "T", "T", "x1", "z4", "x0", "T", "y3",),
        *("y2", "T", "y4", "C3", "z5", "O", "z6", "C0", "x2", "x4", "C1", "C2", "y5", "C4",),
        *("E0", "E1", "z7", "y6", "E2", "E3", "C6", "x5", "y7", "B6", "C5", "C7", "B7", "B5",),
        *("N",),
    )
    plan.o_s, plan.o_r = alloc.take(S), alloc.take(S)
    plan.l = alloc.take(40)
    plan.sems = alloc.n
    return plan


def forward(S, F, x, wq, wk, wv, small, wo, w1, w2, cot):
    rows, width = x.shape
    ff = w1.shape[1]
    plan = forward_plan(S, F, rows, width, ff)
    wide = plan.wide
    length = rows * S
    sds = jax.ShapeDtypeStruct
    any_ = pl.BlockSpec(memory_space=pl.ANY)
    vmem = pltpu.VMEM
    return pl.pallas_call(
        functools.partial(forward_kernel, plan),
        out_shape=(
            sds((length, width), bf16),
            sds((width, 3 * wide), bf16),
            sds((length, wide), bf16),
            sds((length, wide), bf16),
            sds((length, wide), bf16),
            sds((wide, length), bf16),
            sds((wide, length), bf16),
            sds((wide, length), bf16),
            sds((8, length), f32),
            sds((rows, width), bf16),
            sds((width, width), bf16),
            sds((width, ff), bf16),
            sds((ff, width), bf16),
            sds((rows, width), bf16),
            sds((rows, width), f32),
            sds((rows, 128), f32),
            sds((rows, ff), bf16),
            sds((rows, ff), bf16),
            sds((rows, width), bf16),
            sds((rows, width), f32),
            sds((8, width), f32),
            sds((16, width), f32),
        ),
        in_specs=[any_] * 9,
        out_specs=(any_,) * 22,
        scratch_shapes=[
            vmem((length, width), bf16),
            vmem((width, 3 * wide), bf16),
            vmem((F * 16, plan.vec), bf16),
            vmem((length, wide), bf16),
            vmem((length, wide), bf16),
            vmem((length, wide), bf16),
            vmem((wide, length), bf16),
            vmem((wide, length), bf16),
            vmem((wide, length), bf16),
            vmem((wide, length), bf16),
            vmem((8, length), f32),
            vmem((wide, rows), f32),
            vmem((S, rows, wide), bf16),
            vmem((width, width), bf16),
            vmem((width, ff), bf16),
            vmem((ff, width), bf16),
            vmem((rows, width), bf16),
            vmem((F * 16, width), f32),
            vmem((16, width), f32),
            vmem((rows, width), f32),
            vmem((rows, width), f32),
            vmem((rows, 128), f32),
            vmem((rows, width), bf16),
            vmem((rows, ff), bf16),
            vmem((rows, ff), bf16),
            vmem((rows, width), f32),
            vmem((rows, width), bf16),
            vmem((rows, width), bf16),
            vmem((rows, width), f32),
            vmem((8, width), f32),
            pltpu.SemaphoreType.DMA((plan.sems,)),
        ],
        compiler_params=pltpu.CompilerParams(collective_id=0, has_side_effects=True, vmem_limit_bytes=63 << 20),
        name="forward_with_weight_gather",
    )(x, wq, wk, wv, small, wo, w1, w2, cot)


class Reduce:
    def __init__(self, alloc, S, F, Y, R, C, kind):
        self.kind, self.R, self.C = kind, R, C
        self.S, self.F, self.Y, self.Z, self.H = S, F, Y, F // Y, S // 2
        Z, H = self.Z, self.H
        self.w = {"half": C // 2, "quarter": C // S, "own": C}[kind]
        w = self.w
        self.n = H if kind == "quarter" else 1
        self.shapes = [(self.n, Z, Y, R, w), (Y - 1, Z, R, w), (Z, R, w)]
        if kind == "own":
            self.shapes += [(S, R, w)]
        else:
            self.shapes += [(self.n, Z, Y, R, w), (R, C)]
            self.shapes += [(H - 1, Z, Y, R, w) if kind == "quarter" else (H - 1, R, w)]
        self.shapes = [pltpu.VMEM(s, bf16) for s in self.shapes]
        self.load = alloc.take(H)
        self.ds, self.dr = alloc.take(H), alloc.take(H)
        self.xs, self.xr = alloc.take(H), alloc.take(H)
        self.ys, self.yr = alloc.take(Y), alloc.take(Y)
        self.zs, self.zr = alloc.take(Z), alloc.take(Z)
        self.fs, self.fr = alloc.take(2 * H), alloc.take(2 * H)
        self.out = alloc.take(1)

    def bind(self, g, sems, refs, source, dest):
        self.g, self.sems, self.source, self.dest = g, sems, source, dest
        if self.kind == "own":
            self.own, self.ry, self.rz, self.fin = refs
        else:
            self.own, self.ry, self.rz, self.rd, self.fin, self.rx = refs
        self.sends = []

    def send(self, src, dst, s, r, to):
        copy = rcopy(self.sems, src, dst, s, r, to)
        copy.start()
        self.sends.append(copy)

    def recv(self, ref, r):
        rcopy(self.sems, ref, ref, r, r, (self.g.sib(), self.g.f)).wait_recv()

    def column(self, hi, c):
        return (hi * 2 + c) * self.w if self.kind == "quarter" else c * self.w

    def start(self):
        g = self.g
        self.loads = []
        for m in range(self.n):
            hi = (g.hi + m) % g.H
            self.send(
                self.source(self.column(hi, 1 - g.c), self.w),
                self.rd.at[m],
                self.ds + m,
                self.dr + m,
                (g.sib(), g.f),
            )
            copy = pltpu.make_async_copy(
                self.source(self.column(hi, g.c), self.w), self.own.at[m], self.sems.at[self.load + m]
            )
            copy.start()
            self.loads.append(copy)

    def add_all(self, m, other):
        @pl.loop(0, self.Z * self.Y)
        def _(i):
            a, b = i // self.Y, i % self.Y
            self.own[m, a, b] = (self.own[m, a, b].astype(f32) + other(a, b).astype(f32)).astype(bf16)

    def over_cores(self):
        for m in list(range(1, self.n)) + [0]:
            self.loads[m].wait()
            self.recv(self.rd.at[m], self.dr + m)
            self.add_all(m, lambda a, b: self.rd[m, a, b])
            if m:
                self.send(self.own.at[m], self.rx.at[m - 1], self.xs + m, self.xr + m, (self.g.xp(m), self.g.f))
        if self.kind == "half":
            self.send_y()

    def over_x_first(self):
        for m in range(1, self.H):
            self.recv(self.rx.at[m - 1], self.xr + m)
            self.add_all(0, lambda a, b: self.rx[m - 1, a, b])
        self.send_y()

    def send_y(self):
        g = self.g
        for j in range(1, g.Y):
            y = (g.y + j) % g.Y
            self.send(self.own.at[0, :, y], self.ry.at[j - 1], self.ys + j, self.yr + j, (g.s, g.yp(j)))

    def over_y(self):
        g = self.g
        for j in range(1, g.Y):
            self.recv(self.ry.at[j - 1], self.yr + j)

        @pl.loop(0, self.Z)
        def _(a):
            total = self.own[0, a, g.y].astype(f32)
            for j in range(1, g.Y):
                total += self.ry[j - 1, a].astype(f32)
            self.own[0, a, g.y] = total.astype(bf16)

        for k in range(1, g.Z):
            z = (g.z + k) % g.Z
            self.send(self.own.at[0, z, g.y], self.rz.at[k], self.zs + k, self.zr + k, (g.s, g.zp(k)))

    def over_z(self):
        g = self.g
        total = self.own[0, g.z, g.y].astype(f32)
        for k in range(1, g.Z):
            self.recv(self.rz.at[k], self.zr + k)
            total += self.rz[k].astype(f32)
        total = total.astype(bf16)
        if self.kind == "half":
            self.rz[0] = total
            for m in range(1, g.H):
                self.send(self.rz.at[0], self.rx.at[m - 1], self.xs + m, self.xr + m, (g.xp(m), g.f))
            return
        if self.kind == "own":
            self.fin[g.s] = total
            ref = self.fin.at[g.s]
        else:
            at = pl.multiple_of(self.column(g.hi, g.c), self.w)
            self.fin[:, pl.ds(at, self.w)] = total
            ref = self.fin.at[:, pl.ds(at, self.w)]
        for m in range(1, g.H):
            self.send(ref, ref, self.fs + m, self.fr + m, (g.xp(m), g.f))
        self.send(ref, ref, self.fs, self.fr, (g.sib(), g.f))

    def over_x_last(self):
        g = self.g
        if self.kind == "half":
            total = self.rz[0].astype(f32)
            for m in range(1, g.H):
                self.recv(self.rx.at[m - 1], self.xr + m)
                total += self.rx[m - 1].astype(f32)
            at = pl.multiple_of(g.c * self.w, self.w)
            self.fin[:, pl.ds(at, self.w)] = total.astype(bf16)
            ref = self.fin.at[:, pl.ds(at, self.w)]
            self.send(ref, ref, self.fs, self.fr, (g.sib(), g.f))
            return
        for m in range(1, g.H):
            hi = (g.hi + g.H - m) % g.H
            if self.kind == "own":
                ref = self.fin.at[hi * 2 + g.c]
            else:
                ref = self.fin.at[:, pl.ds(self.column(hi, g.c), self.w)]
            self.recv(ref, self.fr + m)
            self.send(ref, ref, self.fs + g.H + m, self.fr + g.H + m, (g.sib(), g.f))

    def finish(self):
        g = self.g
        for m in range(g.H if self.kind != "half" else 1):
            hi = (g.hi + g.H - m) % g.H
            if self.kind == "own":
                ref = self.fin.at[hi * 2 + 1 - g.c]
            else:
                ref = self.fin.at[:, pl.ds(self.column(hi, 1 - g.c), self.w)]
            self.recv(ref, self.fr + (g.H + m if m else 0))
        self.copy_out = pltpu.make_async_copy(self.fin, self.dest, self.sems.at[self.out])
        self.copy_out.start()

    def done(self):
        for copy in self.sends:
            copy.wait_send()
        self.copy_out.wait()

    def step(self, name):
        {
            "D": self.over_cores,
            "X": self.over_x_first if self.kind == "quarter" else self.over_x_last,
            "Y": self.over_y,
            "Z": self.over_z,
            "L": self.over_x_last,
            "F": self.finish,
        }[name]()


def backward_kernel(plan, g_o, q_i, k_i, v_i, qt_i, kt_i, ot_i, lse_i, x_i, w_i, gh, table_i, dwo, dw1, dw2, *rest):
    dx_o, dqkv_o, dwo_o, dw1_o, dw2_o, table_o = rest[:6]
    (go, qn, kn, vn, qt, kt, ot, lse, xs, ws, dk, dv, dqt, dt, delta, grads) = rest[6:22]
    (dx, dx_send, dx_core, dx_out, dx_x, tab, tab_core, tab_x, tab_y, tab_s, tab_z, sems) = rest[22:34]
    pools = rest[34:]
    S, F, rows, heads, wide, vec = plan.S, plan.F, plan.rows, plan.heads, plan.wide, plan.vec
    g = Grid(S, F)
    g.greet(pltpu.get_barrier_semaphore())

    def keep(src, dst, at):
        copy = pltpu.make_async_copy(src, dst, sems.at[at])
        copy.start()
        return copy

    sent = []

    def send(src, dst, s, r, to):
        copy = rcopy(sems, src, dst, s, r, to)
        copy.start()
        sent.append(copy)

    def recv(ref, r):
        rcopy(sems, ref, ref, r, r, (g.sib(), g.f)).wait_recv()

    for m in [*range(1, g.H), 0]:
        for flip in range(2):
            if m or flip:
                to = ((g.hi + m) % g.H) * 2 + (g.c + flip) % 2
                send(
                    g_o.at[:, pl.ds(to * wide, wide)],
                    go.at[g.s],
                    plan.o_s + m * 2 + flip,
                    plan.o_r + g.s,
                    (to, g.f),
                )
    used = 0
    for item, which, col, row in plan.items:
        n = len(item.shapes)
        src, dst = {"o": (dwo, dwo_o), "1": (dw1, dw1_o), "2": (dw2, dw2_o)}[which]
        item.bind(
            g,
            sems,
            pools[used : used + n],
            lambda lo, width, src=src, item=item, col=col, row=row: src.at[
                :, :, pl.ds(row, item.R), pl.ds(col + lo, width)
            ],
            dst.at[pl.ds(row, item.R), pl.ds(col, item.C)],
        )
        used += n
        item.start()
    for i, item in enumerate(plan.qkv):
        item.bind(g, sems, pools[used : used + 4], None, dqkv_o.at[i])
        used += 4
    loads = [
        keep(src, dst, plan.l + i)
        for i, (src, dst) in enumerate(
            (
                (g_o.at[:, pl.ds(g.s * wide, wide)], go.at[g.s]),
                (q_i, qn),
                (k_i, kn),
                (v_i, vn),
                (qt_i, qt),
                (kt_i, kt),
                (ot_i, ot),
                (lse_i, lse),
                (x_i, xs),
                (w_i, ws),
                (gh, dx),
                (table_i, tab),
            )
        )
    ]
    items = [entry[0] for entry in plan.items]
    dk[...] = jnp.zeros_like(dk)
    dv[...] = jnp.zeros_like(dv)
    for copy in loads:
        copy.wait()
    head_of = lax.broadcasted_iota(jnp.int32, (wide, rows), 0) // HD
    head_at = lax.broadcasted_iota(jnp.int32, (rows, wide), 1) // HD
    none = jnp.zeros((), bf16)

    def attend(t):
        if t == 0:
            for i in range(1, S):
                peer = (g.s + i) % S
                recv(go.at[peer], plan.o_r + peer)
        span = pl.ds(t * rows, rows)
        turned = go[t].astype(f32).T
        dt[...] = turned.astype(bf16)
        weighed = turned * ot[:, span].astype(f32)
        for h in range(heads):
            delta[pl.ds(h, 1), :] = jnp.sum(weighed[h * HD : (h + 1) * HD], axis=0, keepdims=True)

        @pl.loop(0, heads)
        def _(h):
            band = pl.ds(pl.multiple_of(h * HD, HD), HD)
            s = jnp.dot(kn[...], jnp.where(head_of == h, qt[:, span], none), preferred_element_type=f32)
            p = jnp.exp(s - lse[pl.ds(h, 1), span])
            dp = jnp.dot(vn[...], jnp.where(head_of == h, dt[...], none), preferred_element_type=f32)
            ds = (p * (dp - delta[pl.ds(h, 1), :])).astype(bf16)
            dv[...] += jnp.dot(p.astype(bf16), jnp.where(head_at == h, go[t], none), preferred_element_type=f32)
            dk[...] += jnp.dot(ds, jnp.where(head_at == h, qn[span, :], none), preferred_element_type=f32)
            dqt[band, span] = jnp.dot(kt[band, :], ds, preferred_element_type=f32) * 0.125

    totals = []

    def projections(i):
        if i == 0:
            sum_q = jnp.zeros((1, wide), f32)
            sum_v = jnp.zeros((1, wide), f32)
            for t in range(S):
                span = pl.ds(t * rows, rows)
                q = dqt[:, span].T.astype(bf16)
                v = dv[span, :].astype(bf16)
                grads[span, pl.ds(0, wide)] = q
                grads[span, pl.ds(wide, wide)] = dk[span, :].astype(bf16)
                grads[span, pl.ds(2 * wide, wide)] = v
                sum_q += jnp.sum(q.astype(f32), axis=0, keepdims=True)
                sum_v += jnp.sum(v.astype(f32), axis=0, keepdims=True)
            totals.extend((sum_q, sum_v))
        item = plan.qkv[i]
        part_rows, width = item.R, xs.shape[1]
        step = max(part_rows, 256)
        for lo in range(0, width, step):
            prod = lax.dot_general(
                xs[:, pl.ds(lo, step)],
                grads[:, pl.ds(i * wide, wide)],
                (((0,), (0,)), ((), ())),
                preferred_element_type=f32,
            ).astype(bf16)
            for j in range(step // part_rows):
                to = lo // part_rows + j
                item.own[0, to // g.Y, to % g.Y] = prod[j * part_rows : (j + 1) * part_rows]
        item.send_y()

    def part(to):
        return lax.dot_general(
            grads[pl.ds(pl.multiple_of(to * rows, rows), rows), :],
            ws[...],
            (((1,), (1,)), ((), ())),
            preferred_element_type=f32,
        )

    def input_parts():
        for m in [*range(1, g.H), 0]:
            hi = (g.hi + m) % g.H
            dx_send[m] = part(hi * 2 + 1 - g.c).astype(bf16)
            send(dx_send.at[m], dx_core.at[m], plan.dx + m, plan.dx + g.H + m, (g.sib(), g.f))
        for m in [*range(1, g.H), 0]:
            hi = (g.hi + m) % g.H
            value = part(hi * 2 + g.c)
            recv(dx_core.at[m], plan.dx + g.H + m)
            value += dx_core[m].astype(f32)
            if m:
                dx_out[m - 1] = value.astype(bf16)
                send(dx_out.at[m - 1], dx_x.at[m - 1], plan.dx + 2 * g.H + m, plan.dx + 3 * g.H + m, (g.xp(m), g.f))
            else:
                dx[...] += value

    out = []

    def input_done():
        for m in range(1, g.H):
            recv(dx_x.at[m - 1], plan.dx + 3 * g.H + m)
            dx[...] += dx_x[m - 1].astype(f32)
        out.append(keep(dx, dx_o, plan.l + 13))

    def vectors(stage):
        Y = g.Y
        if stage == 0:
            base = g.s * (wide // vec)
            for i in range(wide // vec):
                to = base + i
                for row, value in enumerate(totals):
                    tab[to // Y, to % Y, pl.ds(row, 1), :] = value[:, i * vec : (i + 1) * vec]
            send(tab, tab_core, plan.t, plan.t + 1, (g.sib(), g.f))
        if stage == 1:
            recv(tab_core, plan.t + 1)
            tab_x[g.hi] = tab[...] + tab_core[...]
            for m in range(1, g.H):
                send(tab_x.at[g.hi], tab_x.at[g.hi], plan.tx + m, plan.tx + g.H + g.hi, (g.xp(m), g.f))
        if stage == 2:
            for m in range(1, g.H):
                hi = (g.hi + m) % g.H
                recv(tab_x.at[hi], plan.tx + g.H + hi)
            total = tab_x[0]
            for m in range(1, g.H):
                total += tab_x[m]
            tab_core[...] = total
            tab_y[g.y] = tab_core[:, g.y]
            for j in range(1, Y):
                y = (g.y + j) % Y
                send(tab_core.at[:, y], tab_y.at[g.y], plan.ty + j, plan.ty + Y + g.y, (g.s, g.yp(j)))
        if stage == 3:
            for j in range(1, Y):
                y = (g.y + j) % Y
                recv(tab_y.at[y], plan.ty + Y + y)
            total = tab_y[0]
            for j in range(1, Y):
                total += tab_y[j]
            tab_s[...] = total
            tab_z[g.z] = tab_s[g.z]
            for k in range(1, g.Z):
                z = (g.z + k) % g.Z
                send(tab_s.at[z], tab_z.at[g.z], plan.tz + k, plan.tz + g.Z + g.z, (g.s, g.zp(k)))
        if stage == 4:
            for k in range(1, g.Z):
                z = (g.z + k) % g.Z
                recv(tab_z.at[z], plan.tz + g.Z + z)
            total = tab_z[0]
            for k in range(1, g.Z):
                total += tab_z[k]
            tab_y[0, 0] = total
            out.append(keep(tab_y.at[0, 0], table_o, plan.l + 12))

    named = {chr(ord("a") + i): item for i, item in enumerate(items)}
    named.update({"q%d" % i: item for i, item in enumerate(plan.qkv)})
    for op in plan.order:
        what, on = op[0], op[1:]
        if what == "T":
            attend(int(on))
        elif what == "G":
            projections(int(on))
        elif what == "I":
            input_parts()
        elif what == "J":
            input_done()
        elif what == "V":
            vectors(int(on))
        else:
            named[on].step(what)
    for item in (*items, *plan.qkv):
        item.done()
    for copy in sent:
        copy.wait_send()
    for copy in out:
        copy.wait()


def backward_plan(S, F, rows, width, ff):
    plan = Plan()
    alloc = Sems()
    plan.S, plan.F, plan.rows = S, F, rows
    plan.wide = width // S
    plan.heads = plan.wide // HD
    plan.vec = width // F
    Y = 2 if F % 2 == 0 and F <= 8 else 4
    R, R2 = width // F, ff // F
    ones = [(Reduce(alloc, S, F, Y, R, width, "quarter"), "1", i * width, 0) for i in range(ff // width)]
    twos = [(Reduce(alloc, S, F, Y, R2 // 4, width, "half"), "2", 0, i * (R2 // 4)) for i in range(4)]
    plan.items = [e for pair in zip(ones, twos) for e in pair]
    plan.items.append((Reduce(alloc, S, F, Y, R, width, "half"), "o", 0, 0))
    plan.qkv = [Reduce(alloc, S, F, Y, R, plan.wide, "own") for _ in range(3)]
    plan.o_s, plan.o_r = alloc.take(S), alloc.take(S)
    plan.dx = alloc.take(4 * S)
    plan.t, plan.tx, plan.ty, plan.tz = alloc.take(2), alloc.take(S), alloc.take(2 * Y), alloc.take(2 * F // Y)
    plan.l = alloc.take(14)
    plan.order = (
        "Da", "Db", "Dc", "Dd", "T0", "Df", "De", "Yb", "T1", "Xa", "T2", "Dg", "Yd", "Dh", "Zb", "Xc",
        "T3", "Yf", "G0", "Xe", "Ya", "Zd", "G1", "G2", "I", "Xg", "V0", "Yh", "Xb", "Zf", "V1", "Fb",
        "Xd", "Fd", "Yc", "Za", "Yq0", "Ye", "Di", "Zh", "J", "Yq1", "Xf", "Zc", "V2", "Ff", "La", "Fa",
        "Yq2", "Xh", "Zq0", "Lc", "Fh", "Fc", "Lq0", "Yg", "Fq0", "Ze", "Le", "Fe", "Zq1", "Lq1", "Yi", "Fq1",
        "V3", "Zq2", "Lq2", "Fq2", "Zg", "Lg", "Fg", "Zi", "V4", "Xi", "Fi",
    )
    plan.sems = alloc.n
    return plan


def backward(S, F, g_o, q, k, v, qt, kt, ot, lse, x, w, gh, table, dwo, dw1, dw2):
    rows, width = g_o.shape
    ff = dw1.shape[-1]
    plan = backward_plan(S, F, rows, width, ff)
    wide, vec = plan.wide, plan.vec
    length = rows * S
    Z, Y = table.shape[:2]
    H = S // 2
    R, R2 = width // F, ff // F
    sds = jax.ShapeDtypeStruct
    any_ = pl.BlockSpec(memory_space=pl.ANY)
    pools = [s for e in plan.items for s in e[0].shapes] + [s for i in plan.qkv for s in i.shapes]
    return pl.pallas_call(
        functools.partial(backward_kernel, plan),
        out_shape=(
            sds((rows, width), f32),
            sds((3, S, R, wide), bf16),
            sds((R, width), bf16),
            sds((R, ff), bf16),
            sds((R2, width), bf16),
            sds((16, vec), f32),
        ),
        in_specs=[any_] * 15,
        out_specs=(any_,) * 6,
        scratch_shapes=[
            pltpu.VMEM((S, rows, wide), bf16),
            pltpu.VMEM((length, wide), bf16),
            pltpu.VMEM((length, wide), bf16),
            pltpu.VMEM((length, wide), bf16),
            pltpu.VMEM((wide, length), bf16),
            pltpu.VMEM((wide, length), bf16),
            pltpu.VMEM((wide, length), bf16),
            pltpu.VMEM((8, length), f32),
            pltpu.VMEM((length, width), bf16),
            pltpu.VMEM((width, 3 * wide), bf16),
            pltpu.VMEM((length, wide), f32),
            pltpu.VMEM((length, wide), f32),
            pltpu.VMEM((wide, length), f32),
            pltpu.VMEM((wide, rows), bf16),
            pltpu.VMEM((8, rows), f32),
            pltpu.VMEM((length, 3 * wide), bf16),
            pltpu.VMEM((rows, width), f32),
            pltpu.VMEM((H, rows, width), bf16),
            pltpu.VMEM((H, rows, width), bf16),
            pltpu.VMEM((H - 1, rows, width), bf16),
            pltpu.VMEM((H - 1, rows, width), bf16),
            pltpu.VMEM((Z, Y, 16, vec), f32),
            pltpu.VMEM((Z, Y, 16, vec), f32),
            pltpu.VMEM((H, Z, Y, 16, vec), f32),
            pltpu.VMEM((Y, Z, 16, vec), f32),
            pltpu.VMEM((Z, 16, vec), f32),
            pltpu.VMEM((Z, 16, vec), f32),
            pltpu.SemaphoreType.DMA((plan.sems,)),
            *pools,
        ],
        compiler_params=pltpu.CompilerParams(collective_id=1, has_side_effects=True, vmem_limit_bytes=63 << 20),
        name="attention_backward_and_gradient_sums",
    )(g_o, q, k, v, qt, kt, ot, lse, x, w, gh, table, dwo, dw1, dw2)


def layer_norm(stream, gain, shift):
    centre = stream - jnp.mean(stream, axis=-1, keepdims=True)
    variance = jnp.mean(centre * centre, axis=-1, keepdims=True)
    return centre * lax.rsqrt(variance + 1e-05) * gain + shift


def gelu_exact(inputs):
    return jax.nn.gelu(inputs, approximate=False)


def column_sums(matrix):
    return jnp.sum(matrix.astype(f32), axis=0)


def local(
    layer_input,
    query_weight,
    key_weight,
    value_weight,
    output_weight,
    query_bias,
    value_bias,
    output_bias,
    attn_gain,
    attn_shift,
    in_weight,
    in_bias,
    out_weight,
    out_bias,
    out_gain,
    out_shift,
    out_cotangent,
):
    F = lax.axis_size("fsdp")
    S = lax.axis_size("seq")
    width = layer_input.shape[-1]
    tokens = layer_input.reshape(-1, width)
    rows = tokens.shape[0]
    vec = query_bias.shape[0]
    held = (query_bias, value_bias, output_bias, attn_gain, attn_shift, out_bias, out_gain, out_shift)
    fan = in_bias.shape[0] // vec
    small = jnp.concatenate(
        [v.reshape(1, vec) for v in held]
        + [in_bias.reshape(fan, vec), jnp.zeros((16 - len(held) - fan, vec), bf16)]
    )
    (xfull, wqkv, q, k, v, qt, kt, ot, lse, mixed, wo, w1, w2, nlow, nhat, inv, hidden, slope, out, grad_stream, sums, vectors) = (
        forward(
            S,
            F,
            tokens,
            query_weight,
            key_weight,
            value_weight,
            small,
            output_weight,
            in_weight,
            out_weight,
            out_cotangent.reshape(rows, width),
        )
    )
    gain_one = vectors[3]
    grad_gain_two, grad_shift_two, grad_bias_out = sums[0], sums[1], sums[2]
    squares = jnp.sum(sums[3:8], axis=1)
    inv = inv[:, :1]
    grad_branch = grad_stream.astype(bf16)
    grad_out = jnp.dot(hidden.T, grad_branch, preferred_element_type=f32)
    grad_hidden = jnp.dot(grad_branch, w2.T, preferred_element_type=f32)
    grad_pre = (grad_hidden * slope.astype(f32)).astype(bf16)
    grad_bias_in = column_sums(grad_pre)
    grad_in = jnp.dot(nlow.T, grad_pre, preferred_element_type=f32)
    grad_normed = grad_stream + jnp.dot(grad_pre, w1.T, preferred_element_type=f32)
    grad_gain_one = jnp.sum(grad_normed * nhat, axis=0)
    grad_shift_one = jnp.sum(grad_normed, axis=0)
    weighed = grad_normed * gain_one
    grad_h = inv * (
        weighed
        - jnp.mean(weighed, axis=1, keepdims=True)
        - nhat * jnp.mean(weighed * nhat, axis=1, keepdims=True)
    )
    grad_attn = grad_h.astype(bf16)
    grad_bias_output = column_sums(grad_attn)
    grad_output = jnp.dot(mixed.T, grad_attn, preferred_element_type=f32)
    grad_mixed = jnp.dot(grad_attn, wo.T, preferred_element_type=f32).astype(bf16)
    f_y = 2 if F % 2 == 0 and F <= 8 else 4
    parts = [jnp.zeros((width,), f32)] * 2 + [
        grad_bias_output,
        grad_gain_one,
        grad_shift_one,
        grad_bias_out,
        grad_gain_two,
        grad_shift_two,
    ]
    table = jnp.stack(parts).reshape(8, F, vec).swapaxes(0, 1)
    extra = jnp.zeros((F, 16 - 8 - fan, vec), f32).at[:, 0, :5].set(squares)
    table = jnp.concatenate([table, grad_bias_in.reshape(F, fan, vec), extra], axis=1)
    by_rows = lambda t: t.astype(bf16).reshape(F // f_y, f_y, t.shape[0] // F, t.shape[1])
    input_grad, grad_qkv, grad_output, grad_in, grad_out, table = backward(
        S,
        F,
        grad_mixed,
        q,
        k,
        v,
        qt,
        kt,
        ot,
        lse,
        xfull,
        wqkv,
        grad_h,
        table.reshape(F // f_y, f_y, 16, vec),
        by_rows(grad_output),
        by_rows(grad_in),
        by_rows(grad_out),
    )
    wide = q.shape[1]
    grad_query, grad_key, grad_value = (
        t.astype(f32).swapaxes(0, 1).reshape(-1, width) for t in grad_qkv
    )
    weights = [t.astype(f32) for t in (grad_output, grad_in, grad_out)]
    small_grads = table
    grad_bias_in = table[8 : 8 + fan].reshape(-1)
    rms = jnp.sqrt(table[8 + fan, :5] / f32(rows * width * S * F))
    return (
        out.reshape(layer_input.shape),
        input_grad.reshape(layer_input.shape),
        grad_query,
        grad_key,
        grad_value,
        weights[0],
        small_grads[0],
        small_grads[1],
        small_grads[2],
        small_grads[3],
        small_grads[4],
        weights[1],
        grad_bias_in,
        weights[2],
        small_grads[5],
        small_grads[6],
        small_grads[7],
        rms,
    )


def solution(mesh):
    placed = (
        P("fsdp", "seq", None),
        P("fsdp", None),
        P("fsdp", None),
        P("fsdp", None),
        P("fsdp", None),
        P("fsdp"),
        P("fsdp"),
        P("fsdp"),
        P("fsdp"),
        P("fsdp"),
        P("fsdp", None),
        P("fsdp"),
        P("fsdp", None),
        P("fsdp"),
        P("fsdp"),
        P("fsdp"),
        P("fsdp", "seq", None),
    )
    return jax.shard_map(
        local,
        mesh=mesh,
        in_specs=placed,
        out_specs=(
            P("fsdp", "seq", None),
            P("fsdp", "seq", None),
            P("fsdp", None),
            P("fsdp", None),
            P("fsdp", None),
            P("fsdp", None),
            P("fsdp"),
            P("fsdp"),
            P("fsdp"),
            P("fsdp"),
            P("fsdp"),
            P("fsdp", None),
            P("fsdp"),
            P("fsdp", None),
            P("fsdp"),
            P("fsdp"),
            P("fsdp"),
            P(),
        ),
        check_vma=False,
    )
```

```python
import functools
import jax
import jax.numpy as jnp
from jax import lax
from jax.experimental import pallas as pl
from jax.experimental.pallas import tpu as pltpu
from jax.sharding import PartitionSpec as P

HD = 64
MESH = pl.DeviceIdType.MESH
bf16 = jnp.bfloat16
f32 = jnp.float32


def each(lo, hi, body):
    if hi - lo <= 8:
        for i in range(lo, hi):
            body(i)
    else:
        pl.loop(lo, hi)(body)


class Grid:
    def __init__(self, seq_count, fsdp_count):
        self.S, self.F = seq_count, fsdp_count
        self.H = seq_count // 2
        self.Y = 2 if fsdp_count % 2 == 0 and fsdp_count <= 8 else 4
        self.Z = fsdp_count // self.Y
        self.s = lax.axis_index("seq")
        self.f = lax.axis_index("fsdp")
        self.c = self.s % 2
        self.hi = self.s // 2
        self.z = self.f // self.Y
        self.y = self.f % self.Y

    def zp(self, k):
        return ((self.z + k) % self.Z) * self.Y + self.y

    def yp(self, j):
        return self.z * self.Y + (self.y + j) % self.Y

    def xp(self, m):
        return ((self.hi + m) % self.H) * 2 + self.c

    def sib(self):
        return self.hi * 2 + 1 - self.c

    def origin(self, r):
        j, k = r // self.Z, r % self.Z
        return ((self.z + self.Z - k) % self.Z) * self.Y + (self.y + self.Y - j) % self.Y

    def greet(self, barrier):
        count = 0
        for m in range(self.H):
            for flip in range(2):
                if m or flip:
                    to = ((self.hi + m) % self.H) * 2 + (self.c + flip) % 2
                    pl.semaphore_signal(barrier, inc=1, device_id=(to, self.f), device_id_type=MESH)
                    count += 1
        for k in range(1, self.Z):
            pl.semaphore_signal(barrier, inc=1, device_id=(self.s, self.zp(k)), device_id_type=MESH)
            count += 1
        for j in range(1, self.Y):
            pl.semaphore_signal(barrier, inc=1, device_id=(self.s, self.yp(j)), device_id_type=MESH)
            count += 1
        pl.semaphore_wait(barrier, count)


class Sems:
    def __init__(self):
        self.n = 0

    def take(self, n):
        at = self.n
        self.n += n
        return at


def rcopy(sems, src, dst, send, recv, to):
    return pltpu.make_async_remote_copy(
        src_ref=src,
        dst_ref=dst,
        send_sem=sems.at[send],
        recv_sem=sems.at[recv],
        device_id=to,
        device_id_type=MESH,
    )


class Gather:
    def __init__(self, alloc, S, F, Y, kind):
        self.kind = kind
        Z = F // Y
        self.zs = alloc.take(Z - 1) - 1
        self.ys = alloc.take((Y - 1) * Z)
        self.ir = alloc.take(F - 1) - 1
        if kind != "own":
            self.ss, self.sr = alloc.take(F - 1) - 1, alloc.take(F - 1) - 1
        if kind == "quarter":
            n = (S // 2 - 1) * F
            self.xs, self.xr = alloc.take(n), alloc.take(n)
            self.ts, self.tr = alloc.take(n), alloc.take(n)

    def bind(self, g, sems, piece, place):
        self.g, self.sems, self.piece, self.place = g, sems, piece, place

    def part(self, hi=None, c=None):
        g = self.g
        c = g.c if c is None else c
        hi = g.hi if hi is None else hi
        return {"own": g.s, "half": c, "quarter": hi * 2 + c}[self.kind]

    def start_z(self):
        g, p = self.g, self.part()
        src, dst = self.piece(p), self.place(g.f, p)
        for k in range(1, g.Z):
            rcopy(self.sems, src, dst, self.zs + k, self.ir + k, (g.s, g.zp(k))).start()

    def start_y(self):
        g, p = self.g, self.part()
        src, dst = self.piece(p), self.place(g.f, p)
        for j in range(1, g.Y):
            rcopy(self.sems, src, dst, self.ys + (j - 1) * g.Z, self.ir + j * g.Z, (g.s, g.yp(j))).start()

    def wait_in(self, r):
        ref = self.place(self.g.origin(r), self.part())
        rcopy(self.sems, ref, ref, self.ir + r, self.ir + r, (self.g.sib(), self.g.f)).wait_recv()

    def pass_on(self, r):
        g = self.g
        ref = self.place(g.origin(r), self.part())
        if self.kind == "quarter":
            for m in range(1, g.H):
                rcopy(self.sems, ref, ref, self.xs + (m - 1) * g.F + r, self.xr + (m - 1) * g.F + r, (g.xp(m), g.f)).start()
        if self.kind != "own":
            rcopy(self.sems, ref, ref, self.ss + r, self.sr + r, (g.sib(), g.f)).start()

    def on_z(self):
        g = self.g

        def body(k):
            self.wait_in(k)
            ref = self.place(g.origin(k), self.part())
            for j in range(1, g.Y):
                at = j * g.Z + k
                rcopy(self.sems, ref, ref, self.ys + at - g.Z, self.ir + at, (g.s, g.yp(j))).start()
            self.pass_on(k)

        each(1, g.Z, body)

    def on_y(self):
        def body(r):
            self.wait_in(r)
            self.pass_on(r)

        each(self.g.Z, self.g.F, body)

    def on_x(self):
        if self.kind != "quarter":
            return
        g = self.g
        for m in range(1, g.H):
            part = self.part(hi=(g.hi + g.H - m) % g.H)

            def body(r):
                ref = self.place(g.origin(r), part)
                at = (m - 1) * g.F + r
                rcopy(self.sems, ref, ref, self.xr + at, self.xr + at, (g.sib(), g.f)).wait_recv()
                rcopy(self.sems, ref, ref, self.ts + at, self.tr + at, (g.sib(), g.f)).start()

            each(1, g.F, body)

    def complete(self):
        g = self.g
        other = 1 - g.c

        def got(ref, at):
            rcopy(self.sems, ref, ref, at, at, (g.sib(), g.f)).wait_recv()

        if self.kind != "own":
            each(1, g.F, lambda r: got(self.place(g.origin(r), self.part(c=other)), self.sr + r))
        if self.kind == "quarter":
            for m in range(1, g.H):
                part = self.part(hi=(g.hi + g.H - m) % g.H, c=other)
                each(1, g.F, lambda r: got(self.place(g.origin(r), part), self.tr + (m - 1) * g.F + r))

    def drain(self):
        g = self.g

        def sent(ref, at):
            rcopy(self.sems, ref, ref, at, at, (g.sib(), g.f)).wait_send()

        mine = self.piece(self.part())
        for k in range(1, g.Z):
            sent(mine, self.zs + k)
        for j in range(1, g.Y):
            each(0, g.Z, lambda k: sent(mine, self.ys + (j - 1) * g.Z + k))
        if self.kind != "own":
            each(1, g.F, lambda r: sent(mine, self.ss + r))
        if self.kind == "quarter":
            for m in range(1, g.H):
                each(1, g.F, lambda r: sent(mine, self.xs + (m - 1) * g.F + r))
                each(1, g.F, lambda r: sent(mine, self.ts + (m - 1) * g.F + r))


def forward_kernel(plan, x, wq, wk, wv, small, wo, w1, w2, cot, *rest):
    (xfull, wqkv, q_o, k_o, v_o, qt_o, kt_o, ot_o, lse_o, mixed_o, wo_o, w1_o, w2_o) = rest[:13]
    (nlow_o, nhat_o, inv_o, hidden_o, slope_o, out_o, gs_o, sums_o, vecs_o) = rest[13:22]
    (xs, ws, sm, qn, kn, vn, qt, kt, vt, ot, lse, oblk, onat) = rest[22:35]
    (wo_f, w1_f, w2_f, mixed, spread, vecs, normed, nhat, inv, nlow, hidden, slope) = rest[35:47]
    (branch, cots, outs, gs, sums, sems) = rest[47:]
    S, F, rows, heads, wide, vec = plan.S, plan.F, plan.rows, plan.heads, plan.wide, plan.vec
    width, ff = w1_f.shape
    g = Grid(S, F)
    g.greet(pltpu.get_barrier_semaphore())
    part_rows = wq.shape[0]

    def keep(src, dst, at):
        copy = pltpu.make_async_copy(src, dst, sems.at[at])
        copy.start()
        return copy

    mine = xs.at[pl.ds(g.s * rows, rows)]
    x_out = [rcopy(sems, x, mine, plan.x_s, plan.x_r, (g.sib(), g.f))]
    for m in range(1, g.H):
        x_out.append(rcopy(sems, x, mine, plan.x_s + m, plan.x_r + m, (g.xp(m), g.f)))
    for copy in x_out[::-1]:
        copy.start()
    for item, src, col in ((plan.gq, wq, 0), (plan.gk, wk, 1), (plan.gv, wv, 2)):
        item.bind(
            g,
            sems,
            lambda p, src=src: src.at[:, pl.ds(p * wide, wide)],
            lambda o, p, col=col: ws.at[pl.ds(o * part_rows, part_rows), pl.ds(col * wide, wide)],
        )
    plan.gs.bind(g, sems, lambda p: small, lambda o, p: sm.at[pl.ds(o * 16, 16)])
    first = (plan.gs, plan.gq, plan.gk, plan.gv)
    for item in first:
        item.start_z()
        item.start_y()
    for dst, src, entries in ((wo_f, wo, plan.go), (w1_f, w1, plan.g1), (w2_f, w2, plan.g2)):
        n = src.shape[0]
        for item, lo, part in entries:
            item.bind(
                g,
                sems,
                lambda p, src=src, lo=lo, part=part: src.at[:, pl.ds(lo + p * part, part)],
                lambda o, p, dst=dst, n=n, lo=lo, part=part: dst.at[pl.ds(o * n, n), pl.ds(lo + p * part, part)],
            )
    entries = plan.g1[:3] + plan.go + plan.g1[3:] + plan.g2
    big = [e[0] for e in entries]
    for item in big[:1]:
        item.start_y()
    for item in big[: plan.ahead]:
        item.start_z()
    local = [keep(x, mine, plan.l), keep(small, sm.at[pl.ds(g.f * 16, 16)], plan.l + 1), keep(cot, cots, plan.l + 2)]
    for col, src in enumerate((wq, wk, wv)):
        local.append(
            keep(
                src.at[:, pl.ds(g.s * wide, wide)],
                ws.at[pl.ds(g.f * part_rows, part_rows), pl.ds(col * wide, wide)],
                plan.l + 3 + col,
            )
        )
    for i, (src, dst) in enumerate(((wo, wo_f), (w1, w1_f), (w2, w2_f))):
        n = src.shape[0]
        local.append(keep(src, dst.at[pl.ds(g.f * n, n)], plan.l + 6 + i))
    for item in first:
        item.on_z()
    x_pass = []
    for m in range(1, g.H):
        theirs = xs.at[pl.ds(((g.hi + g.H - m) % g.H * 2 + g.c) * rows, rows)]
        rcopy(sems, theirs, theirs, plan.x_s, plan.x_r + m, (g.sib(), g.f)).wait_recv()
        copy = rcopy(sems, theirs, theirs, plan.x_s + g.H + m, plan.x_r + g.H + m, (g.sib(), g.f))
        copy.start()
        x_pass.append(copy)
    for item in first:
        item.on_y()
    rcopy(sems, mine, mine, plan.x_s, plan.x_r, (g.sib(), g.f)).wait_recv()
    for m in range(1, g.H):
        rcopy(sems, mine, mine, plan.x_s, plan.x_r + g.H + m, (g.sib(), g.f)).wait_recv()
    for copy in local:
        copy.wait()

    lane = lax.broadcasted_iota(jnp.int32, (vec, width), 1)
    pick = (lane % vec == lax.broadcasted_iota(jnp.int32, (vec, width), 0)).astype(f32).astype(bf16)
    spread[...] = jnp.dot(sm[...], pick, preferred_element_type=f32)
    fan = ff // width

    @pl.loop(0, 8 + fan)
    def _(i):
        row = lax.broadcasted_iota(jnp.int32, spread.shape, 0)
        column = lax.broadcasted_iota(jnp.int32, spread.shape, 1)
        at = (i - 8) * width + column
        plain = (column // vec) * 16 + i
        want = jnp.where(i < 8, plain, (at // (fan * vec)) * 16 + 8 + (at // vec) % fan)
        vecs[pl.ds(i, 1), :] = jnp.sum(jnp.where(row == want, spread[...], 0.0), axis=0, keepdims=True)

    own = pl.ds(pl.multiple_of(g.s * wide, wide), wide)

    def queries(b):
        at = pl.multiple_of(b * rows, rows)
        prod = jnp.dot(xs[pl.ds(at, rows), :], ws[...], preferred_element_type=f32)
        q = (prod[:, :wide] + vecs[0:1, own]).astype(bf16).astype(f32) * 0.125
        k = prod[:, wide : 2 * wide]
        v = prod[:, 2 * wide :] + vecs[1:2, own]
        qn[pl.ds(at, rows), :] = q.astype(bf16)
        kn[pl.ds(at, rows), :] = k.astype(bf16)
        vn[pl.ds(at, rows), :] = v.astype(bf16)
        qt[:, pl.ds(at, rows)] = q.T.astype(bf16)
        kt[:, pl.ds(at, rows)] = k.T.astype(bf16)
        vt[:, pl.ds(at, rows)] = v.T.astype(bf16)

    stores = []
    head_of = lax.broadcasted_iota(jnp.int32, (wide, rows), 0) // HD
    sent = []

    def attend(t):
        hi = (g.hi + 1 + t // 2) % g.H
        c = (g.c + t + t // (2 * (g.H - 1))) % 2
        to = hi * 2 + c
        at = pl.multiple_of(to * rows, rows)

        @pl.loop(0, heads)
        def _(h):
            q = jnp.where(head_of == h, qt[:, pl.ds(at, rows)], jnp.zeros((), bf16))
            s = jnp.dot(kn[...], q, preferred_element_type=f32)
            m = jnp.max(s, axis=0, keepdims=True)
            e = jnp.exp(s - m)
            l = jnp.sum(e, axis=0, keepdims=True)
            band = pl.ds(pl.multiple_of(h * HD, HD), HD)
            o = jnp.dot(vt[band, :], e.astype(bf16), preferred_element_type=f32) / l
            oblk[band, :] = o
            lse[pl.ds(h, 1), pl.ds(at, rows)] = m + jnp.log(l)

        ot[:, pl.ds(at, rows)] = oblk[...].astype(bf16)
        onat[t] = oblk[...].T.astype(bf16)
        dst = mixed.at[:, pl.ds(g.s * wide, wide)]
        if t < S - 1:
            copy = rcopy(sems, onat.at[t], dst, plan.o_s + t, plan.o_r + g.s, (to, g.f))
            copy.start()
            sent.append(copy)
        else:
            mixed[:, own] = onat[t]
            stores.append(keep(ot, ot_o, plan.l + 16))
            stores.append(keep(lse, lse_o, plan.l + 17))

    def normalize(stream):
        centre = stream - jnp.mean(stream, axis=1, keepdims=True)
        scale = lax.rsqrt(jnp.mean(centre * centre, axis=1, keepdims=True) + 1e-05)
        return centre * scale, scale

    def count(row, value):
        sums[pl.ds(row, 1), :] += jnp.sum(value, axis=0, keepdims=True)

    chunk = 128 if rows % 128 == 0 else rows

    def project():
        for i in range(1, S):
            peer = (g.s + i) % S
            ref = mixed.at[:, pl.ds(peer * wide, wide)]
            rcopy(sems, ref, ref, plan.o_r + peer, plan.o_r + peer, (peer, g.f)).wait_recv()
        sums[...] = jnp.zeros_like(sums)

        @pl.loop(0, rows // chunk)
        def _(b):
            at = pl.ds(pl.multiple_of(b * chunk, chunk), chunk)
            tokens = xs[pl.ds(pl.multiple_of(g.s * rows + b * chunk, chunk), chunk), :].astype(f32)
            attn = jnp.dot(mixed[at, :], wo_f[...], preferred_element_type=f32) + vecs[2:3, :]
            count(3, tokens * tokens)
            count(4, attn * attn)
            unit, scale = normalize(tokens + attn)
            value = unit * vecs[3:4, :] + vecs[4:5, :]
            count(5, value * value)
            normed[at, :] = value
            nhat[at, :] = unit
            inv[at, :] = jnp.broadcast_to(scale, (chunk, inv.shape[1]))
            nlow[at, :] = value.astype(bf16)

        for i, (src, dst) in enumerate(
            ((mixed, mixed_o), (nhat, nhat_o), (inv, inv_o), (nlow, nlow_o), (wo_f, wo_o))
        ):
            stores.append(keep(src, dst, plan.l + 18 + i))

    def expand(b):
        part = width // 2

        @pl.loop(0, 2)
        def _(i):
            at = pl.ds(pl.multiple_of(b * width + i * part, part), part)
            bias = vecs[8 + b : 9 + b, pl.ds(pl.multiple_of(i * part, part), part)]
            pre = jnp.dot(nlow[...], w1_f[:, at], preferred_element_type=f32) + bias
            below = 0.5 * lax.erf(pre * 0.7071067811865476) + 0.5
            hidden[:, at] = (pre * below).astype(bf16)
            slope[:, at] = (below + pre * (jnp.exp(pre * pre * -0.5) * 0.3989422804014327)).astype(bf16)

    def contract(i):
        lo, part = entries[i][1:]
        n = part * (S if big[i].kind == "quarter" else 2)
        at = pl.ds(lo, n)
        branch[:, at] = jnp.dot(hidden[...], w2_f[:, at], preferred_element_type=f32) + vecs[5:6, at]
        stores.append(keep(w2_f.at[:, at], w2_o.at[:, at], plan.l + 31 + i))

    def close():
        @pl.loop(0, rows // chunk)
        def _(b):
            at = pl.ds(pl.multiple_of(b * chunk, chunk), chunk)
            value = branch[at, :]
            count(6, value * value)
            unit, scale = normalize(normed[at, :] + value)
            gain = vecs[6:7, :]
            value = unit * gain + vecs[7:8, :]
            count(7, value * value)
            outs[at, :] = value.astype(bf16)
            r = cots[at, :].astype(f32)
            count(0, r * unit)
            count(1, r)
            rg = r * gain
            grad = rg - jnp.mean(rg, axis=1, keepdims=True) - unit * jnp.mean(rg * unit, axis=1, keepdims=True)
            grad = grad * scale
            gs[at, :] = grad
            count(2, grad.astype(bf16).astype(f32))

        for i, (src, dst) in enumerate(((outs, out_o), (gs, gs_o), (sums, sums_o), (vecs, vecs_o))):
            stores.append(keep(src, dst, plan.l + 23 + i))

    turn = 0
    for op in plan.order:
        what, on = op[0], int(op[1:] or 0)
        if what == "P":
            pl.loop(0, S)(queries)
            for i, (src, dst) in enumerate(
                ((xs, xfull), (ws, wqkv), (qn, q_o), (kn, k_o), (vn, v_o), (qt, qt_o), (kt, kt_o))
            ):
                stores.append(keep(src, dst, plan.l + 9 + i))
        elif what == "T":
            attend(turn)
            turn += 1
        elif what in "zyxC":
            item = big[on]
            {"z": item.on_z, "y": item.on_y, "x": item.on_x, "C": item.complete}[what]()
            if what == "z" and 1 <= on + 1 < len(big):
                big[on + 1].start_y()
            if what == "z" and on + plan.ahead < len(big):
                big[on + plan.ahead].start_z()
        elif what == "O":
            project()
        elif what == "E":
            expand(on)
            if on == fan - 1:
                for i, (src, dst) in enumerate(((hidden, hidden_o), (slope, slope_o), (w1_f, w1_o))):
                    stores.append(keep(src, dst, plan.l + 28 + i))
        elif what == "B":
            contract(on)
        else:
            close()
    for item in (*first, *big):
        item.drain()
    for copy in sent + x_out + x_pass:
        copy.wait_send()
    for copy in stores:
        copy.wait()


class Plan:
    pass


def forward_plan(S, F, rows, width, ff):
    plan = Plan()
    alloc = Sems()
    plan.S, plan.F, plan.rows = S, F, rows
    plan.wide = width // S
    plan.heads = plan.wide // HD
    plan.vec = width // F
    Y = 2 if F % 2 == 0 and F <= 8 else 4
    plan.x_s, plan.x_r = alloc.take(S), alloc.take(S)
    plan.gq, plan.gk, plan.gv, plan.gs = (Gather(alloc, S, F, Y, "own") for _ in range(4))
    half = width // 2
    plan.go = [(Gather(alloc, S, F, Y, "half"), 0, half)]
    fan = ff // width
    kind, shares = ("quarter", S) if F <= 8 else ("half", 2)
    plan.g1 = [(Gather(alloc, S, F, Y, kind), i * width, width // shares) for i in range(fan)]
    plan.g2 = [(Gather(alloc, S, F, Y, "quarter"), 0, half // S)]
    plan.g2 += [(Gather(alloc, S, F, Y, "half"), half + i * half // 2, half // 4) for i in range(2)]
    plan.ahead = 2
    plan.order = (
        *("z0", "y0", "z1", "z2", "y1", "P", "z3", "T", "T", "x1", "z4", "x0", "T", "y3",),
        *("y2", "T", "y4", "C3", "z5", "O", "z6", "C0", "x2", "x4", "C1", "C2", "y5", "C4",),
        *("E0", "E1", "z7", "y6", "E2", "E3", "C6", "x5", "y7", "B6", "C5", "C7", "B7", "B5",),
        *("N",),
    )
    plan.o_s, plan.o_r = alloc.take(S), alloc.take(S)
    plan.l = alloc.take(40)
    plan.sems = alloc.n
    return plan


def forward(S, F, x, wq, wk, wv, small, wo, w1, w2, cot):
    rows, width = x.shape
    ff = w1.shape[1]
    plan = forward_plan(S, F, rows, width, ff)
    wide = plan.wide
    length = rows * S
    sds = jax.ShapeDtypeStruct
    any_ = pl.BlockSpec(memory_space=pl.ANY)
    vmem = pltpu.VMEM
    return pl.pallas_call(
        functools.partial(forward_kernel, plan),
        out_shape=(
            sds((length, width), bf16),
            sds((width, 3 * wide), bf16),
            sds((length, wide), bf16),
            sds((length, wide), bf16),
            sds((length, wide), bf16),
            sds((wide, length), bf16),
            sds((wide, length), bf16),
            sds((wide, length), bf16),
            sds((8, length), f32),
            sds((rows, width), bf16),
            sds((width, width), bf16),
            sds((width, ff), bf16),
            sds((ff, width), bf16),
            sds((rows, width), bf16),
            sds((rows, width), f32),
            sds((rows, 128), f32),
            sds((rows, ff), bf16),
            sds((rows, ff), bf16),
            sds((rows, width), bf16),
            sds((rows, width), f32),
            sds((8, width), f32),
            sds((16, width), f32),
        ),
        in_specs=[any_] * 9,
        out_specs=(any_,) * 22,
        scratch_shapes=[
            vmem((length, width), bf16),
            vmem((width, 3 * wide), bf16),
            vmem((F * 16, plan.vec), bf16),
            vmem((length, wide), bf16),
            vmem((length, wide), bf16),
            vmem((length, wide), bf16),
            vmem((wide, length), bf16),
            vmem((wide, length), bf16),
            vmem((wide, length), bf16),
            vmem((wide, length), bf16),
            vmem((8, length), f32),
            vmem((wide, rows), f32),
            vmem((S, rows, wide), bf16),
            vmem((width, width), bf16),
            vmem((width, ff), bf16),
            vmem((ff, width), bf16),
            vmem((rows, width), bf16),
            vmem((F * 16, width), f32),
            vmem((16, width), f32),
            vmem((rows, width), f32),
            vmem((rows, width), f32),
            vmem((rows, 128), f32),
            vmem((rows, width), bf16),
            vmem((rows, ff), bf16),
            vmem((rows, ff), bf16),
            vmem((rows, width), f32),
            vmem((rows, width), bf16),
            vmem((rows, width), bf16),
            vmem((rows, width), f32),
            vmem((8, width), f32),
            pltpu.SemaphoreType.DMA((plan.sems,)),
        ],
        compiler_params=pltpu.CompilerParams(collective_id=0, has_side_effects=True, vmem_limit_bytes=63 << 20),
        name="forward_with_weight_gather",
    )(x, wq, wk, wv, small, wo, w1, w2, cot)


class Reduce:
    def __init__(self, alloc, S, F, Y, R, C, kind):
        self.kind, self.R, self.C = kind, R, C
        self.S, self.F, self.Y, self.Z, self.H = S, F, Y, F // Y, S // 2
        Z, H = self.Z, self.H
        self.w = {"half": C // 2, "quarter": C // S, "own": C}[kind]
        w = self.w
        self.n = H if kind == "quarter" else 1
        self.shapes = [(self.n, Z, Y, R, w), (Y - 1, Z, R, w), (Z, R, w)]
        if kind == "own":
            self.shapes += [(S, R, w)]
        else:
            self.shapes += [(self.n, Z, Y, R, w), (R, C)]
            self.shapes += [(H - 1, Z, Y, R, w) if kind == "quarter" else (H - 1, R, w)]
        self.shapes = [pltpu.VMEM(s, bf16) for s in self.shapes]
        self.load = alloc.take(H)
        self.ds, self.dr = alloc.take(H), alloc.take(H)
        self.xs, self.xr = alloc.take(H), alloc.take(H)
        self.ys, self.yr = alloc.take(Y), alloc.take(Y)
        self.zs, self.zr = alloc.take(Z), alloc.take(Z)
        self.fs, self.fr = alloc.take(2 * H), alloc.take(2 * H)
        self.out = alloc.take(1)

    def bind(self, g, sems, refs, source, dest):
        self.g, self.sems, self.source, self.dest = g, sems, source, dest
        if self.kind == "own":
            self.own, self.ry, self.rz, self.fin = refs
        else:
            self.own, self.ry, self.rz, self.rd, self.fin, self.rx = refs
        self.sends = []

    def send(self, src, dst, s, r, to):
        copy = rcopy(self.sems, src, dst, s, r, to)
        copy.start()
        self.sends.append(copy)

    def recv(self, ref, r):
        rcopy(self.sems, ref, ref, r, r, (self.g.sib(), self.g.f)).wait_recv()

    def column(self, hi, c):
        return (hi * 2 + c) * self.w if self.kind == "quarter" else c * self.w

    def start(self):
        g = self.g
        self.loads = []
        for m in range(self.n):
            hi = (g.hi + m) % g.H
            self.send(
                self.source(self.column(hi, 1 - g.c), self.w),
                self.rd.at[m],
                self.ds + m,
                self.dr + m,
                (g.sib(), g.f),
            )
            copy = pltpu.make_async_copy(
                self.source(self.column(hi, g.c), self.w), self.own.at[m], self.sems.at[self.load + m]
            )
            copy.start()
            self.loads.append(copy)

    def add_all(self, m, other):
        @pl.loop(0, self.Z * self.Y)
        def _(i):
            a, b = i // self.Y, i % self.Y
            self.own[m, a, b] = (self.own[m, a, b].astype(f32) + other(a, b).astype(f32)).astype(bf16)

    def over_cores(self):
        for m in list(range(1, self.n)) + [0]:
            self.loads[m].wait()
            self.recv(self.rd.at[m], self.dr + m)
            self.add_all(m, lambda a, b: self.rd[m, a, b])
            if m:
                self.send(self.own.at[m], self.rx.at[m - 1], self.xs + m, self.xr + m, (self.g.xp(m), self.g.f))
        if self.kind == "half":
            self.send_y()

    def over_x_first(self):
        for m in range(1, self.H):
            self.recv(self.rx.at[m - 1], self.xr + m)
            self.add_all(0, lambda a, b: self.rx[m - 1, a, b])
        self.send_y()

    def send_y(self):
        g = self.g
        for j in range(1, g.Y):
            y = (g.y + j) % g.Y
            self.send(self.own.at[0, :, y], self.ry.at[j - 1], self.ys + j, self.yr + j, (g.s, g.yp(j)))

    def over_y(self):
        g = self.g
        for j in range(1, g.Y):
            self.recv(self.ry.at[j - 1], self.yr + j)

        @pl.loop(0, self.Z)
        def _(a):
            total = self.own[0, a, g.y].astype(f32)
            for j in range(1, g.Y):
                total += self.ry[j - 1, a].astype(f32)
            self.own[0, a, g.y] = total.astype(bf16)

        for k in range(1, g.Z):
            z = (g.z + k) % g.Z
            self.send(self.own.at[0, z, g.y], self.rz.at[k], self.zs + k, self.zr + k, (g.s, g.zp(k)))

    def over_z(self):
        g = self.g
        total = self.own[0, g.z, g.y].astype(f32)
        for k in range(1, g.Z):
            self.recv(self.rz.at[k], self.zr + k)
            total += self.rz[k].astype(f32)
        total = total.astype(bf16)
        if self.kind == "half":
            self.rz[0] = total
            for m in range(1, g.H):
                self.send(self.rz.at[0], self.rx.at[m - 1], self.xs + m, self.xr + m, (g.xp(m), g.f))
            return
        if self.kind == "own":
            self.fin[g.s] = total
            ref = self.fin.at[g.s]
        else:
            at = pl.multiple_of(self.column(g.hi, g.c), self.w)
            self.fin[:, pl.ds(at, self.w)] = total
            ref = self.fin.at[:, pl.ds(at, self.w)]
        for m in range(1, g.H):
            self.send(ref, ref, self.fs + m, self.fr + m, (g.xp(m), g.f))
        self.send(ref, ref, self.fs, self.fr, (g.sib(), g.f))

    def over_x_last(self):
        g = self.g
        if self.kind == "half":
            total = self.rz[0].astype(f32)
            for m in range(1, g.H):
                self.recv(self.rx.at[m - 1], self.xr + m)
                total += self.rx[m - 1].astype(f32)
            at = pl.multiple_of(g.c * self.w, self.w)
            self.fin[:, pl.ds(at, self.w)] = total.astype(bf16)
            ref = self.fin.at[:, pl.ds(at, self.w)]
            self.send(ref, ref, self.fs, self.fr, (g.sib(), g.f))
            return
        for m in range(1, g.H):
            hi = (g.hi + g.H - m) % g.H
            if self.kind == "own":
                ref = self.fin.at[hi * 2 + g.c]
            else:
                ref = self.fin.at[:, pl.ds(self.column(hi, g.c), self.w)]
            self.recv(ref, self.fr + m)
            self.send(ref, ref, self.fs + g.H + m, self.fr + g.H + m, (g.sib(), g.f))

    def finish(self):
        g = self.g
        for m in range(g.H if self.kind != "half" else 1):
            hi = (g.hi + g.H - m) % g.H
            if self.kind == "own":
                ref = self.fin.at[hi * 2 + 1 - g.c]
            else:
                ref = self.fin.at[:, pl.ds(self.column(hi, 1 - g.c), self.w)]
            self.recv(ref, self.fr + (g.H + m if m else 0))
        self.copy_out = pltpu.make_async_copy(self.fin, self.dest, self.sems.at[self.out])
        self.copy_out.start()

    def done(self):
        for copy in self.sends:
            copy.wait_send()
        self.copy_out.wait()

    def step(self, name):
        {
            "D": self.over_cores,
            "X": self.over_x_first if self.kind == "quarter" else self.over_x_last,
            "Y": self.over_y,
            "Z": self.over_z,
            "L": self.over_x_last,
            "F": self.finish,
        }[name]()


def backward_kernel(plan, g_o, q_i, k_i, v_i, qt_i, kt_i, ot_i, lse_i, x_i, w_i, gh, table_i, dwo, dw1, dw2, *rest):
    dx_o, dqkv_o, dwo_o, dw1_o, dw2_o, table_o = rest[:6]
    (go, qn, kn, vn, qt, kt, ot, lse, xs, ws, dk, dv, dqt, dt, delta, grads) = rest[6:22]
    (dx, dx_send, dx_core, dx_out, dx_x, tab, tab_core, tab_x, tab_y, tab_s, tab_z, sems) = rest[22:34]
    pools = rest[34:]
    S, F, rows, heads, wide, vec = plan.S, plan.F, plan.rows, plan.heads, plan.wide, plan.vec
    g = Grid(S, F)
    g.greet(pltpu.get_barrier_semaphore())

    def keep(src, dst, at):
        copy = pltpu.make_async_copy(src, dst, sems.at[at])
        copy.start()
        return copy

    sent = []

    def send(src, dst, s, r, to):
        copy = rcopy(sems, src, dst, s, r, to)
        copy.start()
        sent.append(copy)

    def recv(ref, r):
        rcopy(sems, ref, ref, r, r, (g.sib(), g.f)).wait_recv()

    for m in [*range(1, g.H), 0]:
        for flip in range(2):
            if m or flip:
                to = ((g.hi + m) % g.H) * 2 + (g.c + flip) % 2
                send(
                    g_o.at[:, pl.ds(to * wide, wide)],
                    go.at[g.s],
                    plan.o_s + m * 2 + flip,
                    plan.o_r + g.s,
                    (to, g.f),
                )
    used = 0
    for item, which, col, row in plan.items:
        n = len(item.shapes)
        src, dst = {"o": (dwo, dwo_o), "1": (dw1, dw1_o), "2": (dw2, dw2_o)}[which]
        item.bind(
            g,
            sems,
            pools[used : used + n],
            lambda lo, width, src=src, item=item, col=col, row=row: src.at[
                :, :, pl.ds(row, item.R), pl.ds(col + lo, width)
            ],
            dst.at[pl.ds(row, item.R), pl.ds(col, item.C)],
        )
        used += n
        item.start()
    for i, item in enumerate(plan.qkv):
        item.bind(g, sems, pools[used : used + 4], None, dqkv_o.at[i])
        used += 4
    loads = [
        keep(src, dst, plan.l + i)
        for i, (src, dst) in enumerate(
            (
                (g_o.at[:, pl.ds(g.s * wide, wide)], go.at[g.s]),
                (q_i, qn),
                (k_i, kn),
                (v_i, vn),
                (qt_i, qt),
                (kt_i, kt),
                (ot_i, ot),
                (lse_i, lse),
                (x_i, xs),
                (w_i, ws),
                (gh, dx),
                (table_i, tab),
            )
        )
    ]
    items = [entry[0] for entry in plan.items]
    dk[...] = jnp.zeros_like(dk)
    dv[...] = jnp.zeros_like(dv)
    for copy in loads:
        copy.wait()
    head_of = lax.broadcasted_iota(jnp.int32, (wide, rows), 0) // HD
    head_at = lax.broadcasted_iota(jnp.int32, (rows, wide), 1) // HD
    none = jnp.zeros((), bf16)

    def attend(t):
        if t == 0:
            for i in range(1, S):
                peer = (g.s + i) % S
                recv(go.at[peer], plan.o_r + peer)
        span = pl.ds(t * rows, rows)
        turned = go[t].astype(f32).T
        dt[...] = turned.astype(bf16)
        weighed = turned * ot[:, span].astype(f32)
        for h in range(heads):
            delta[pl.ds(h, 1), :] = jnp.sum(weighed[h * HD : (h + 1) * HD], axis=0, keepdims=True)

        @pl.loop(0, heads)
        def _(h):
            band = pl.ds(pl.multiple_of(h * HD, HD), HD)
            s = jnp.dot(kn[...], jnp.where(head_of == h, qt[:, span], none), preferred_element_type=f32)
            p = jnp.exp(s - lse[pl.ds(h, 1), span])
            dp = jnp.dot(vn[...], jnp.where(head_of == h, dt[...], none), preferred_element_type=f32)
            ds = (p * (dp - delta[pl.ds(h, 1), :])).astype(bf16)
            dv[...] += jnp.dot(p.astype(bf16), jnp.where(head_at == h, go[t], none), preferred_element_type=f32)
            dk[...] += jnp.dot(ds, jnp.where(head_at == h, qn[span, :], none), preferred_element_type=f32)
            dqt[band, span] = jnp.dot(kt[band, :], ds, preferred_element_type=f32) * 0.125

    totals = []

    def projections(i):
        if i == 0:
            sum_q = jnp.zeros((1, wide), f32)
            sum_v = jnp.zeros((1, wide), f32)
            for t in range(S):
                span = pl.ds(t * rows, rows)
                q = dqt[:, span].T.astype(bf16)
                v = dv[span, :].astype(bf16)
                grads[span, pl.ds(0, wide)] = q
                grads[span, pl.ds(wide, wide)] = dk[span, :].astype(bf16)
                grads[span, pl.ds(2 * wide, wide)] = v
                sum_q += jnp.sum(q.astype(f32), axis=0, keepdims=True)
                sum_v += jnp.sum(v.astype(f32), axis=0, keepdims=True)
            totals.extend((sum_q, sum_v))
        item = plan.qkv[i]
        part_rows, width = item.R, xs.shape[1]
        step = max(part_rows, 256)
        for lo in range(0, width, step):
            prod = lax.dot_general(
                xs[:, pl.ds(lo, step)],
                grads[:, pl.ds(i * wide, wide)],
                (((0,), (0,)), ((), ())),
                preferred_element_type=f32,
            ).astype(bf16)
            for j in range(step // part_rows):
                to = lo // part_rows + j
                item.own[0, to // g.Y, to % g.Y] = prod[j * part_rows : (j + 1) * part_rows]
        item.send_y()

    def part(to):
        return lax.dot_general(
            grads[pl.ds(pl.multiple_of(to * rows, rows), rows), :],
            ws[...],
            (((1,), (1,)), ((), ())),
            preferred_element_type=f32,
        )

    def input_parts():
        for m in [*range(1, g.H), 0]:
            hi = (g.hi + m) % g.H
            dx_send[m] = part(hi * 2 + 1 - g.c).astype(bf16)
            send(dx_send.at[m], dx_core.at[m], plan.dx + m, plan.dx + g.H + m, (g.sib(), g.f))
        for m in [*range(1, g.H), 0]:
            hi = (g.hi + m) % g.H
            value = part(hi * 2 + g.c)
            recv(dx_core.at[m], plan.dx + g.H + m)
            value += dx_core[m].astype(f32)
            if m:
                dx_out[m - 1] = value.astype(bf16)
                send(dx_out.at[m - 1], dx_x.at[m - 1], plan.dx + 2 * g.H + m, plan.dx + 3 * g.H + m, (g.xp(m), g.f))
            else:
                dx[...] += value

    out = []

    def input_done():
        for m in range(1, g.H):
            recv(dx_x.at[m - 1], plan.dx + 3 * g.H + m)
            dx[...] += dx_x[m - 1].astype(f32)
        out.append(keep(dx, dx_o, plan.l + 13))

    def vectors(stage):
        Y = g.Y
        if stage == 0:
            base = g.s * (wide // vec)
            for i in range(wide // vec):
                to = base + i
                for row, value in enumerate(totals):
                    tab[to // Y, to % Y, pl.ds(row, 1), :] = value[:, i * vec : (i + 1) * vec]
            send(tab, tab_core, plan.t, plan.t + 1, (g.sib(), g.f))
        if stage == 1:
            recv(tab_core, plan.t + 1)
            tab_x[g.hi] = tab[...] + tab_core[...]
            for m in range(1, g.H):
                send(tab_x.at[g.hi], tab_x.at[g.hi], plan.tx + m, plan.tx + g.H + g.hi, (g.xp(m), g.f))
        if stage == 2:
            for m in range(1, g.H):
                hi = (g.hi + m) % g.H
                recv(tab_x.at[hi], plan.tx + g.H + hi)
            total = tab_x[0]
            for m in range(1, g.H):
                total += tab_x[m]
            tab_core[...] = total
            tab_y[g.y] = tab_core[:, g.y]
            for j in range(1, Y):
                y = (g.y + j) % Y
                send(tab_core.at[:, y], tab_y.at[g.y], plan.ty + j, plan.ty + Y + g.y, (g.s, g.yp(j)))
        if stage == 3:
            for j in range(1, Y):
                y = (g.y + j) % Y
                recv(tab_y.at[y], plan.ty + Y + y)
            total = tab_y[0]
            for j in range(1, Y):
                total += tab_y[j]
            tab_s[...] = total
            tab_z[g.z] = tab_s[g.z]
            for k in range(1, g.Z):
                z = (g.z + k) % g.Z
                send(tab_s.at[z], tab_z.at[g.z], plan.tz + k, plan.tz + g.Z + g.z, (g.s, g.zp(k)))
        if stage == 4:
            for k in range(1, g.Z):
                z = (g.z + k) % g.Z
                recv(tab_z.at[z], plan.tz + g.Z + z)
            total = tab_z[0]
            for k in range(1, g.Z):
                total += tab_z[k]
            tab_y[0, 0] = total
            out.append(keep(tab_y.at[0, 0], table_o, plan.l + 12))

    named = {chr(ord("a") + i): item for i, item in enumerate(items)}
    named.update({"q%d" % i: item for i, item in enumerate(plan.qkv)})
    for op in plan.order:
        what, on = op[0], op[1:]
        if what == "T":
            attend(int(on))
        elif what == "G":
            projections(int(on))
        elif what == "I":
            input_parts()
        elif what == "J":
            input_done()
        elif what == "V":
            vectors(int(on))
        else:
            named[on].step(what)
    for item in (*items, *plan.qkv):
        item.done()
    for copy in sent:
        copy.wait_send()
    for copy in out:
        copy.wait()


def backward_plan(S, F, rows, width, ff):
    plan = Plan()
    alloc = Sems()
    plan.S, plan.F, plan.rows = S, F, rows
    plan.wide = width // S
    plan.heads = plan.wide // HD
    plan.vec = width // F
    Y = 2 if F % 2 == 0 and F <= 8 else 4
    R, R2 = width // F, ff // F
    ones = [(Reduce(alloc, S, F, Y, R, width, kind), "1", i * width, 0) for i, kind in enumerate(("quarter", "quarter", "quarter", "quarter"))]
    twos = [(Reduce(alloc, S, F, Y, R2 // 4, width, kind), "2", 0, i * (R2 // 4)) for i, kind in enumerate(("half", "half", "half", "quarter"))]
    plan.items = [e for pair in zip(ones, twos) for e in pair]
    plan.items.append((Reduce(alloc, S, F, Y, R, width, "half"), "o", 0, 0))
    plan.qkv = [Reduce(alloc, S, F, Y, R, plan.wide, "own") for _ in range(3)]
    plan.o_s, plan.o_r = alloc.take(S), alloc.take(S)
    plan.dx = alloc.take(4 * S)
    plan.t, plan.tx, plan.ty, plan.tz = alloc.take(2), alloc.take(S), alloc.take(2 * Y), alloc.take(2 * F // Y)
    plan.l = alloc.take(14)
    plan.order = (
        *("Da", "Db", "Dd", "T0", "Dc", "T1", "Yb", "Df", "Xa", "De", "T2", "Yd", "T3", "Xc",),
        *("Dg", "Zb", "G0", "Yf", "G1", "G2", "Xe", "I", "Ya", "Zd", "V0", "Yc", "V1", "Xg",),
        *("Yq0", "Zf", "Xb", "Fb", "Yq1", "Za", "Yq2", "Di", "Zc", "Dh", "Ye", "Zq0", "J", "Xd",),
        *("V2", "Fd", "Yg", "Zq1", "Xf", "La", "Ff", "Lc", "Fa", "Zq2", "Fc", "Yi", "Ze", "V3",),
        *("Xh", "Zg", "Lq0", "Lq1", "Fq0", "Lq2", "Fq1", "Le", "Fq2", "Lg", "Fe", "Yh", "Fg", "Zi",),
        *("V4", "Xi", "Zh", "Fi", "Lh", "Fh",),
    )
    plan.sems = alloc.n
    return plan


def backward(S, F, g_o, q, k, v, qt, kt, ot, lse, x, w, gh, table, dwo, dw1, dw2):
    rows, width = g_o.shape
    ff = dw1.shape[-1]
    plan = backward_plan(S, F, rows, width, ff)
    wide, vec = plan.wide, plan.vec
    length = rows * S
    Z, Y = table.shape[:2]
    H = S // 2
    R, R2 = width // F, ff // F
    sds = jax.ShapeDtypeStruct
    any_ = pl.BlockSpec(memory_space=pl.ANY)
    pools = [s for e in plan.items for s in e[0].shapes] + [s for i in plan.qkv for s in i.shapes]
    return pl.pallas_call(
        functools.partial(backward_kernel, plan),
        out_shape=(
            sds((rows, width), f32),
            sds((3, S, R, wide), bf16),
            sds((R, width), bf16),
            sds((R, ff), bf16),
            sds((R2, width), bf16),
            sds((16, vec), f32),
        ),
        in_specs=[any_] * 15,
        out_specs=(any_,) * 6,
        scratch_shapes=[
            pltpu.VMEM((S, rows, wide), bf16),
            pltpu.VMEM((length, wide), bf16),
            pltpu.VMEM((length, wide), bf16),
            pltpu.VMEM((length, wide), bf16),
            pltpu.VMEM((wide, length), bf16),
            pltpu.VMEM((wide, length), bf16),
            pltpu.VMEM((wide, length), bf16),
            pltpu.VMEM((8, length), f32),
            pltpu.VMEM((length, width), bf16),
            pltpu.VMEM((width, 3 * wide), bf16),
            pltpu.VMEM((length, wide), f32),
            pltpu.VMEM((length, wide), f32),
            pltpu.VMEM((wide, length), f32),
            pltpu.VMEM((wide, rows), bf16),
            pltpu.VMEM((8, rows), f32),
            pltpu.VMEM((length, 3 * wide), bf16),
            pltpu.VMEM((rows, width), f32),
            pltpu.VMEM((H, rows, width), bf16),
            pltpu.VMEM((H, rows, width), bf16),
            pltpu.VMEM((H - 1, rows, width), bf16),
            pltpu.VMEM((H - 1, rows, width), bf16),
            pltpu.VMEM((Z, Y, 16, vec), f32),
            pltpu.VMEM((Z, Y, 16, vec), f32),
            pltpu.VMEM((H, Z, Y, 16, vec), f32),
            pltpu.VMEM((Y, Z, 16, vec), f32),
            pltpu.VMEM((Z, 16, vec), f32),
            pltpu.VMEM((Z, 16, vec), f32),
            pltpu.SemaphoreType.DMA((plan.sems,)),
            *pools,
        ],
        compiler_params=pltpu.CompilerParams(collective_id=1, has_side_effects=True, vmem_limit_bytes=63 << 20),
        name="attention_backward_and_gradient_sums",
    )(g_o, q, k, v, qt, kt, ot, lse, x, w, gh, table, dwo, dw1, dw2)


def layer_norm(stream, gain, shift):
    centre = stream - jnp.mean(stream, axis=-1, keepdims=True)
    variance = jnp.mean(centre * centre, axis=-1, keepdims=True)
    return centre * lax.rsqrt(variance + 1e-05) * gain + shift


def gelu_exact(inputs):
    return jax.nn.gelu(inputs, approximate=False)


def column_sums(matrix):
    return jnp.sum(matrix.astype(f32), axis=0)


def local(
    layer_input,
    query_weight,
    key_weight,
    value_weight,
    output_weight,
    query_bias,
    value_bias,
    output_bias,
    attn_gain,
    attn_shift,
    in_weight,
    in_bias,
    out_weight,
    out_bias,
    out_gain,
    out_shift,
    out_cotangent,
):
    F = lax.axis_size("fsdp")
    S = lax.axis_size("seq")
    width = layer_input.shape[-1]
    tokens = layer_input.reshape(-1, width)
    rows = tokens.shape[0]
    vec = query_bias.shape[0]
    held = (query_bias, value_bias, output_bias, attn_gain, attn_shift, out_bias, out_gain, out_shift)
    fan = in_bias.shape[0] // vec
    small = jnp.concatenate(
        [v.reshape(1, vec) for v in held]
        + [in_bias.reshape(fan, vec), jnp.zeros((16 - len(held) - fan, vec), bf16)]
    )
    (xfull, wqkv, q, k, v, qt, kt, ot, lse, mixed, wo, w1, w2, nlow, nhat, inv, hidden, slope, out, grad_stream, sums, vectors) = (
        forward(
            S,
            F,
            tokens,
            query_weight,
            key_weight,
            value_weight,
            small,
            output_weight,
            in_weight,
            out_weight,
            out_cotangent.reshape(rows, width),
        )
    )
    gain_one = vectors[3]
    grad_gain_two, grad_shift_two, grad_bias_out = sums[0], sums[1], sums[2]
    squares = jnp.sum(sums[3:8], axis=1)
    inv = inv[:, :1]
    grad_branch = grad_stream.astype(bf16)
    grad_out = jnp.dot(hidden.T, grad_branch, preferred_element_type=f32)
    grad_hidden = jnp.dot(grad_branch, w2.T, preferred_element_type=f32)
    grad_pre = (grad_hidden * slope.astype(f32)).astype(bf16)
    grad_bias_in = column_sums(grad_pre)
    grad_in = jnp.dot(nlow.T, grad_pre, preferred_element_type=f32)
    grad_normed = grad_stream + jnp.dot(grad_pre, w1.T, preferred_element_type=f32)
    grad_gain_one = jnp.sum(grad_normed * nhat, axis=0)
    grad_shift_one = jnp.sum(grad_normed, axis=0)
    weighed = grad_normed * gain_one
    grad_h = inv * (
        weighed
        - jnp.mean(weighed, axis=1, keepdims=True)
        - nhat * jnp.mean(weighed * nhat, axis=1, keepdims=True)
    )
    grad_attn = grad_h.astype(bf16)
    grad_bias_output = column_sums(grad_attn)
    grad_output = jnp.dot(mixed.T, grad_attn, preferred_element_type=f32)
    grad_mixed = jnp.dot(grad_attn, wo.T, preferred_element_type=f32).astype(bf16)
    f_y = 2 if F % 2 == 0 and F <= 8 else 4
    parts = [jnp.zeros((width,), f32)] * 2 + [
        grad_bias_output,
        grad_gain_one,
        grad_shift_one,
        grad_bias_out,
        grad_gain_two,
        grad_shift_two,
    ]
    table = jnp.stack(parts).reshape(8, F, vec).swapaxes(0, 1)
    extra = jnp.zeros((F, 16 - 8 - fan, vec), f32).at[:, 0, :5].set(squares)
    table = jnp.concatenate([table, grad_bias_in.reshape(F, fan, vec), extra], axis=1)
    by_rows = lambda t: t.astype(bf16).reshape(F // f_y, f_y, t.shape[0] // F, t.shape[1])
    input_grad, grad_qkv, grad_output, grad_in, grad_out, table = backward(
        S,
        F,
        grad_mixed,
        q,
        k,
        v,
        qt,
        kt,
        ot,
        lse,
        xfull,
        wqkv,
        grad_h,
        table.reshape(F // f_y, f_y, 16, vec),
        by_rows(grad_output),
        by_rows(grad_in),
        by_rows(grad_out),
    )
    wide = q.shape[1]
    grad_query, grad_key, grad_value = (
        t.astype(f32).swapaxes(0, 1).reshape(-1, width) for t in grad_qkv
    )
    weights = [t.astype(f32) for t in (grad_output, grad_in, grad_out)]
    small_grads = table
    grad_bias_in = table[8 : 8 + fan].reshape(-1)
    rms = jnp.sqrt(table[8 + fan, :5] / f32(rows * width * S * F))
    return (
        out.reshape(layer_input.shape),
        input_grad.reshape(layer_input.shape),
        grad_query,
        grad_key,
        grad_value,
        weights[0],
        small_grads[0],
        small_grads[1],
        small_grads[2],
        small_grads[3],
        small_grads[4],
        weights[1],
        grad_bias_in,
        weights[2],
        small_grads[5],
        small_grads[6],
        small_grads[7],
        rms,
    )


def solution(mesh):
    placed = (
        P("fsdp", "seq", None),
        P("fsdp", None),
        P("fsdp", None),
        P("fsdp", None),
        P("fsdp", None),
        P("fsdp"),
        P("fsdp"),
        P("fsdp"),
        P("fsdp"),
        P("fsdp"),
        P("fsdp", None),
        P("fsdp"),
        P("fsdp", None),
        P("fsdp"),
        P("fsdp"),
        P("fsdp"),
        P("fsdp", "seq", None),
    )
    return jax.shard_map(
        local,
        mesh=mesh,
        in_specs=placed,
        out_specs=(
            P("fsdp", "seq", None),
            P("fsdp", "seq", None),
            P("fsdp", None),
            P("fsdp", None),
            P("fsdp", None),
            P("fsdp", None),
            P("fsdp"),
            P("fsdp"),
            P("fsdp"),
            P("fsdp"),
            P("fsdp"),
            P("fsdp", None),
            P("fsdp"),
            P("fsdp", None),
            P("fsdp"),
            P("fsdp"),
            P("fsdp"),
            P(),
        ),
        check_vma=False,
    )
```

```python
import functools
import jax
import jax.numpy as jnp
from jax import lax
from jax.experimental import pallas as pl
from jax.experimental.pallas import tpu as pltpu
from jax.sharding import PartitionSpec as P

HD = 64
MESH = pl.DeviceIdType.MESH
bf16 = jnp.bfloat16
f32 = jnp.float32


def each(lo, hi, body):
    if hi - lo <= 8:
        for i in range(lo, hi):
            body(i)
    else:
        pl.loop(lo, hi)(body)


class Grid:
    def __init__(self, seq_count, fsdp_count):
        self.S, self.F = seq_count, fsdp_count
        self.H = seq_count // 2
        self.Y = 2 if fsdp_count % 2 == 0 and fsdp_count <= 8 else 4
        self.Z = fsdp_count // self.Y
        self.s = lax.axis_index("seq")
        self.f = lax.axis_index("fsdp")
        self.c = self.s % 2
        self.hi = self.s // 2
        self.z = self.f // self.Y
        self.y = self.f % self.Y

    def zp(self, k):
        return ((self.z + k) % self.Z) * self.Y + self.y

    def yp(self, j):
        return self.z * self.Y + (self.y + j) % self.Y

    def xp(self, m):
        return ((self.hi + m) % self.H) * 2 + self.c

    def sib(self):
        return self.hi * 2 + 1 - self.c

    def origin(self, r):
        j, k = r // self.Z, r % self.Z
        return ((self.z + self.Z - k) % self.Z) * self.Y + (self.y + self.Y - j) % self.Y

    def greet(self, barrier):
        count = 0
        for m in range(self.H):
            for flip in range(2):
                if m or flip:
                    to = ((self.hi + m) % self.H) * 2 + (self.c + flip) % 2
                    pl.semaphore_signal(barrier, inc=1, device_id=(to, self.f), device_id_type=MESH)
                    count += 1
        for k in range(1, self.Z):
            pl.semaphore_signal(barrier, inc=1, device_id=(self.s, self.zp(k)), device_id_type=MESH)
            count += 1
        for j in range(1, self.Y):
            pl.semaphore_signal(barrier, inc=1, device_id=(self.s, self.yp(j)), device_id_type=MESH)
            count += 1
        pl.semaphore_wait(barrier, count)


class Sems:
    def __init__(self):
        self.n = 0

    def take(self, n):
        at = self.n
        self.n += n
        return at


def rcopy(sems, src, dst, send, recv, to):
    return pltpu.make_async_remote_copy(
        src_ref=src,
        dst_ref=dst,
        send_sem=sems.at[send],
        recv_sem=sems.at[recv],
        device_id=to,
        device_id_type=MESH,
    )


class Gather:
    def __init__(self, alloc, S, F, Y, kind):
        self.kind = kind
        Z = F // Y
        self.zs = alloc.take(Z - 1) - 1
        self.ys = alloc.take((Y - 1) * Z)
        self.ir = alloc.take(F - 1) - 1
        if kind != "own":
            self.ss, self.sr = alloc.take(F - 1) - 1, alloc.take(F - 1) - 1
        if kind == "quarter":
            n = (S // 2 - 1) * F
            self.xs, self.xr = alloc.take(n), alloc.take(n)
            self.ts, self.tr = alloc.take(n), alloc.take(n)

    def bind(self, g, sems, piece, place):
        self.g, self.sems, self.piece, self.place = g, sems, piece, place

    def part(self, hi=None, c=None):
        g = self.g
        c = g.c if c is None else c
        hi = g.hi if hi is None else hi
        return {"own": g.s, "half": c, "quarter": hi * 2 + c}[self.kind]

    def start_z(self):
        g, p = self.g, self.part()
        src, dst = self.piece(p), self.place(g.f, p)
        for k in range(1, g.Z):
            rcopy(self.sems, src, dst, self.zs + k, self.ir + k, (g.s, g.zp(k))).start()

    def start_y(self):
        g, p = self.g, self.part()
        src, dst = self.piece(p), self.place(g.f, p)
        for j in range(1, g.Y):
            rcopy(self.sems, src, dst, self.ys + (j - 1) * g.Z, self.ir + j * g.Z, (g.s, g.yp(j))).start()

    def wait_in(self, r):
        ref = self.place(self.g.origin(r), self.part())
        rcopy(self.sems, ref, ref, self.ir + r, self.ir + r, (self.g.sib(), self.g.f)).wait_recv()

    def pass_on(self, r):
        g = self.g
        ref = self.place(g.origin(r), self.part())
        if self.kind == "quarter":
            for m in range(1, g.H):
                rcopy(self.sems, ref, ref, self.xs + (m - 1) * g.F + r, self.xr + (m - 1) * g.F + r, (g.xp(m), g.f)).start()
        if self.kind != "own":
            rcopy(self.sems, ref, ref, self.ss + r, self.sr + r, (g.sib(), g.f)).start()

    def on_z(self):
        g = self.g

        def body(k):
            self.wait_in(k)
            ref = self.place(g.origin(k), self.part())
            for j in range(1, g.Y):
                at = j * g.Z + k
                rcopy(self.sems, ref, ref, self.ys + at - g.Z, self.ir + at, (g.s, g.yp(j))).start()
            self.pass_on(k)

        each(1, g.Z, body)

    def on_y(self):
        def body(r):
            self.wait_in(r)
            self.pass_on(r)

        each(self.g.Z, self.g.F, body)

    def on_x(self):
        if self.kind != "quarter":
            return
        g = self.g
        for m in range(1, g.H):
            part = self.part(hi=(g.hi + g.H - m) % g.H)

            def body(r):
                ref = self.place(g.origin(r), part)
                at = (m - 1) * g.F + r
                rcopy(self.sems, ref, ref, self.xr + at, self.xr + at, (g.sib(), g.f)).wait_recv()
                rcopy(self.sems, ref, ref, self.ts + at, self.tr + at, (g.sib(), g.f)).start()

            each(1, g.F, body)

    def complete(self):
        g = self.g
        other = 1 - g.c

        def got(ref, at):
            rcopy(self.sems, ref, ref, at, at, (g.sib(), g.f)).wait_recv()

        if self.kind != "own":
            each(1, g.F, lambda r: got(self.place(g.origin(r), self.part(c=other)), self.sr + r))
        if self.kind == "quarter":
            for m in range(1, g.H):
                part = self.part(hi=(g.hi + g.H - m) % g.H, c=other)
                each(1, g.F, lambda r: got(self.place(g.origin(r), part), self.tr + (m - 1) * g.F + r))

    def drain(self):
        g = self.g

        def sent(ref, at):
            rcopy(self.sems, ref, ref, at, at, (g.sib(), g.f)).wait_send()

        mine = self.piece(self.part())
        for k in range(1, g.Z):
            sent(mine, self.zs + k)
        for j in range(1, g.Y):
            each(0, g.Z, lambda k: sent(mine, self.ys + (j - 1) * g.Z + k))
        if self.kind != "own":
            each(1, g.F, lambda r: sent(mine, self.ss + r))
        if self.kind == "quarter":
            for m in range(1, g.H):
                each(1, g.F, lambda r: sent(mine, self.xs + (m - 1) * g.F + r))
                each(1, g.F, lambda r: sent(mine, self.ts + (m - 1) * g.F + r))


def forward_kernel(plan, x, wq, wk, wv, small, wo, w1, w2, cot, *rest):
    (xfull, wqkv, q_o, k_o, v_o, qt_o, kt_o, ot_o, lse_o, mixed_o, wo_o, w1_o, w2_o) = rest[:13]
    (nlow_o, nhat_o, inv_o, hidden_o, slope_o, out_o, gs_o, sums_o, vecs_o) = rest[13:22]
    (xs, ws, sm, qn, kn, vn, qt, kt, vt, ot, lse, oblk, onat) = rest[22:35]
    (wo_f, w1_f, w2_f, mixed, spread, vecs, normed, nhat, inv, nlow, hidden, slope) = rest[35:47]
    (branch, cots, outs, gs, sums, sems) = rest[47:]
    S, F, rows, heads, wide, vec = plan.S, plan.F, plan.rows, plan.heads, plan.wide, plan.vec
    width, ff = w1_f.shape
    g = Grid(S, F)
    g.greet(pltpu.get_barrier_semaphore())
    part_rows = wq.shape[0]

    def keep(src, dst, at):
        copy = pltpu.make_async_copy(src, dst, sems.at[at])
        copy.start()
        return copy

    mine = xs.at[pl.ds(g.s * rows, rows)]
    x_out = [rcopy(sems, x, mine, plan.x_s, plan.x_r, (g.sib(), g.f))]
    for m in range(1, g.H):
        x_out.append(rcopy(sems, x, mine, plan.x_s + m, plan.x_r + m, (g.xp(m), g.f)))
    for copy in x_out[::-1]:
        copy.start()
    for item, src, col in ((plan.gq, wq, 0), (plan.gk, wk, 1), (plan.gv, wv, 2)):
        item.bind(
            g,
            sems,
            lambda p, src=src: src.at[:, pl.ds(p * wide, wide)],
            lambda o, p, col=col: ws.at[pl.ds(o * part_rows, part_rows), pl.ds(col * wide, wide)],
        )
    plan.gs.bind(g, sems, lambda p: small, lambda o, p: sm.at[pl.ds(o * 16, 16)])
    first = (plan.gs, plan.gq, plan.gk, plan.gv)
    for item in first:
        item.start_z()
        item.start_y()
    for dst, src, entries in ((wo_f, wo, plan.go), (w1_f, w1, plan.g1), (w2_f, w2, plan.g2)):
        n = src.shape[0]
        for item, lo, part in entries:
            item.bind(
                g,
                sems,
                lambda p, src=src, lo=lo, part=part: src.at[:, pl.ds(lo + p * part, part)],
                lambda o, p, dst=dst, n=n, lo=lo, part=part: dst.at[pl.ds(o * n, n), pl.ds(lo + p * part, part)],
            )
    entries = plan.g1[:3] + plan.go + plan.g1[3:] + plan.g2
    big = [e[0] for e in entries]
    for item in big[:1]:
        item.start_y()
    for item in big[: plan.ahead]:
        item.start_z()
    local = [keep(x, mine, plan.l), keep(small, sm.at[pl.ds(g.f * 16, 16)], plan.l + 1), keep(cot, cots, plan.l + 2)]
    for col, src in enumerate((wq, wk, wv)):
        local.append(
            keep(
                src.at[:, pl.ds(g.s * wide, wide)],
                ws.at[pl.ds(g.f * part_rows, part_rows), pl.ds(col * wide, wide)],
                plan.l + 3 + col,
            )
        )
    for i, (src, dst) in enumerate(((wo, wo_f), (w1, w1_f), (w2, w2_f))):
        n = src.shape[0]
        local.append(keep(src, dst.at[pl.ds(g.f * n, n)], plan.l + 6 + i))
    for item in first:
        item.on_z()
    x_pass = []
    for m in range(1, g.H):
        theirs = xs.at[pl.ds(((g.hi + g.H - m) % g.H * 2 + g.c) * rows, rows)]
        rcopy(sems, theirs, theirs, plan.x_s, plan.x_r + m, (g.sib(), g.f)).wait_recv()
        copy = rcopy(sems, theirs, theirs, plan.x_s + g.H + m, plan.x_r + g.H + m, (g.sib(), g.f))
        copy.start()
        x_pass.append(copy)
    for item in first:
        item.on_y()
    rcopy(sems, mine, mine, plan.x_s, plan.x_r, (g.sib(), g.f)).wait_recv()
    for m in range(1, g.H):
        rcopy(sems, mine, mine, plan.x_s, plan.x_r + g.H + m, (g.sib(), g.f)).wait_recv()
    for copy in local:
        copy.wait()

    lane = lax.broadcasted_iota(jnp.int32, (vec, width), 1)
    pick = (lane % vec == lax.broadcasted_iota(jnp.int32, (vec, width), 0)).astype(f32).astype(bf16)
    spread[...] = jnp.dot(sm[...], pick, preferred_element_type=f32)
    fan = ff // width

    @pl.loop(0, 8 + fan)
    def _(i):
        row = lax.broadcasted_iota(jnp.int32, spread.shape, 0)
        column = lax.broadcasted_iota(jnp.int32, spread.shape, 1)
        at = (i - 8) * width + column
        plain = (column // vec) * 16 + i
        want = jnp.where(i < 8, plain, (at // (fan * vec)) * 16 + 8 + (at // vec) % fan)
        vecs[pl.ds(i, 1), :] = jnp.sum(jnp.where(row == want, spread[...], 0.0), axis=0, keepdims=True)

    own = pl.ds(pl.multiple_of(g.s * wide, wide), wide)

    def queries(b):
        at = pl.multiple_of(b * rows, rows)
        prod = jnp.dot(xs[pl.ds(at, rows), :], ws[...], preferred_element_type=f32)
        q = (prod[:, :wide] + vecs[0:1, own]).astype(bf16).astype(f32) * 0.125
        k = prod[:, wide : 2 * wide]
        v = prod[:, 2 * wide :] + vecs[1:2, own]
        qn[pl.ds(at, rows), :] = q.astype(bf16)
        kn[pl.ds(at, rows), :] = k.astype(bf16)
        vn[pl.ds(at, rows), :] = v.astype(bf16)
        qt[:, pl.ds(at, rows)] = q.T.astype(bf16)
        kt[:, pl.ds(at, rows)] = k.T.astype(bf16)
        vt[:, pl.ds(at, rows)] = v.T.astype(bf16)

    stores = []
    head_of = lax.broadcasted_iota(jnp.int32, (wide, rows), 0) // HD
    sent = []

    def attend(t):
        hi = (g.hi + 1 + t // 2) % g.H
        c = (g.c + t + t // (2 * (g.H - 1))) % 2
        to = hi * 2 + c
        at = pl.multiple_of(to * rows, rows)

        @pl.loop(0, heads)
        def _(h):
            q = jnp.where(head_of == h, qt[:, pl.ds(at, rows)], jnp.zeros((), bf16))
            s = jnp.dot(kn[...], q, preferred_element_type=f32)
            m = jnp.max(s, axis=0, keepdims=True)
            e = jnp.exp(s - m)
            l = jnp.sum(e, axis=0, keepdims=True)
            band = pl.ds(pl.multiple_of(h * HD, HD), HD)
            o = jnp.dot(vt[band, :], e.astype(bf16), preferred_element_type=f32) / l
            oblk[band, :] = o
            lse[pl.ds(h, 1), pl.ds(at, rows)] = m + jnp.log(l)

        ot[:, pl.ds(at, rows)] = oblk[...].astype(bf16)
        onat[t] = oblk[...].T.astype(bf16)
        dst = mixed.at[:, pl.ds(g.s * wide, wide)]
        if t < S - 1:
            copy = rcopy(sems, onat.at[t], dst, plan.o_s + t, plan.o_r + g.s, (to, g.f))
            copy.start()
            sent.append(copy)
        else:
            mixed[:, own] = onat[t]
            stores.append(keep(ot, ot_o, plan.l + 16))
            stores.append(keep(lse, lse_o, plan.l + 17))

    def normalize(stream):
        centre = stream - jnp.mean(stream, axis=1, keepdims=True)
        scale = lax.rsqrt(jnp.mean(centre * centre, axis=1, keepdims=True) + 1e-05)
        return centre * scale, scale

    def count(row, value):
        sums[pl.ds(row, 1), :] += jnp.sum(value, axis=0, keepdims=True)

    chunk = 128 if rows % 128 == 0 else rows

    def project():
        for i in range(1, S):
            peer = (g.s + i) % S
            ref = mixed.at[:, pl.ds(peer * wide, wide)]
            rcopy(sems, ref, ref, plan.o_r + peer, plan.o_r + peer, (peer, g.f)).wait_recv()
        sums[...] = jnp.zeros_like(sums)

        @pl.loop(0, rows // chunk)
        def _(b):
            at = pl.ds(pl.multiple_of(b * chunk, chunk), chunk)
            tokens = xs[pl.ds(pl.multiple_of(g.s * rows + b * chunk, chunk), chunk), :].astype(f32)
            attn = jnp.dot(mixed[at, :], wo_f[...], preferred_element_type=f32) + vecs[2:3, :]
            count(3, tokens * tokens)
            count(4, attn * attn)
            unit, scale = normalize(tokens + attn)
            value = unit * vecs[3:4, :] + vecs[4:5, :]
            count(5, value * value)
            normed[at, :] = value
            nhat[at, :] = unit
            inv[at, :] = jnp.broadcast_to(scale, (chunk, inv.shape[1]))
            nlow[at, :] = value.astype(bf16)

        for i, (src, dst) in enumerate(
            ((mixed, mixed_o), (nhat, nhat_o), (inv, inv_o), (nlow, nlow_o), (wo_f, wo_o))
        ):
            stores.append(keep(src, dst, plan.l + 18 + i))

    def expand(b):
        part = width // 2

        @pl.loop(0, 2)
        def _(i):
            at = pl.ds(pl.multiple_of(b * width + i * part, part), part)
            bias = vecs[8 + b : 9 + b, pl.ds(pl.multiple_of(i * part, part), part)]
            pre = jnp.dot(nlow[...], w1_f[:, at], preferred_element_type=f32) + bias
            below = 0.5 * lax.erf(pre * 0.7071067811865476) + 0.5
            hidden[:, at] = (pre * below).astype(bf16)
            slope[:, at] = (below + pre * (jnp.exp(pre * pre * -0.5) * 0.3989422804014327)).astype(bf16)

    def contract(i):
        lo, part = entries[i][1:]
        n = part * (S if big[i].kind == "quarter" else 2)
        at = pl.ds(lo, n)
        branch[:, at] = jnp.dot(hidden[...], w2_f[:, at], preferred_element_type=f32) + vecs[5:6, at]
        stores.append(keep(w2_f.at[:, at], w2_o.at[:, at], plan.l + 31 + i))

    def close():
        @pl.loop(0, rows // chunk)
        def _(b):
            at = pl.ds(pl.multiple_of(b * chunk, chunk), chunk)
            value = branch[at, :]
            count(6, value * value)
            unit, scale = normalize(normed[at, :] + value)
            gain = vecs[6:7, :]
            value = unit * gain + vecs[7:8, :]
            count(7, value * value)
            outs[at, :] = value.astype(bf16)
            r = cots[at, :].astype(f32)
            count(0, r * unit)
            count(1, r)
            rg = r * gain
            grad = rg - jnp.mean(rg, axis=1, keepdims=True) - unit * jnp.mean(rg * unit, axis=1, keepdims=True)
            grad = grad * scale
            gs[at, :] = grad
            count(2, grad.astype(bf16).astype(f32))

        for i, (src, dst) in enumerate(((outs, out_o), (gs, gs_o), (sums, sums_o), (vecs, vecs_o))):
            stores.append(keep(src, dst, plan.l + 23 + i))

    turn = 0
    for op in plan.order:
        what, on = op[0], int(op[1:] or 0)
        if what == "P":
            pl.loop(0, S)(queries)
            for i, (src, dst) in enumerate(
                ((xs, xfull), (ws, wqkv), (qn, q_o), (kn, k_o), (vn, v_o), (qt, qt_o), (kt, kt_o))
            ):
                stores.append(keep(src, dst, plan.l + 9 + i))
        elif what == "T":
            attend(turn)
            turn += 1
        elif what in "zyxC":
            item = big[on]
            {"z": item.on_z, "y": item.on_y, "x": item.on_x, "C": item.complete}[what]()
            if what == "z" and 1 <= on + 1 < len(big):
                big[on + 1].start_y()
            if what == "z" and on + plan.ahead < len(big):
                big[on + plan.ahead].start_z()
        elif what == "O":
            project()
        elif what == "E":
            expand(on)
            if on == fan - 1:
                for i, (src, dst) in enumerate(((hidden, hidden_o), (slope, slope_o), (w1_f, w1_o))):
                    stores.append(keep(src, dst, plan.l + 28 + i))
        elif what == "B":
            contract(on)
        else:
            close()
    for item in (*first, *big):
        item.drain()
    for copy in sent + x_out + x_pass:
        copy.wait_send()
    for copy in stores:
        copy.wait()


class Plan:
    pass


def forward_plan(S, F, rows, width, ff):
    plan = Plan()
    alloc = Sems()
    plan.S, plan.F, plan.rows = S, F, rows
    plan.wide = width // S
    plan.heads = plan.wide // HD
    plan.vec = width // F
    Y = 2 if F % 2 == 0 and F <= 8 else 4
    plan.x_s, plan.x_r = alloc.take(S), alloc.take(S)
    plan.gq, plan.gk, plan.gv, plan.gs = (Gather(alloc, S, F, Y, "own") for _ in range(4))
    half = width // 2
    plan.go = [(Gather(alloc, S, F, Y, "half"), 0, half)]
    fan = ff // width
    kind, shares = ("quarter", S) if F <= 8 else ("half", 2)
    plan.g1 = [(Gather(alloc, S, F, Y, kind), i * width, width // shares) for i in range(fan)]
    plan.g2 = [(Gather(alloc, S, F, Y, "quarter"), 0, half // S)]
    plan.g2 += [(Gather(alloc, S, F, Y, "half"), half + i * half // 2, half // 4) for i in range(2)]
    plan.ahead = 2
    plan.order = (
        *("z0", "y0", "z1", "z2", "y1", "P", "z3", "T", "T", "x1", "z4", "x0", "T", "y3",),
        *("y2", "T", "y4", "C3", "z5", "O", "z6", "C0", "x2", "x4", "C1", "C2", "y5", "C4",),
        *("E0", "E1", "z7", "y6", "E2", "E3", "C6", "x5", "y7", "B6", "C5", "C7", "B7", "B5",),
        *("N",),
    )
    plan.o_s, plan.o_r = alloc.take(S), alloc.take(S)
    plan.l = alloc.take(40)
    plan.sems = alloc.n
    return plan


def forward(S, F, x, wq, wk, wv, small, wo, w1, w2, cot):
    rows, width = x.shape
    ff = w1.shape[1]
    plan = forward_plan(S, F, rows, width, ff)
    wide = plan.wide
    length = rows * S
    sds = jax.ShapeDtypeStruct
    any_ = pl.BlockSpec(memory_space=pl.ANY)
    vmem = pltpu.VMEM
    return pl.pallas_call(
        functools.partial(forward_kernel, plan),
        out_shape=(
            sds((length, width), bf16),
            sds((width, 3 * wide), bf16),
            sds((length, wide), bf16),
            sds((length, wide), bf16),
            sds((length, wide), bf16),
            sds((wide, length), bf16),
            sds((wide, length), bf16),
            sds((wide, length), bf16),
            sds((8, length), f32),
            sds((rows, width), bf16),
            sds((width, width), bf16),
            sds((width, ff), bf16),
            sds((ff, width), bf16),
            sds((rows, width), bf16),
            sds((rows, width), f32),
            sds((rows, 128), f32),
            sds((rows, ff), bf16),
            sds((rows, ff), bf16),
            sds((rows, width), bf16),
            sds((rows, width), f32),
            sds((8, width), f32),
            sds((16, width), f32),
        ),
        in_specs=[any_] * 9,
        out_specs=(any_,) * 22,
        scratch_shapes=[
            vmem((length, width), bf16),
            vmem((width, 3 * wide), bf16),
            vmem((F * 16, plan.vec), bf16),
            vmem((length, wide), bf16),
            vmem((length, wide), bf16),
            vmem((length, wide), bf16),
            vmem((wide, length), bf16),
            vmem((wide, length), bf16),
            vmem((wide, length), bf16),
            vmem((wide, length), bf16),
            vmem((8, length), f32),
            vmem((wide, rows), f32),
            vmem((S, rows, wide), bf16),
            vmem((width, width), bf16),
            vmem((width, ff), bf16),
            vmem((ff, width), bf16),
            vmem((rows, width), bf16),
            vmem((F * 16, width), f32),
            vmem((16, width), f32),
            vmem((rows, width), f32),
            vmem((rows, width), f32),
            vmem((rows, 128), f32),
            vmem((rows, width), bf16),
            vmem((rows, ff), bf16),
            vmem((rows, ff), bf16),
            vmem((rows, width), f32),
            vmem((rows, width), bf16),
            vmem((rows, width), bf16),
            vmem((rows, width), f32),
            vmem((8, width), f32),
            pltpu.SemaphoreType.DMA((plan.sems,)),
        ],
        compiler_params=pltpu.CompilerParams(collective_id=0, has_side_effects=True, vmem_limit_bytes=63 << 20),
        name="forward_with_weight_gather",
    )(x, wq, wk, wv, small, wo, w1, w2, cot)


class Reduce:
    def __init__(self, alloc, S, F, Y, R, C, kind):
        self.kind, self.R, self.C = kind, R, C
        self.S, self.F, self.Y, self.Z, self.H = S, F, Y, F // Y, S // 2
        Z, H = self.Z, self.H
        self.w = {"half": C // 2, "quarter": C // S, "own": C}[kind]
        w = self.w
        self.n = H if kind == "quarter" else 1
        self.shapes = [(self.n, Z, Y, R, w), (Y - 1, Z, R, w), (Z, R, w)]
        if kind == "own":
            self.shapes += [(S, R, w)]
        else:
            self.shapes += [(self.n, Z, Y, R, w), (R, C)]
            self.shapes += [(H - 1, Z, Y, R, w) if kind == "quarter" else (H - 1, R, w)]
        self.shapes = [pltpu.VMEM(s, bf16) for s in self.shapes]
        self.load = alloc.take(H)
        self.ds, self.dr = alloc.take(H), alloc.take(H)
        self.xs, self.xr = alloc.take(H), alloc.take(H)
        self.ys, self.yr = alloc.take(Y), alloc.take(Y)
        self.zs, self.zr = alloc.take(Z), alloc.take(Z)
        self.fs, self.fr = alloc.take(2 * H), alloc.take(2 * H)
        self.out = alloc.take(1)

    def bind(self, g, sems, refs, source, dest):
        self.g, self.sems, self.source, self.dest = g, sems, source, dest
        if self.kind == "own":
            self.own, self.ry, self.rz, self.fin = refs
        else:
            self.own, self.ry, self.rz, self.rd, self.fin, self.rx = refs
        self.sends = []

    def send(self, src, dst, s, r, to):
        copy = rcopy(self.sems, src, dst, s, r, to)
        copy.start()
        self.sends.append(copy)

    def recv(self, ref, r):
        rcopy(self.sems, ref, ref, r, r, (self.g.sib(), self.g.f)).wait_recv()

    def column(self, hi, c):
        return (hi * 2 + c) * self.w if self.kind == "quarter" else c * self.w

    def start(self):
        g = self.g
        self.loads = []
        for m in range(self.n):
            hi = (g.hi + m) % g.H
            self.send(
                self.source(self.column(hi, 1 - g.c), self.w),
                self.rd.at[m],
                self.ds + m,
                self.dr + m,
                (g.sib(), g.f),
            )
            copy = pltpu.make_async_copy(
                self.source(self.column(hi, g.c), self.w), self.own.at[m], self.sems.at[self.load + m]
            )
            copy.start()
            self.loads.append(copy)

    def add_all(self, m, other):
        @pl.loop(0, self.Z * self.Y)
        def _(i):
            a, b = i // self.Y, i % self.Y
            self.own[m, a, b] = (self.own[m, a, b].astype(f32) + other(a, b).astype(f32)).astype(bf16)

    def over_cores(self):
        for m in list(range(1, self.n)) + [0]:
            self.loads[m].wait()
            self.recv(self.rd.at[m], self.dr + m)
            self.add_all(m, lambda a, b: self.rd[m, a, b])
            if m:
                self.send(self.own.at[m], self.rx.at[m - 1], self.xs + m, self.xr + m, (self.g.xp(m), self.g.f))
        if self.kind == "half":
            self.send_y()

    def over_x_first(self):
        for m in range(1, self.H):
            self.recv(self.rx.at[m - 1], self.xr + m)
            self.add_all(0, lambda a, b: self.rx[m - 1, a, b])
        self.send_y()

    def send_y(self):
        g = self.g
        for j in range(1, g.Y):
            y = (g.y + j) % g.Y
            self.send(self.own.at[0, :, y], self.ry.at[j - 1], self.ys + j, self.yr + j, (g.s, g.yp(j)))

    def over_y(self):
        g = self.g
        for j in range(1, g.Y):
            self.recv(self.ry.at[j - 1], self.yr + j)

        @pl.loop(0, self.Z)
        def _(a):
            total = self.own[0, a, g.y].astype(f32)
            for j in range(1, g.Y):
                total += self.ry[j - 1, a].astype(f32)
            self.own[0, a, g.y] = total.astype(bf16)

        for k in range(1, g.Z):
            z = (g.z + k) % g.Z
            self.send(self.own.at[0, z, g.y], self.rz.at[k], self.zs + k, self.zr + k, (g.s, g.zp(k)))

    def over_z(self):
        g = self.g
        total = self.own[0, g.z, g.y].astype(f32)
        for k in range(1, g.Z):
            self.recv(self.rz.at[k], self.zr + k)
            total += self.rz[k].astype(f32)
        total = total.astype(bf16)
        if self.kind == "half":
            self.rz[0] = total
            for m in range(1, g.H):
                self.send(self.rz.at[0], self.rx.at[m - 1], self.xs + m, self.xr + m, (g.xp(m), g.f))
            return
        if self.kind == "own":
            self.fin[g.s] = total
            ref = self.fin.at[g.s]
        else:
            at = pl.multiple_of(self.column(g.hi, g.c), self.w)
            self.fin[:, pl.ds(at, self.w)] = total
            ref = self.fin.at[:, pl.ds(at, self.w)]
        for m in range(1, g.H):
            self.send(ref, ref, self.fs + m, self.fr + m, (g.xp(m), g.f))
        self.send(ref, ref, self.fs, self.fr, (g.sib(), g.f))

    def over_x_last(self):
        g = self.g
        if self.kind == "half":
            total = self.rz[0].astype(f32)
            for m in range(1, g.H):
                self.recv(self.rx.at[m - 1], self.xr + m)
                total += self.rx[m - 1].astype(f32)
            at = pl.multiple_of(g.c * self.w, self.w)
            self.fin[:, pl.ds(at, self.w)] = total.astype(bf16)
            ref = self.fin.at[:, pl.ds(at, self.w)]
            self.send(ref, ref, self.fs, self.fr, (g.sib(), g.f))
            return
        for m in range(1, g.H):
            hi = (g.hi + g.H - m) % g.H
            if self.kind == "own":
                ref = self.fin.at[hi * 2 + g.c]
            else:
                ref = self.fin.at[:, pl.ds(self.column(hi, g.c), self.w)]
            self.recv(ref, self.fr + m)
            self.send(ref, ref, self.fs + g.H + m, self.fr + g.H + m, (g.sib(), g.f))

    def finish(self):
        g = self.g
        for m in range(g.H if self.kind != "half" else 1):
            hi = (g.hi + g.H - m) % g.H
            if self.kind == "own":
                ref = self.fin.at[hi * 2 + 1 - g.c]
            else:
                ref = self.fin.at[:, pl.ds(self.column(hi, 1 - g.c), self.w)]
            self.recv(ref, self.fr + (g.H + m if m else 0))
        self.copy_out = pltpu.make_async_copy(self.fin, self.dest, self.sems.at[self.out])
        self.copy_out.start()

    def done(self):
        for copy in self.sends:
            copy.wait_send()
        self.copy_out.wait()

    def step(self, name):
        {
            "D": self.over_cores,
            "X": self.over_x_first if self.kind == "quarter" else self.over_x_last,
            "Y": self.over_y,
            "Z": self.over_z,
            "L": self.over_x_last,
            "F": self.finish,
        }[name]()


def backward_kernel(plan, g_o, q_i, k_i, v_i, qt_i, kt_i, ot_i, lse_i, x_i, w_i, gh, table_i, dwo, dw1, dw2, *rest):
    dx_o, dqkv_o, dwo_o, dw1_o, dw2_o, table_o = rest[:6]
    (go, qn, kn, vn, qt, kt, ot, lse, xs, ws, dk, dv, dqt, dt, delta, grads) = rest[6:22]
    (dx, dx_send, dx_core, dx_out, dx_x, tab, tab_core, tab_x, tab_y, tab_s, tab_z, sems) = rest[22:34]
    pools = rest[34:]
    S, F, rows, heads, wide, vec = plan.S, plan.F, plan.rows, plan.heads, plan.wide, plan.vec
    g = Grid(S, F)
    g.greet(pltpu.get_barrier_semaphore())

    def keep(src, dst, at):
        copy = pltpu.make_async_copy(src, dst, sems.at[at])
        copy.start()
        return copy

    sent = []

    def send(src, dst, s, r, to):
        copy = rcopy(sems, src, dst, s, r, to)
        copy.start()
        sent.append(copy)

    def recv(ref, r):
        rcopy(sems, ref, ref, r, r, (g.sib(), g.f)).wait_recv()

    for m in [*range(1, g.H), 0]:
        for flip in range(2):
            if m or flip:
                to = ((g.hi + m) % g.H) * 2 + (g.c + flip) % 2
                send(
                    g_o.at[:, pl.ds(to * wide, wide)],
                    go.at[g.s],
                    plan.o_s + m * 2 + flip,
                    plan.o_r + g.s,
                    (to, g.f),
                )
    used = 0
    for item, which, col, row in plan.items:
        n = len(item.shapes)
        src, dst = {"o": (dwo, dwo_o), "1": (dw1, dw1_o), "2": (dw2, dw2_o)}[which]
        item.bind(
            g,
            sems,
            pools[used : used + n],
            lambda lo, width, src=src, item=item, col=col, row=row: src.at[
                :, :, pl.ds(row, item.R), pl.ds(col + lo, width)
            ],
            dst.at[pl.ds(row, item.R), pl.ds(col, item.C)],
        )
        used += n
        item.start()
    for i, item in enumerate(plan.qkv):
        item.bind(g, sems, pools[used : used + 4], None, dqkv_o.at[i])
        used += 4
    loads = [
        keep(src, dst, plan.l + i)
        for i, (src, dst) in enumerate(
            (
                (g_o.at[:, pl.ds(g.s * wide, wide)], go.at[g.s]),
                (q_i, qn),
                (k_i, kn),
                (v_i, vn),
                (qt_i, qt),
                (kt_i, kt),
                (ot_i, ot),
                (lse_i, lse),
                (x_i, xs),
                (w_i, ws),
                (gh, dx),
                (table_i, tab),
            )
        )
    ]
    items = [entry[0] for entry in plan.items]
    head_of = lax.broadcasted_iota(jnp.int32, (wide, rows), 0) // HD
    head_at = lax.broadcasted_iota(jnp.int32, (rows, wide), 1) // HD
    none = jnp.zeros((), bf16)

    def attend(t):
        if t == 0:
            dk[...] = jnp.zeros_like(dk)
            dv[...] = jnp.zeros_like(dv)
            for copy in loads:
                copy.wait()
            for i in range(1, S):
                peer = (g.s + i) % S
                recv(go.at[peer], plan.o_r + peer)
        span = pl.ds(t * rows, rows)
        turned = go[t].astype(f32).T
        dt[...] = turned.astype(bf16)
        weighed = turned * ot[:, span].astype(f32)
        for h in range(heads):
            delta[pl.ds(h, 1), :] = jnp.sum(weighed[h * HD : (h + 1) * HD], axis=0, keepdims=True)

        @pl.loop(0, heads)
        def _(h):
            band = pl.ds(pl.multiple_of(h * HD, HD), HD)
            s = jnp.dot(kn[...], jnp.where(head_of == h, qt[:, span], none), preferred_element_type=f32)
            p = jnp.exp(s - lse[pl.ds(h, 1), span])
            dp = jnp.dot(vn[...], jnp.where(head_of == h, dt[...], none), preferred_element_type=f32)
            ds = (p * (dp - delta[pl.ds(h, 1), :])).astype(bf16)
            dv[...] += jnp.dot(p.astype(bf16), jnp.where(head_at == h, go[t], none), preferred_element_type=f32)
            dk[...] += jnp.dot(ds, jnp.where(head_at == h, qn[span, :], none), preferred_element_type=f32)
            dqt[band, span] = jnp.dot(kt[band, :], ds, preferred_element_type=f32) * 0.125

    totals = []

    def projections(i):
        if i == 0:
            sum_q = jnp.zeros((1, wide), f32)
            sum_v = jnp.zeros((1, wide), f32)
            for t in range(S):
                span = pl.ds(t * rows, rows)
                q = dqt[:, span].T.astype(bf16)
                v = dv[span, :].astype(bf16)
                grads[span, pl.ds(0, wide)] = q
                grads[span, pl.ds(wide, wide)] = dk[span, :].astype(bf16)
                grads[span, pl.ds(2 * wide, wide)] = v
                sum_q += jnp.sum(q.astype(f32), axis=0, keepdims=True)
                sum_v += jnp.sum(v.astype(f32), axis=0, keepdims=True)
            totals.extend((sum_q, sum_v))
        item = plan.qkv[i]
        part_rows, width = item.R, xs.shape[1]
        step = max(part_rows, 256)
        for lo in range(0, width, step):
            prod = lax.dot_general(
                xs[:, pl.ds(lo, step)],
                grads[:, pl.ds(i * wide, wide)],
                (((0,), (0,)), ((), ())),
                preferred_element_type=f32,
            ).astype(bf16)
            for j in range(step // part_rows):
                to = lo // part_rows + j
                item.own[0, to // g.Y, to % g.Y] = prod[j * part_rows : (j + 1) * part_rows]
        item.send_y()

    def part(to):
        return lax.dot_general(
            grads[pl.ds(pl.multiple_of(to * rows, rows), rows), :],
            ws[...],
            (((1,), (1,)), ((), ())),
            preferred_element_type=f32,
        )

    def input_parts():
        for m in [*range(1, g.H), 0]:
            hi = (g.hi + m) % g.H
            dx_send[m] = part(hi * 2 + 1 - g.c).astype(bf16)
            send(dx_send.at[m], dx_core.at[m], plan.dx + m, plan.dx + g.H + m, (g.sib(), g.f))
        for m in [*range(1, g.H), 0]:
            hi = (g.hi + m) % g.H
            value = part(hi * 2 + g.c)
            recv(dx_core.at[m], plan.dx + g.H + m)
            value += dx_core[m].astype(f32)
            if m:
                dx_out[m - 1] = value.astype(bf16)
                send(dx_out.at[m - 1], dx_x.at[m - 1], plan.dx + 2 * g.H + m, plan.dx + 3 * g.H + m, (g.xp(m), g.f))
            else:
                dx[...] += value

    out = []

    def input_done():
        for m in range(1, g.H):
            recv(dx_x.at[m - 1], plan.dx + 3 * g.H + m)
            dx[...] += dx_x[m - 1].astype(f32)
        out.append(keep(dx, dx_o, plan.l + 13))

    def vectors(stage):
        Y = g.Y
        if stage == 0:
            base = g.s * (wide // vec)
            for i in range(wide // vec):
                to = base + i
                for row, value in enumerate(totals):
                    tab[to // Y, to % Y, pl.ds(row, 1), :] = value[:, i * vec : (i + 1) * vec]
            send(tab, tab_core, plan.t, plan.t + 1, (g.sib(), g.f))
        if stage == 1:
            recv(tab_core, plan.t + 1)
            tab_x[g.hi] = tab[...] + tab_core[...]
            for m in range(1, g.H):
                send(tab_x.at[g.hi], tab_x.at[g.hi], plan.tx + m, plan.tx + g.H + g.hi, (g.xp(m), g.f))
        if stage == 2:
            for m in range(1, g.H):
                hi = (g.hi + m) % g.H
                recv(tab_x.at[hi], plan.tx + g.H + hi)
            total = tab_x[0]
            for m in range(1, g.H):
                total += tab_x[m]
            tab_core[...] = total
            tab_y[g.y] = tab_core[:, g.y]
            for j in range(1, Y):
                y = (g.y + j) % Y
                send(tab_core.at[:, y], tab_y.at[g.y], plan.ty + j, plan.ty + Y + g.y, (g.s, g.yp(j)))
        if stage == 3:
            for j in range(1, Y):
                y = (g.y + j) % Y
                recv(tab_y.at[y], plan.ty + Y + y)
            total = tab_y[0]
            for j in range(1, Y):
                total += tab_y[j]
            tab_s[...] = total
            tab_z[g.z] = tab_s[g.z]
            for k in range(1, g.Z):
                z = (g.z + k) % g.Z
                send(tab_s.at[z], tab_z.at[g.z], plan.tz + k, plan.tz + g.Z + g.z, (g.s, g.zp(k)))
        if stage == 4:
            for k in range(1, g.Z):
                z = (g.z + k) % g.Z
                recv(tab_z.at[z], plan.tz + g.Z + z)
            total = tab_z[0]
            for k in range(1, g.Z):
                total += tab_z[k]
            tab_y[0, 0] = total
            out.append(keep(tab_y.at[0, 0], table_o, plan.l + 12))

    named = {chr(ord("a") + i): item for i, item in enumerate(items)}
    named.update({"q%d" % i: item for i, item in enumerate(plan.qkv)})
    for op in plan.order:
        what, on = op[0], op[1:]
        if what == "T":
            attend(int(on))
        elif what == "G":
            projections(int(on))
        elif what == "I":
            input_parts()
        elif what == "J":
            input_done()
        elif what == "V":
            vectors(int(on))
        else:
            named[on].step(what)
    for item in (*items, *plan.qkv):
        item.done()
    for copy in sent:
        copy.wait_send()
    for copy in out:
        copy.wait()


def backward_plan(S, F, rows, width, ff):
    plan = Plan()
    alloc = Sems()
    plan.S, plan.F, plan.rows = S, F, rows
    plan.wide = width // S
    plan.heads = plan.wide // HD
    plan.vec = width // F
    Y = 2 if F % 2 == 0 and F <= 8 else 4
    R, R2 = width // F, ff // F
    ones = [(Reduce(alloc, S, F, Y, R, width, kind), "1", i * width, 0) for i, kind in enumerate(("quarter", "quarter", "quarter", "quarter"))]
    twos = [(Reduce(alloc, S, F, Y, R2 // 4, width, kind), "2", 0, i * (R2 // 4)) for i, kind in enumerate(("half", "half", "half", "quarter"))]
    plan.items = [e for pair in zip(ones, twos) for e in pair]
    plan.items.append((Reduce(alloc, S, F, Y, R, width, "half"), "o", 0, 0))
    plan.qkv = [Reduce(alloc, S, F, Y, R, plan.wide, "own") for _ in range(3)]
    plan.o_s, plan.o_r = alloc.take(S), alloc.take(S)
    plan.dx = alloc.take(4 * S)
    plan.t, plan.tx, plan.ty, plan.tz = alloc.take(2), alloc.take(S), alloc.take(2 * Y), alloc.take(2 * F // Y)
    plan.l = alloc.take(14)
    plan.order = (
        *("Da", "Db", "Dd", "T0", "Dc", "T1", "Yb", "Df", "Xa", "De", "T2", "Yd", "T3", "Xc",),
        *("Dg", "Zb", "G0", "Yf", "G1", "G2", "Xe", "I", "Ya", "Zd", "V0", "Yc", "V1", "Xg",),
        *("Yq0", "Zf", "Xb", "Fb", "Yq1", "Za", "Yq2", "Di", "Zc", "Dh", "Ye", "Zq0", "J", "Xd",),
        *("V2", "Fd", "Yg", "Zq1", "Xf", "La", "Ff", "Lc", "Fa", "Zq2", "Fc", "Yi", "Ze", "V3",),
        *("Xh", "Zg", "Lq0", "Lq1", "Fq0", "Lq2", "Fq1", "Le", "Fq2", "Lg", "Fe", "Yh", "Fg", "Zi",),
        *("V4", "Xi", "Zh", "Fi", "Lh", "Fh",),
    )
    plan.sems = alloc.n
    return plan


def backward(S, F, g_o, q, k, v, qt, kt, ot, lse, x, w, gh, table, dwo, dw1, dw2):
    rows, width = g_o.shape
    ff = dw1.shape[-1]
    plan = backward_plan(S, F, rows, width, ff)
    wide, vec = plan.wide, plan.vec
    length = rows * S
    Z, Y = table.shape[:2]
    H = S // 2
    R, R2 = width // F, ff // F
    sds = jax.ShapeDtypeStruct
    any_ = pl.BlockSpec(memory_space=pl.ANY)
    pools = [s for e in plan.items for s in e[0].shapes] + [s for i in plan.qkv for s in i.shapes]
    return pl.pallas_call(
        functools.partial(backward_kernel, plan),
        out_shape=(
            sds((rows, width), f32),
            sds((3, S, R, wide), bf16),
            sds((R, width), bf16),
            sds((R, ff), bf16),
            sds((R2, width), bf16),
            sds((16, vec), f32),
        ),
        in_specs=[any_] * 15,
        out_specs=(any_,) * 6,
        scratch_shapes=[
            pltpu.VMEM((S, rows, wide), bf16),
            pltpu.VMEM((length, wide), bf16),
            pltpu.VMEM((length, wide), bf16),
            pltpu.VMEM((length, wide), bf16),
            pltpu.VMEM((wide, length), bf16),
            pltpu.VMEM((wide, length), bf16),
            pltpu.VMEM((wide, length), bf16),
            pltpu.VMEM((8, length), f32),
            pltpu.VMEM((length, width), bf16),
            pltpu.VMEM((width, 3 * wide), bf16),
            pltpu.VMEM((length, wide), f32),
            pltpu.VMEM((length, wide), f32),
            pltpu.VMEM((wide, length), f32),
            pltpu.VMEM((wide, rows), bf16),
            pltpu.VMEM((8, rows), f32),
            pltpu.VMEM((length, 3 * wide), bf16),
            pltpu.VMEM((rows, width), f32),
            pltpu.VMEM((H, rows, width), bf16),
            pltpu.VMEM((H, rows, width), bf16),
            pltpu.VMEM((H - 1, rows, width), bf16),
            pltpu.VMEM((H - 1, rows, width), bf16),
            pltpu.VMEM((Z, Y, 16, vec), f32),
            pltpu.VMEM((Z, Y, 16, vec), f32),
            pltpu.VMEM((H, Z, Y, 16, vec), f32),
            pltpu.VMEM((Y, Z, 16, vec), f32),
            pltpu.VMEM((Z, 16, vec), f32),
            pltpu.VMEM((Z, 16, vec), f32),
            pltpu.SemaphoreType.DMA((plan.sems,)),
            *pools,
        ],
        compiler_params=pltpu.CompilerParams(collective_id=1, has_side_effects=True, vmem_limit_bytes=63 << 20),
        name="attention_backward_and_gradient_sums",
    )(g_o, q, k, v, qt, kt, ot, lse, x, w, gh, table, dwo, dw1, dw2)


def layer_norm(stream, gain, shift):
    centre = stream - jnp.mean(stream, axis=-1, keepdims=True)
    variance = jnp.mean(centre * centre, axis=-1, keepdims=True)
    return centre * lax.rsqrt(variance + 1e-05) * gain + shift


def gelu_exact(inputs):
    return jax.nn.gelu(inputs, approximate=False)


def column_sums(matrix):
    return jnp.sum(matrix.astype(f32), axis=0)


def local(
    layer_input,
    query_weight,
    key_weight,
    value_weight,
    output_weight,
    query_bias,
    value_bias,
    output_bias,
    attn_gain,
    attn_shift,
    in_weight,
    in_bias,
    out_weight,
    out_bias,
    out_gain,
    out_shift,
    out_cotangent,
):
    F = lax.axis_size("fsdp")
    S = lax.axis_size("seq")
    width = layer_input.shape[-1]
    tokens = layer_input.reshape(-1, width)
    rows = tokens.shape[0]
    vec = query_bias.shape[0]
    held = (query_bias, value_bias, output_bias, attn_gain, attn_shift, out_bias, out_gain, out_shift)
    fan = in_bias.shape[0] // vec
    small = jnp.concatenate(
        [v.reshape(1, vec) for v in held]
        + [in_bias.reshape(fan, vec), jnp.zeros((16 - len(held) - fan, vec), bf16)]
    )
    (xfull, wqkv, q, k, v, qt, kt, ot, lse, mixed, wo, w1, w2, nlow, nhat, inv, hidden, slope, out, grad_stream, sums, vectors) = (
        forward(
            S,
            F,
            tokens,
            query_weight,
            key_weight,
            value_weight,
            small,
            output_weight,
            in_weight,
            out_weight,
            out_cotangent.reshape(rows, width),
        )
    )
    gain_one = vectors[3]
    grad_gain_two, grad_shift_two, grad_bias_out = sums[0], sums[1], sums[2]
    squares = jnp.sum(sums[3:8], axis=1)
    inv = inv[:, :1]
    grad_branch = grad_stream.astype(bf16)
    grad_out = jnp.dot(hidden.T, grad_branch, preferred_element_type=f32)
    grad_hidden = jnp.dot(grad_branch, w2.T, preferred_element_type=f32)
    grad_pre = (grad_hidden * slope.astype(f32)).astype(bf16)
    grad_bias_in = column_sums(grad_pre)
    grad_in = jnp.dot(nlow.T, grad_pre, preferred_element_type=f32)
    grad_normed = grad_stream + jnp.dot(grad_pre, w1.T, preferred_element_type=f32)
    grad_gain_one = jnp.sum(grad_normed * nhat, axis=0)
    grad_shift_one = jnp.sum(grad_normed, axis=0)
    weighed = grad_normed * gain_one
    grad_h = inv * (
        weighed
        - jnp.mean(weighed, axis=1, keepdims=True)
        - nhat * jnp.mean(weighed * nhat, axis=1, keepdims=True)
    )
    grad_attn = grad_h.astype(bf16)
    grad_bias_output = column_sums(grad_attn)
    grad_output = jnp.dot(mixed.T, grad_attn, preferred_element_type=f32)
    grad_mixed = jnp.dot(grad_attn, wo.T, preferred_element_type=f32).astype(bf16)
    f_y = 2 if F % 2 == 0 and F <= 8 else 4
    parts = [jnp.zeros((width,), f32)] * 2 + [
        grad_bias_output,
        grad_gain_one,
        grad_shift_one,
        grad_bias_out,
        grad_gain_two,
        grad_shift_two,
    ]
    table = jnp.stack(parts).reshape(8, F, vec).swapaxes(0, 1)
    extra = jnp.zeros((F, 16 - 8 - fan, vec), f32).at[:, 0, :5].set(squares)
    table = jnp.concatenate([table, grad_bias_in.reshape(F, fan, vec), extra], axis=1)
    by_rows = lambda t: t.astype(bf16).reshape(F // f_y, f_y, t.shape[0] // F, t.shape[1])
    input_grad, grad_qkv, grad_output, grad_in, grad_out, table = backward(
        S,
        F,
        grad_mixed,
        q,
        k,
        v,
        qt,
        kt,
        ot,
        lse,
        xfull,
        wqkv,
        grad_h,
        table.reshape(F // f_y, f_y, 16, vec),
        by_rows(grad_output),
        by_rows(grad_in),
        by_rows(grad_out),
    )
    wide = q.shape[1]
    grad_query, grad_key, grad_value = (
        t.astype(f32).swapaxes(0, 1).reshape(-1, width) for t in grad_qkv
    )
    weights = [t.astype(f32) for t in (grad_output, grad_in, grad_out)]
    small_grads = table
    grad_bias_in = table[8 : 8 + fan].reshape(-1)
    rms = jnp.sqrt(table[8 + fan, :5] / f32(rows * width * S * F))
    return (
        out.reshape(layer_input.shape),
        input_grad.reshape(layer_input.shape),
        grad_query,
        grad_key,
        grad_value,
        weights[0],
        small_grads[0],
        small_grads[1],
        small_grads[2],
        small_grads[3],
        small_grads[4],
        weights[1],
        grad_bias_in,
        weights[2],
        small_grads[5],
        small_grads[6],
        small_grads[7],
        rms,
    )


def solution(mesh):
    placed = (
        P("fsdp", "seq", None),
        P("fsdp", None),
        P("fsdp", None),
        P("fsdp", None),
        P("fsdp", None),
        P("fsdp"),
        P("fsdp"),
        P("fsdp"),
        P("fsdp"),
        P("fsdp"),
        P("fsdp", None),
        P("fsdp"),
        P("fsdp", None),
        P("fsdp"),
        P("fsdp"),
        P("fsdp"),
        P("fsdp", "seq", None),
    )
    return jax.shard_map(
        local,
        mesh=mesh,
        in_specs=placed,
        out_specs=(
            P("fsdp", "seq", None),
            P("fsdp", "seq", None),
            P("fsdp", None),
            P("fsdp", None),
            P("fsdp", None),
            P("fsdp", None),
            P("fsdp"),
            P("fsdp"),
            P("fsdp"),
            P("fsdp"),
            P("fsdp"),
            P("fsdp", None),
            P("fsdp"),
            P("fsdp", None),
            P("fsdp"),
            P("fsdp"),
            P("fsdp"),
            P(),
        ),
        check_vma=False,
    )
```
